32 devices in a mesh: seq: 4 (over z), fsdp: 8 (over y, x, core).
Axes of the slice: x: 2, y: 2, z: 4, core: 2. Of those that a mesh axis runs over, the one named last changes fastest.
Arguments:
- tokens: bfloat16 [4, 2, 1024, 2048], P('seq', None, 'fsdp'), may hold values from -9 to 9
- doc_starts: int32 [4, 4], P('seq'), may hold values from 0 to 1919, as said below
- norm_in: float32 [2048], P('fsdp'), may hold values from 0.5 to 1.5
- w_query: bfloat16 [2048, 2048], P('fsdp'), may hold values from -0.125 to 0.125
- w_key: bfloat16 [2048, 2048], P('fsdp'), may hold values from -0.125 to 0.125
- w_value: bfloat16 [2048, 2048], P('fsdp'), may hold values from -0.125 to 0.125
- mix_bias: float32 [16], P('fsdp'), may hold values from -0.5 to 2.5
- w_out: bfloat16 [2048, 2048], P('fsdp'), may hold values from -0.1875 to 0.1875
- norm_mid: float32 [2048], P('fsdp'), may hold values from 0.5 to 1.5
- w_gate: bfloat16 [2048, 8192], P('fsdp'), may hold values from -0.125 to 0.125
- w_up: bfloat16 [2048, 8192], P('fsdp'), may hold values from -0.125 to 0.125
- w_down: bfloat16 [8192, 2048], P('fsdp'), may hold values from -0.0625 to 0.0625
- cotangent: bfloat16 [4, 2, 1024, 2048], P('seq', None, 'fsdp'), may hold values from -6 to 6
Outputs:
- block_out: bfloat16 [4, 2, 1024, 2048], P('seq', None, 'fsdp')
- grad_tokens: float32 [4, 2, 1024, 2048], P('seq', None, 'fsdp')
- grad_norm_in: float32 [2048], P('fsdp')
- grad_query: float32 [2048, 2048], P('fsdp')
- grad_key: float32 [2048, 2048], P('fsdp')
- grad_value: float32 [2048, 2048], P('fsdp')
- grad_mix_bias: float32 [16], P('fsdp')
- grad_out: float32 [2048, 2048], P('fsdp')
- grad_norm_mid: float32 [2048], P('fsdp')
- grad_gate: float32 [2048, 8192], P('fsdp')
- grad_up: float32 [2048, 8192], P('fsdp')
- grad_down: float32 [8192, 2048], P('fsdp')
The draws below stay inside these ranges and needn't reach their ends.
Inputs may be any that keep to these rules, and one draw needn't show every extreme that they name: `doc_starts`: entry 0 of every row is 0 and the entries rise strictly; document d of a sequence covers the positions from its entry up to the next entry (or 2048) minus one.
All inputs are finite; a program needn't handle non-finite values.
Results may differ from the reference program's by a relative error of at most 0.035.
Values may be sent and summed in bfloat16 or wider, within the bound.
A program may use at most 704 MiB of HBM per device.

```python
import jax
import jax.numpy as jnp
from jax import lax

D = 2048
HEADS = 16
HEAD_DIM = 128
FF = 8192
ROWS = 128
NSEG = 2
NDOCS = 4
SEG = 1024
LEN = 2048
SEQS = 4


def layout_starts(base_key):
    folded_key = jax.random.fold_in(base_key, 11)
    first_key, second_key, third_key = jax.random.split(folded_key, 3)
    first_start = jax.random.randint(first_key, (SEQS,), SEG // 4, SEG // 2)
    second_start = SEG + jax.random.randint(second_key, (SEQS,), SEG // 4, SEG // 2)
    third_start = SEG + jax.random.randint(third_key, (SEQS,), 5 * SEG // 8, 7 * SEG // 8)
    third_start = third_start.at[0].set(SEG + 7 * SEG // 8 - 1)
    zeroes = jnp.zeros((SEQS,), jnp.int32)
    return jnp.stack([zeroes, first_start, second_start, third_start], axis=1).astype(jnp.int32)


def draw_doc_starts(key, part):
    return layout_starts(key)


def draw_tokens(key, part):
    starts = layout_starts(key)
    places = jnp.arange(LEN, dtype=jnp.int32)
    doc_ids = jnp.sum((starts[:, None, :] <= places[None, :, None]).astype(jnp.int32), axis=2) - 1
    noise_key, doc_key, region_key = jax.random.split(jax.random.fold_in(key, 23), 3)
    noise_part = jax.random.truncated_normal(noise_key, -4.0, 4.0, (SEQS, LEN, D), jnp.float32)
    doc_table = jax.random.truncated_normal(doc_key, -4.0, 4.0, (SEQS, NDOCS, D), jnp.float32)
    region_table = jax.random.truncated_normal(region_key, -4.0, 4.0, (SEQS, LEN // ROWS, D), jnp.float32)
    seq_index = jnp.arange(SEQS, dtype=jnp.int32)[:, None]
    region_ids = jnp.broadcast_to(places[None, :] // ROWS, (SEQS, LEN))
    values = noise_part + 0.6 * doc_table[seq_index, doc_ids] + 0.6 * region_table[seq_index, region_ids]
    return values.reshape(SEQS, NSEG, SEG, D).astype(jnp.bfloat16)


def levels(key, shape, pieces, least, largest):
    gain, own = 1.0, jax.random.fold_in(key, 6)
    for dim, blocks in pieces:
        steps = jnp.exp(jax.random.uniform(jax.random.fold_in(own, dim), (blocks,), jnp.float32, least / len(pieces), largest / len(pieces)))
        gain = gain * jnp.repeat(steps, shape[dim] // blocks).reshape([-1 if axis == dim else 1 for axis in range(len(shape))])
    return gain


def gaussian(own_key, shape, deviation, most, cuts=(), kind=jnp.bfloat16):
    drawn = jax.random.normal(own_key, shape, jnp.float32) * deviation
    if len(cuts) > 0:
        drawn = levels(own_key, shape, cuts, -0.22, 0.18) * drawn
    return jnp.clip(drawn, min=-most, max=most).astype(kind)


def setup_inputs(seed: int = 0) -> dict:
    keys = jax.random.split(jax.random.key(seed), 14)
    tokens = draw_tokens(jax.random.fold_in(keys[13], 71), 0)
    doc_starts = draw_doc_starts(jax.random.fold_in(keys[13], 71), 0)
    norm_in = jnp.clip(1.0 + 0.1 * jax.random.normal(keys[2], (D,), jnp.float32), 0.5, 1.5)
    w_query = gaussian(keys[3], (D, D), D ** -0.5, 0.125, ((0, 8),))
    w_key = gaussian(keys[4], (D, D), D ** -0.5, 0.125, ((0, 8),))
    w_value = gaussian(keys[5], (D, D), D ** -0.5, 0.125, ((0, 8),))
    mix_bias = jnp.clip(-0.5 + 3.0 * jax.random.uniform(keys[6], (HEADS,), jnp.float32) ** levels(keys[6], (HEADS,), ((0, 8),), -0.2, 0.2), -0.5, 2.5)
    w_out = gaussian(keys[7], (D, D), (D // 2) ** -0.5, 0.1875, ((0, 8),))
    norm_mid = jnp.clip(1.0 + 0.1 * jax.random.normal(keys[8], (D,), jnp.float32), 0.5, 1.5)
    w_gate = gaussian(keys[9], (D, FF), D ** -0.5, 0.125, ((0, 8),))
    w_up = gaussian(keys[10], (D, FF), D ** -0.5, 0.125, ((0, 8),))
    w_down = gaussian(keys[11], (FF, D), FF ** -0.5, 0.0625, ((0, 8),))
    cotangent = gaussian(keys[12], (SEQS, NSEG, SEG, D), 1.0, 6.0, ((0, 4), (2, 8)))
    return {"tokens": tokens, "doc_starts": doc_starts, "norm_in": norm_in, "w_query": w_query, "w_key": w_key, "w_value": w_value, "mix_bias": mix_bias, "w_out": w_out, "norm_mid": norm_mid, "w_gate": w_gate, "w_up": w_up, "w_down": w_down, "cotangent": cotangent}


@jax.custom_vjp
def low(v):
    return lax.optimization_barrier(v.astype(jnp.bfloat16)).astype(jnp.float32)

@jax.custom_vjp
def low_back(v):
    return v

def low_keep(v):
    return (low(v), None)

def low_pass(kept, grad):
    return (grad,)

def back_keep(v):
    return (v, None)

def back_low(kept, grad):
    return (low(grad),)
low.defvjp(low_keep, low_pass)
low_back.defvjp(back_keep, back_low)
highest = lax.Precision.HIGHEST
norm_eps = 1e-05

def rms_scale(values, gain_row):
    inverse = lax.rsqrt(lax.optimization_barrier(jnp.mean(values * values, axis=-1, keepdims=True)) + norm_eps)
    return values * inverse * gain_row

def feature(values):
    return jax.nn.elu(values) + 1.0

def project(left_side, right_side):
    return jnp.dot(left_side, right_side, precision=highest)

def local_attention(query_part, key_part, value_part, docs_part):
    raw_scores = jnp.einsum('qhe,khe->hqk', query_part, key_part, precision=highest)
    scores = low_back(raw_scores * HEAD_DIM ** (-0.5))
    places = jnp.arange(SEG, dtype=jnp.int32)
    allowed = (places[None, :] <= places[:, None]) & (docs_part[None, :] == docs_part[:, None])
    masked = jnp.where(allowed[None], scores, -1000000000.0)
    log_total = jax.nn.logsumexp(masked, axis=2, keepdims=True)
    weights = low(jnp.exp(masked - log_total))
    return jnp.einsum('hqk,khe->qhe', weights, value_part, precision=highest)

def one_sequence(params, block, start_row):
    norm_in, w_query, w_key, w_value, mix_bias, w_out, norm_mid, w_gate, w_up, w_down = params
    flat_rows = block.reshape(LEN, D)
    places = jnp.arange(LEN, dtype=jnp.int32)
    doc_ids = lax.optimization_barrier(jnp.sum((start_row[None, :] <= places[:, None]).astype(jnp.int32), axis=1)) - 1
    cross_doc = doc_ids[SEG]
    segment_of = places // SEG
    key_mask = ((segment_of == 0) & (doc_ids == cross_doc)).astype(jnp.float32)
    use_mask = ((segment_of == 1) & (doc_ids == cross_doc)).astype(jnp.float32)
    hidden_in = low(rms_scale(flat_rows, norm_in))
    query_rows = low(low_back(project(hidden_in, w_query))).reshape(LEN, HEADS, HEAD_DIM)
    key_rows = low(low_back(project(hidden_in, w_key))).reshape(LEN, HEADS, HEAD_DIM)
    value_rows = low(low_back(project(hidden_in, w_value))).reshape(LEN, HEADS, HEAD_DIM)
    feat_key = feature(key_rows) * key_mask[:, None, None]
    memory = jnp.einsum('thd,the->hde', feat_key, value_rows, precision=highest)
    norm_vec = lax.optimization_barrier(jnp.sum(feat_key, axis=0))
    feat_query = feature(query_rows)
    numerator = jnp.einsum('thd,hde->the', feat_query, memory, precision=highest)
    denominator = jnp.einsum('thd,hd->th', feat_query, norm_vec, precision=highest) + 1.0
    retrieved = use_mask[:, None, None] * numerator / denominator[:, :, None]
    segment_parts = [local_attention(query_rows[segment * SEG:(segment + 1) * SEG], key_rows[segment * SEG:(segment + 1) * SEG], value_rows[segment * SEG:(segment + 1) * SEG], doc_ids[segment * SEG:(segment + 1) * SEG]) for segment in range(NSEG)]
    direct = low_back(jnp.concatenate(segment_parts, axis=0))
    blend_gate = jax.nn.sigmoid(mix_bias)[None, :, None]
    mixed_rows = low((blend_gate * retrieved + (1.0 - blend_gate) * direct).reshape(LEN, D))
    attn_rows = low_back(project(mixed_rows, w_out))
    residual = flat_rows + attn_rows
    hidden_mid = low(rms_scale(residual, norm_mid))
    gate_rows = low_back(project(hidden_mid, w_gate))
    up_part = low_back(project(hidden_mid, w_up))
    inner_rows = low(jax.nn.silu(gate_rows) * up_part)
    result = residual + low_back(project(inner_rows, w_down))
    return result.reshape(NSEG, SEG, D)

def forward(params, blocks, starts):
    checked = jax.checkpoint(one_sequence)
    return lax.map(lambda item_pair: checked(params, item_pair[0], item_pair[1]), (blocks, starts))

def reference(tokens, doc_starts, norm_in, w_query, w_key, w_value, mix_bias, w_out, norm_mid, w_gate, w_up, w_down, cotangent):
    params = (norm_in, w_query.astype(jnp.float32), w_key.astype(jnp.float32), w_value.astype(jnp.float32), mix_bias, w_out.astype(jnp.float32), norm_mid, w_gate.astype(jnp.float32), w_up.astype(jnp.float32), w_down.astype(jnp.float32))

    def wrapped(weights, blocks):
        return forward(weights, blocks, doc_starts)
    result, pullback = jax.vjp(wrapped, params, tokens.astype(jnp.float32))
    grad_params, grad_tokens = pullback(cotangent.astype(jnp.float32))
    return (result.astype(jnp.bfloat16), grad_tokens, grad_params[0], grad_params[1], grad_params[2], grad_params[3], grad_params[4], grad_params[5], grad_params[6], grad_params[7], grad_params[8], grad_params[9])
```

```python
import functools

import jax
import jax.numpy as jnp
from jax import lax
from jax.experimental import pallas as pl
from jax.experimental.pallas import tpu as pltpu
from jax.sharding import PartitionSpec as P

HEADS = 16
HEAD_DIM = 128
NSEG = 2

highest = lax.Precision.HIGHEST
norm_eps = 1e-05
f32 = jnp.float32
bf16 = jnp.bfloat16


def doc_number(start_row, places):
    return jnp.sum((start_row[None, :] <= places[:, None]).astype(jnp.int32), axis=1) - 1


def norm_back(grad_in, normed, inverse):
    return inverse * (grad_in - normed * jnp.mean(grad_in * normed, axis=-1, keepdims=True))


def mm(a, b):
    return lax.dot_general(a, b, (((1,), (0,)), ((), ())), preferred_element_type=f32)


def mm_t(a, b):
    return lax.dot_general(a, b, (((1,), (1,)), ((), ())), preferred_element_type=f32)


def t_mm(a, b):
    return lax.dot_general(a, b, (((0,), (0,)), ((), ())), preferred_element_type=f32)


def dots(a, b, ca, cb, precision=None):
    return lax.dot_general(a, b, (((ca,), (cb,)), ((), ())), preferred_element_type=f32, precision=precision)


def phi(u):
    return jnp.where(u > 0, u + 1.0, jnp.exp(jnp.minimum(u, 0.0)))


def phi_slope(u):
    return jnp.where(u > 0, 1.0, jnp.exp(jnp.minimum(u, 0.0)))


def attention_kernel(heads, qkv_ref, doc_col, doc_row, side_ref, blend_ref, mixed_ref, diff_ref, lse_ref, mem_ref, nv_ref):
    n, _, rows, _ = qkv_ref.shape
    length = n * rows
    cw = heads * HEAD_DIM
    take = max(1, 256 // rows)
    block = take * rows
    scale = HEAD_DIM ** (-0.5)
    segment = pl.program_id(0)

    def part(kind, h, lo, hi):
        cols = slice(kind * cw + h * HEAD_DIM, kind * cw + (h + 1) * HEAD_DIM)
        return qkv_ref[lo:hi, 0, :, cols].reshape((hi - lo) * rows, HEAD_DIM)

    for h in range(heads):
        cols = slice(h * HEAD_DIM, (h + 1) * HEAD_DIM)

        @pl.when(segment == 0)
        def _():
            fk = phi(part(1, h, 0, n).astype(f32)) * side_ref[0]
            mem_ref[h] = dots(fk, part(2, h, 0, n).astype(f32), 0, 0, highest)
            nv_ref[h] = jnp.sum(fk, axis=0, keepdims=True)

        blend = blend_ref[:, cols]
        for i in range(n // take):
            lo, hi = i * take, (i + 1) * take
            span = (i + 1) * block
            q = part(0, h, lo, hi)
            s = dots(q, part(1, h, 0, hi), 1, 1) * scale
            at = lax.broadcasted_iota(jnp.int32, (block, span), 0) + i * block
            allowed = (lax.broadcasted_iota(jnp.int32, (block, span), 1) <= at) & (
                doc_row[0, :, :span] == doc_col[0, i * block : (i + 1) * block]
            )
            s = jnp.where(allowed, s, -1000000000.0)
            top = jnp.max(s, axis=1, keepdims=True)
            p = jnp.exp(s - top)
            tot = jnp.sum(p, axis=1, keepdims=True)
            lse_ref[h, 0, i * block : (i + 1) * block] = top + jnp.log(tot)
            direct = dots((p / tot).astype(bf16), part(2, h, 0, hi), 1, 0)
            shape = (take, rows, HEAD_DIM)

            @pl.when(segment == 0)
            def _():
                mixed_ref[lo:hi, 0, :, cols] = ((1.0 - blend) * direct).astype(bf16).reshape(shape)
                diff_ref[lo:hi, 0, :, cols] = (-direct).reshape(shape)

            @pl.when(segment != 0)
            def _():
                fq = phi(q.astype(f32))
                numer = dots(fq, mem_ref[h], 1, 0, highest)
                den = jnp.sum(fq * nv_ref[h], axis=1, keepdims=True) + 1.0
                ret = side_ref[0, i * block : (i + 1) * block] * numer / den
                mixed_ref[lo:hi, 0, :, cols] = (blend * ret + (1.0 - blend) * direct).astype(bf16).reshape(shape)
                diff_ref[lo:hi, 0, :, cols] = (ret - direct).reshape(shape)


def attention_back_kernel(
    heads, qkv_ref, dmix_ref, diff_ref, lse_ref, doc_col, doc_row, side_ref, blend_ref, mem_ref, nv_ref,
    out_ref, bias_ref, dk_acc, dv_acc, dmem, dnv,
):
    n, _, rows, _ = qkv_ref.shape
    length = n * rows
    cw = heads * HEAD_DIM
    take = max(1, 256 // rows)
    block = take * rows
    scale = HEAD_DIM ** (-0.5)
    step = pl.program_id(0)
    shape = (take, rows, HEAD_DIM)

    def part(kind, h, lo, hi):
        cols = slice(kind * cw + h * HEAD_DIM, kind * cw + (h + 1) * HEAD_DIM)
        return qkv_ref[lo:hi, 0, :, cols].reshape((hi - lo) * rows, HEAD_DIM)

    @pl.when(step == 0)
    def _():
        bias_ref[...] = jnp.zeros_like(bias_ref)
        dmem[...] = jnp.zeros_like(dmem)
        dnv[...] = jnp.zeros_like(dnv)

    for h in range(heads):
        cols = slice(h * HEAD_DIM, (h + 1) * HEAD_DIM)
        blend = blend_ref[:, cols]
        dk_acc[...] = jnp.zeros_like(dk_acc)
        dv_acc[...] = jnp.zeros_like(dv_acc)
        for i in range(n // take):
            lo, hi = i * take, (i + 1) * take
            span = (i + 1) * block
            here = slice(i * block, (i + 1) * block)
            q, k, v = part(0, h, lo, hi), part(1, h, 0, hi), part(2, h, 0, hi)
            dmix = dmix_ref[lo:hi, 0, :, cols].reshape(block, HEAD_DIM)
            bias_ref[:, cols] += jnp.sum(dmix * diff_ref[lo:hi, 0, :, cols].reshape(block, HEAD_DIM), axis=0, keepdims=True)
            ddir = ((1.0 - blend) * dmix).astype(bf16)
            s = dots(q, k, 1, 1) * scale
            at = lax.broadcasted_iota(jnp.int32, (block, span), 0) + i * block
            allowed = (lax.broadcasted_iota(jnp.int32, (block, span), 1) <= at) & (
                doc_row[0, :, :span] == doc_col[0, here]
            )
            e = jnp.exp(jnp.where(allowed, s, -1000000000.0) - lse_ref[h, 0, here])
            dp = dots(ddir, v, 1, 1)
            bal = jnp.sum(e * dp, axis=1, keepdims=True)
            ds = (e * (dp - bal)).astype(bf16)
            dv_acc[:span] += dots(e.astype(bf16), ddir, 0, 0)
            dk_acc[:span] += dots(ds, q, 0, 0) * scale
            dq = dots(ds, k, 1, 0) * scale

            @pl.when(step != 0)
            def _():
                out_ref[lo:hi, 0, :, cols] = dq.astype(bf16).reshape(shape)

            @pl.when(step == 0)
            def _():
                q32 = q.astype(f32)
                fq = phi(q32)
                numer = dots(fq, mem_ref[h], 1, 0, highest)
                den = jnp.sum(fq * nv_ref[h], axis=1, keepdims=True) + 1.0
                dnum = side_ref[0, here] * (blend * dmix) / den
                dden = -jnp.sum(dnum * numer, axis=1, keepdims=True) / den
                dmem[h] += dots(fq, dnum, 0, 0, highest)
                dnv[h] += jnp.sum(dden * fq, axis=0, keepdims=True)
                dfq = dots(dnum, mem_ref[h], 1, 1, highest) + dden * nv_ref[h]
                out_ref[lo:hi, 0, :, cols] = (dq + dfq * phi_slope(q32)).astype(bf16).reshape(shape)

        whole = (n, rows, HEAD_DIM)
        kcols = slice(cw + h * HEAD_DIM, cw + (h + 1) * HEAD_DIM)
        vcols = slice(2 * cw + h * HEAD_DIM, 2 * cw + (h + 1) * HEAD_DIM)

        @pl.when(step == 0)
        def _():
            out_ref[:, 0, :, kcols] = dk_acc[...].astype(bf16).reshape(whole)
            out_ref[:, 0, :, vcols] = dv_acc[...].astype(bf16).reshape(whole)

        @pl.when(step != 0)
        def _():
            k32 = part(1, h, 0, n).astype(f32)
            v32 = part(2, h, 0, n).astype(f32)
            key_set = side_ref[0]
            mem_v = key_set * dots(phi(k32), dmem[h], 1, 0, highest)
            mem_k = key_set * (dots(v32, dmem[h], 1, 1, highest) + dnv[h]) * phi_slope(k32)
            out_ref[:, 0, :, kcols] = (dk_acc[...] + mem_k).astype(bf16).reshape(whole)
            out_ref[:, 0, :, vcols] = (dv_acc[...] + mem_v).astype(bf16).reshape(whole)


def attention_specs(n, rows, heads, pick):
    length = n * rows
    cw = heads * HEAD_DIM
    wide = pl.BlockSpec((n, 1, rows, 3 * cw), lambda g: (0, pick(g), 0, 0))
    narrow = pl.BlockSpec((n, 1, rows, cw), lambda g: (0, pick(g), 0, 0))
    lse = pl.BlockSpec((heads, 1, length, 1), lambda g: (0, pick(g), 0, 0))
    col = pl.BlockSpec((1, length, 1), lambda g: (pick(g), 0, 0))
    row = pl.BlockSpec((1, 1, length), lambda g: (pick(g), 0, 0))
    line = pl.BlockSpec((1, cw), lambda g: (0, 0))
    mem = pl.BlockSpec((heads, HEAD_DIM, HEAD_DIM), lambda g: (0, 0, 0))
    nv = pl.BlockSpec((heads, 1, HEAD_DIM), lambda g: (0, 0, 0))
    return wide, narrow, lse, col, row, line, mem, nv


def attention(qkv, doc_col, doc_row, side, blend, heads):
    n, _, rows, _ = qkv.shape
    length = n * rows
    cw = heads * HEAD_DIM
    wide, narrow, lse, col, row, line, mem, nv = attention_specs(n, rows, heads, lambda g: g)
    pairs = heads * NSEG * length * length // 2
    return pl.pallas_call(
        functools.partial(attention_kernel, heads),
        grid=(NSEG,),
        in_specs=[wide, col, row, col, line],
        out_specs=[narrow, narrow, lse, mem, nv],
        out_shape=[
            jax.ShapeDtypeStruct((n, NSEG, rows, cw), bf16),
            jax.ShapeDtypeStruct((n, NSEG, rows, cw), f32),
            jax.ShapeDtypeStruct((heads, NSEG, length, 1), f32),
            jax.ShapeDtypeStruct((heads, HEAD_DIM, HEAD_DIM), f32),
            jax.ShapeDtypeStruct((heads, 1, HEAD_DIM), f32),
        ],
        compiler_params=pltpu.CompilerParams(vmem_limit_bytes=48 << 20),
        cost_estimate=pl.CostEstimate(flops=pairs * 4 * HEAD_DIM, transcendentals=pairs, bytes_accessed=8 << 20),
        name="attention",
    )(qkv, doc_col, doc_row, side, blend)


def attention_back(qkv, dmix, diff, lse_rows, doc_col, doc_row, side, blend, mem_all, nv_all, heads):
    n, _, rows, _ = qkv.shape
    length = n * rows
    cw = heads * HEAD_DIM
    wide, narrow, lse, col, row, line, mem, nv = attention_specs(n, rows, heads, lambda g: NSEG - 1 - g)
    pairs = heads * NSEG * length * length // 2
    return pl.pallas_call(
        functools.partial(attention_back_kernel, heads),
        grid=(NSEG,),
        in_specs=[wide, narrow, narrow, lse, col, row, col, line, mem, nv],
        out_specs=[wide, line],
        out_shape=[
            jax.ShapeDtypeStruct((n, NSEG, rows, 3 * cw), bf16),
            jax.ShapeDtypeStruct((1, cw), f32),
        ],
        scratch_shapes=[
            pltpu.VMEM((length, HEAD_DIM), f32),
            pltpu.VMEM((length, HEAD_DIM), f32),
            pltpu.VMEM((heads, HEAD_DIM, HEAD_DIM), f32),
            pltpu.VMEM((heads, 1, HEAD_DIM), f32),
        ],
        compiler_params=pltpu.CompilerParams(vmem_limit_bytes=56 << 20),
        cost_estimate=pl.CostEstimate(flops=pairs * 10 * HEAD_DIM, transcendentals=pairs, bytes_accessed=16 << 20),
        name="attention_back",
    )(qkv, dmix, diff, lse_rows, doc_col, doc_row, side, blend, mem_all, nv_all)


def flip(index, bit):
    return index + bit - 2 * bit * lax.rem(lax.div(index, bit), 2)


def send(src, dst, sems, slot, peer):
    return pltpu.make_async_remote_copy(
        src_ref=src, dst_ref=dst, send_sem=sems[0].at[slot], recv_sem=sems[1].at[slot],
        device_id={"fsdp": peer}, device_id_type=pl.DeviceIdType.MESH,
    )


def greet(peers):
    barrier = pltpu.get_barrier_semaphore()
    for peer in peers:
        pl.semaphore_signal(barrier, inc=1, device_id={"fsdp": peer}, device_id_type=pl.DeviceIdType.MESH)
    pl.semaphore_wait(barrier, len(peers))


PIECES = 4


def gather_kernel(x_ref, out_ref, local_sem, *sems):
    me = lax.axis_index("fsdp")
    sib, xn, yn = flip(me, 1), flip(me, 2), flip(me, 4)
    rows = x_ref.shape[0] // PIECES
    own, over_x, over_y, far = sems[0:2], sems[2:4], sems[4:6], sems[6:8]
    side_x, side_y, side_far = sems[8:10], sems[10:12], sems[12:14]
    greet([sib, xn, yn])

    def at(owner, c):
        return out_ref.at[owner, pl.ds(c * rows, rows)]

    def mine(c):
        return x_ref.at[pl.ds(c * rows, rows)]

    half = PIECES // 2
    started = []

    def go(copy):
        copy.start()
        started.append(copy)

    for j in range(PIECES):
        c, d = j, (j + half) % PIECES
        go(send(mine(c), at(me, c), over_x, c, xn))
        go(send(mine(d), at(me, d), over_y, d, yn))
    for c in range(PIECES):
        go(send(mine(c), at(me, c), own, c, sib))
    local = pltpu.make_async_copy(x_ref, out_ref.at[me], local_sem)
    local.start()
    x_owner, y_owner, far_owner = xn, yn, flip(xn, 4)
    for j in range(PIECES):
        c, d = j, (j + half) % PIECES
        send(at(x_owner, c), at(x_owner, c), over_x, c, xn).wait_recv()
        if c < half:
            go(send(at(x_owner, c), at(x_owner, c), far, c, yn))
        go(send(at(x_owner, c), at(x_owner, c), side_x, c, sib))
        send(at(y_owner, d), at(y_owner, d), over_y, d, yn).wait_recv()
        if d >= half:
            go(send(at(y_owner, d), at(y_owner, d), far, d, xn))
        go(send(at(y_owner, d), at(y_owner, d), side_y, d, sib))
    for j in range(half):
        for c in (j, j + half):
            send(at(far_owner, c), at(far_owner, c), far, c, yn).wait_recv()
            go(send(at(far_owner, c), at(far_owner, c), side_far, c, sib))
    for c in range(PIECES):
        for owner, pair in ((sib, own), (flip(sib, 2), side_x), (flip(sib, 4), side_y), (flip(far_owner, 1), side_far)):
            send(at(owner, c), at(owner, c), pair, c, sib).wait_recv()
    for copy in started:
        copy.wait_send()
    local.wait()


def gather(x, collective_id):
    n = lax.axis_size("fsdp")
    if n != 8:
        return lax.all_gather(x, "fsdp", axis=0)
    return pl.pallas_call(
        gather_kernel,
        in_specs=[pl.BlockSpec(memory_space=pl.ANY)],
        out_specs=pl.BlockSpec(memory_space=pl.ANY),
        out_shape=jax.ShapeDtypeStruct((n, *x.shape), x.dtype),
        scratch_shapes=[pltpu.SemaphoreType.DMA] + [pltpu.SemaphoreType.DMA((PIECES,))] * 14,
        compiler_params=pltpu.CompilerParams(collective_id=collective_id, has_side_effects=True),
        name="gather",
    )(x)


OWN, ACROSS_X, ACROSS_Y, FAR = 0, 1, 2, 3


def scatter_kernel(p_ref, out_ref, part, side, near, last, load_sems, *sems):
    me = lax.axis_index("fsdp")
    sib, xn, yn = flip(me, 1), flip(me, 2), flip(me, 4)
    dest = [me, xn, yn, flip(xn, 4)]
    rows = out_ref.shape[0] // PIECES
    half = PIECES // 2
    core = sems[0:2]
    hop = {"xf": sems[2:4], "xo": sems[4:6], "yf": sems[6:8], "yo": sems[8:10], "last": sems[10:12]}
    order = (FAR, ACROSS_X, ACROSS_Y, OWN)
    loads = [pltpu.make_async_copy(p_ref.at[dest[kind]], part.at[kind], load_sems.at[kind]) for kind in range(4)]
    for kind in order:
        loads[kind].start()
    greet([sib, xn, yn])
    started = []

    def go(copy):
        copy.start()
        started.append(copy)

    for kind in order:
        go(send(p_ref.at[flip(dest[kind], 1)], side.at[kind], core, kind, sib))

    def span(c):
        return pl.ds(c * rows, rows)

    def add(kind, c, other):
        part[kind, span(c)] = (part[kind, span(c)].astype(f32) + other.astype(f32)).astype(bf16)

    for kind in order:
        loads[kind].wait()
        send(side.at[kind], side.at[kind], core, kind, sib).wait_recv()
        for j in range(PIECES):
            add(kind, j, side[kind, span(j)])
            mine = part.at[kind, span(j)]
            if kind == FAR:
                if j < half:
                    go(send(mine, near.at[0, span(j)], hop["xf"], j, xn))
                else:
                    go(send(mine, near.at[0, span(j)], hop["yf"], j, yn))
            if kind == ACROSS_X and j < half:
                go(send(mine, near.at[1, span(j)], hop["xo"], j, xn))
            if kind == ACROSS_Y and j >= half:
                go(send(mine, near.at[1, span(j)], hop["yo"], j, yn))
    for j in range(half):
        for c in (j, j + half):
            kind, came, onward, to = (ACROSS_Y, "xf", yn, xn) if c < half else (ACROSS_X, "yf", xn, yn)
            send(near.at[0, span(c)], near.at[0, span(c)], hop[came], c, to).wait_recv()
            add(kind, c, near[0, span(c)])
            go(send(part.at[kind, span(c)], last.at[span(c)], hop["last"], c, onward))
    for j in range(half):
        for c in (j, j + half):
            send(near.at[1, span(c)], near.at[1, span(c)], hop["xo" if c < half else "yo"], c, xn).wait_recv()
            send(last.at[span(c)], last.at[span(c)], hop["last"], c, xn).wait_recv()
            out_ref[span(c)] = (
                part[OWN, span(c)].astype(f32) + near[1, span(c)].astype(f32) + last[span(c)].astype(f32)
            )
    for copy in started:
        copy.wait_send()


def scatter(x, collective_id):
    n, rows, columns = x.shape
    if n != 8:
        return lax.psum_scatter(x, "fsdp", scatter_dimension=0).astype(f32)
    sems = [4, 4] + [PIECES] * 10
    return pl.pallas_call(
        scatter_kernel,
        in_specs=[pl.BlockSpec(memory_space=pl.ANY)],
        out_specs=pl.BlockSpec(memory_space=pltpu.VMEM),
        out_shape=jax.ShapeDtypeStruct((rows, columns), f32),
        scratch_shapes=[
            pltpu.VMEM((4, rows, columns), bf16),
            pltpu.VMEM((4, rows, columns), bf16),
            pltpu.VMEM((2, rows, columns), bf16),
            pltpu.VMEM((rows, columns), bf16),
            pltpu.SemaphoreType.DMA((4,)),
        ]
        + [pltpu.SemaphoreType.DMA((k,)) for k in sems],
        compiler_params=pltpu.CompilerParams(
            collective_id=collective_id, has_side_effects=True, vmem_limit_bytes=40 << 20
        ),
        name="scatter",
    )(x)


def other(index, bits):
    for bit in (1, 2, 4):
        if bits & bit:
            index = flip(index, bit)
    return index


def link(src, dst, sems, slot, axis, peer):
    return pltpu.make_async_remote_copy(
        src_ref=src, dst_ref=dst, send_sem=sems[0].at[slot], recv_sem=sems[1].at[slot],
        device_id={axis: peer}, device_id_type=pl.DeviceIdType.MESH,
    )


ORDER = (0, 1, 2, 4, 3, 5, 6, 7)
SLOTS = 4


def chunks_of(still, moved):
    out = []
    for t, rows in enumerate(still):
        out += [(t, None, r, 128) for r in range(0, rows, 128)]
    for t, (rows, size) in enumerate(moved):
        out += [(len(still) + t, d, r, size) for d in ORDER for r in range(0, rows, size)]
    return out


def line_kernel(still, moved, *refs):
    kinds = len(still) + len(moved)
    ins, refs = refs[:kinds], refs[kinds:]
    outs, refs = refs[:kinds], refs[kinds:]
    first, refs = refs[:kinds], refs[kinds:]
    second, refs = refs[:kinds], refs[kinds:]
    come, refs = refs[: len(moved)], refs[len(moved) :]
    g_buf, a_buf, t_buf, b_buf, u_buf, loads, stores, *sems = refs
    move = [sems[2 * t : 2 * t + 2] for t in range(len(moved))]
    sems = sems[2 * len(moved) :]
    go_in, cross, back = sems[0:2], sems[2:4], sems[4:6]
    me, place = lax.axis_index("fsdp"), lax.axis_index("seq")
    is_end = (place == 0) | (place == 3)
    chunks = chunks_of(still, moved)
    inward = jnp.where(place < 2, 1, 2)
    outward = jnp.where(place < 2, 0, 3)
    opposite = 3 - inward
    barrier = pltpu.get_barrier_semaphore()
    for d in range(1, 8):
        pl.semaphore_signal(barrier, inc=1, device_id={"fsdp": other(me, d)}, device_id_type=pl.DeviceIdType.MESH)

    @pl.when(is_end)
    def _():
        pl.semaphore_signal(barrier, inc=1, device_id={"seq": inward}, device_id_type=pl.DeviceIdType.MESH)
        pl.semaphore_wait(barrier, 8)

    @pl.when(jnp.logical_not(is_end))
    def _():
        for peer in (outward, opposite):
            pl.semaphore_signal(barrier, inc=1, device_id={"seq": peer}, device_id_type=pl.DeviceIdType.MESH)
        pl.semaphore_wait(barrier, 9)

    def moving(t, d):
        ref = ins[len(still) + t]
        return link(ref.at[other(me, d)], come[t].at[me], move[t], d, "fsdp", other(me, d))

    def arrival(t, d):
        owner = other(me, d)
        return link(come[t].at[owner], come[t].at[owner], move[t], d, "fsdp", owner)

    plan = [(t, d) for t in range(len(moved)) for d in ORDER[1:]]
    begun = []

    def feed(count):
        while plan and count:
            t, d = plan.pop(0)
            moving(t, d).start()
            begun.append((t, d))
            count -= 1

    def view(refs, k):
        t, d, r, rows = chunks[k]
        if d is None:
            return refs[t].at[pl.ds(r, rows)]
        return refs[t].at[other(me, d), pl.ds(r, rows)]

    def source(k):
        t, d, r, rows = chunks[k]
        if d is None:
            return ins[t].at[pl.ds(r, rows)]
        if d == 0:
            return ins[t].at[me, pl.ds(r, rows)]
        return come[t - len(still)].at[other(me, d), pl.ds(r, rows)]

    def await_source(k):
        t, d, r, rows = chunks[k]
        if d and r == 0:
            arrival(t - len(still), d).wait_recv()

    def box(buf, k, depth):
        t, d, r, rows = chunks[k]
        return buf.at[k % depth, pl.ds(0, rows), pl.ds(0, ins[t].shape[-1])]

    def add(dst, left, right):
        rows = dst.shape[0]

        def body(i, _):
            here = pl.ds(pl.multiple_of(i * 16, 16), 16)
            dst[here] = (left[here].astype(f32) + right[here].astype(f32)).astype(bf16)
            return 0

        lax.fori_loop(0, rows // 16, body, 0)

    def end_send(k):
        return link(source(k), view(first, k), go_in, k, "seq", inward)

    def mid_cross(k):
        return link(box(t_buf, k, SLOTS), view(second, k), cross, k, "seq", opposite)

    def mid_back(k):
        return link(box(u_buf, k, SLOTS), view(outs, k), back, k, "seq", outward)

    def store(k):
        return pltpu.make_async_copy(box(u_buf, k, SLOTS), view(outs, k), stores.at[k % SLOTS])

    def finish(k):
        link(view(second, k), view(second, k), cross, k, "seq", opposite).wait_recv()
        load = pltpu.make_async_copy(view(second, k), box(b_buf, k, 2), loads.at[2])
        load.start()
        if k >= SLOTS:
            mid_back(k - SLOTS).wait_send()
            store(k - SLOTS).wait()
        load.wait()
        add(box(u_buf, k, SLOTS), box(t_buf, k, SLOTS), box(b_buf, k, 2))
        mid_back(k).start()
        store(k).start()

    count = len(chunks)
    feed(3)
    for k in range(count):
        if k % 2 == 1:
            feed(1)
        await_source(k)

        @pl.when(is_end)
        def _():
            end_send(k).start()

        @pl.when(jnp.logical_not(is_end))
        def _():
            own = pltpu.make_async_copy(source(k), box(g_buf, k, 2), loads.at[0])
            own.start()
            link(view(first, k), view(first, k), go_in, k, "seq", outward).wait_recv()
            got = pltpu.make_async_copy(view(first, k), box(a_buf, k, 2), loads.at[1])
            got.start()
            if k >= SLOTS:
                mid_cross(k - SLOTS).wait_send()
            own.wait()
            got.wait()
            add(box(t_buf, k, SLOTS), box(g_buf, k, 2), box(a_buf, k, 2))
            mid_cross(k).start()
            if k >= 1:
                finish(k - 1)

    @pl.when(is_end)
    def _():
        for k in range(count):
            link(view(outs, k), view(outs, k), back, k, "seq", inward).wait_recv()
            end_send(k).wait_send()

    @pl.when(jnp.logical_not(is_end))
    def _():
        finish(count - 1)
        for k in range(max(0, count - SLOTS), count):
            mid_cross(k).wait_send()
            mid_back(k).wait_send()
            store(k).wait()

    for t, d in begun:
        moving(t, d).wait_send()


def line_sum(still, moved, collective_id):
    if lax.axis_size("seq") != 4 or lax.axis_size("fsdp") != 8:
        swapped = [lax.all_to_all(x, "fsdp", split_axis=0, concat_axis=0, tiled=True) for x in moved]
        return [lax.psum(x, "seq") for x in still], [lax.psum(x, "seq") for x in swapped]
    still_rows = [x.shape[0] for x in still]
    moved_rows = [(x.shape[1], 128 if x.shape[2] > 1024 else 256) for x in moved]
    arrays = [*still, *moved]
    shapes = [jax.ShapeDtypeStruct(x.shape, bf16) for x in arrays]
    count = len(chunks_of(still_rows, moved_rows))
    rows = max([128] + [size for _, size in moved_rows])
    width = max(x.shape[-1] for x in arrays)
    anywhere = pl.BlockSpec(memory_space=pl.ANY)
    outs = pl.pallas_call(
        functools.partial(line_kernel, still_rows, moved_rows),
        in_specs=[anywhere] * len(arrays),
        out_specs=[anywhere] * (3 * len(arrays) + len(moved)),
        out_shape=shapes * 3 + shapes[len(still) :],
        scratch_shapes=[pltpu.VMEM((depth, rows, width), bf16) for depth in (2, 2, SLOTS, 2, SLOTS)]
        + [pltpu.SemaphoreType.DMA((3,)), pltpu.SemaphoreType.DMA((SLOTS,))]
        + [pltpu.SemaphoreType.DMA((8,))] * (2 * len(moved))
        + [pltpu.SemaphoreType.DMA((count,))] * 6,
        compiler_params=pltpu.CompilerParams(
            collective_id=collective_id, has_side_effects=True, vmem_limit_bytes=40 << 20
        ),
        name="line_sum",
    )(*arrays)
    return outs[: len(still)], outs[len(still) : len(arrays)]


def to_columns(weights, n):
    rows, cols = weights[0].shape
    parts = jnp.stack([w.reshape(rows, n, cols // n) for w in weights], axis=2)
    parts = parts.reshape(rows, n, len(weights) * (cols // n))
    out = lax.all_to_all(parts, "fsdp", split_axis=1, concat_axis=0, tiled=True)
    return out.reshape(n * rows, len(weights) * (cols // n))


def to_columns_in_turns(weights, n):
    s = lax.axis_size("seq")
    share = weights[0].shape[0] // s
    first = lax.axis_index("seq") * share
    part = to_columns([lax.dynamic_slice_in_dim(w, first, share, 0) for w in weights], n)
    part = part.reshape(n, share, part.shape[1])
    return lax.all_gather(part, "seq", axis=1, tiled=True).reshape(n * share * s, part.shape[2])


def to_rows(parts, count):
    n, rows, c = parts.shape
    parts = parts.reshape(n, rows, count, c // count).astype(f32)
    return [parts[:, :, i].transpose(1, 0, 2).reshape(rows, n * (c // count)) for i in range(count)]


def shards(
    tokens,
    doc_starts,
    norm_in,
    w_query,
    w_key,
    w_value,
    mix_bias,
    w_out,
    norm_mid,
    w_gate,
    w_up,
    w_down,
    cotangent,
):
    rows = tokens.shape[2]
    width = tokens.shape[3]
    n = lax.axis_size("fsdp")
    s = lax.axis_size("seq")
    own = NSEG * rows
    total = n * own
    seg_len = rows * n
    heads = HEADS // n
    cw = heads * HEAD_DIM
    fw = w_gate.shape[1] // n

    gains = lax.all_gather(jnp.stack([norm_in, norm_mid]), "fsdp", axis=1, tiled=True)
    gain_in, gain_mid = gains[0][None], gains[1][None]
    wqkv = to_columns([w_query, w_key, w_value], n)
    wgu = to_columns_in_turns([w_gate, w_up], n)

    flat_in = tokens.reshape(own, width).astype(f32)
    inv_in = lax.rsqrt(jnp.mean(flat_in * flat_in, axis=1, keepdims=True) + norm_eps)
    normed_in = flat_in * inv_in
    h_in = gather((normed_in * gain_in).astype(bf16), 0).reshape(total, width)
    dy = lax.all_gather(cotangent.reshape(own, width), "fsdp", axis=0, tiled=True)

    qkv = mm(h_in, wqkv).astype(bf16)

    qkv = qkv.reshape(n, NSEG, rows, 3 * cw)
    start_row = doc_starts[0]
    docs = doc_number(start_row, jnp.arange(NSEG * seg_len, dtype=jnp.int32)).reshape(NSEG, seg_len)
    side = (docs == docs[1, 0]).astype(f32)[:, :, None]
    doc_col, doc_row = docs[:, :, None], docs[:, None, :]
    blend = jax.nn.sigmoid(mix_bias)
    blend_row = jnp.repeat(blend, HEAD_DIM)[None]
    mixed, diff, lse, memory, norm_vec = attention(qkv, doc_col, doc_row, side, blend_row, heads)
    mixed = mixed.reshape(total, cw)

    attn_sum = scatter(mm(mixed, w_out).astype(bf16).reshape(n, own, width), 3)
    residual = flat_in + attn_sum
    inv_mid = lax.rsqrt(jnp.mean(residual * residual, axis=1, keepdims=True) + norm_eps)
    normed_mid = residual * inv_mid
    h_mid = gather((normed_mid * gain_mid).astype(bf16), 1).reshape(total, width)

    gate_up = mm(h_mid, wgu)
    gate, up = gate_up[:, :fw], gate_up[:, fw:]
    sig = jax.nn.sigmoid(gate)
    inner = (gate * sig * up).astype(bf16)
    mlp_sum = lax.psum_scatter(mm(inner, w_down).astype(bf16), "fsdp", scatter_dimension=0, tiled=True)
    block_out = (residual + mlp_sum.astype(f32)).astype(bf16).reshape(tokens.shape)

    grad_down = lax.psum(t_mm(inner, dy).astype(bf16), "seq").astype(f32)
    d_inner = mm_t(dy, w_down)
    d_gate = (d_inner * up * (sig * (1.0 + gate * (1.0 - sig)))).astype(bf16)
    d_up = (d_inner * (gate * sig)).astype(bf16)
    d_gu = jnp.concatenate([d_gate, d_up], axis=1)
    d_hmid = scatter(mm_t(d_gu, wgu).astype(bf16).reshape(n, own, width), 4)
    part_gu = t_mm(h_mid, d_gu).astype(bf16).reshape(n, width // n, 2 * fw)

    gain_mid_term = jnp.sum(normed_mid * d_hmid, axis=0)
    d_resid = cotangent.reshape(own, width).astype(f32) + norm_back(d_hmid * gain_mid, normed_mid, inv_mid)
    d_attn = gather(d_resid.astype(bf16), 2).reshape(total, width)

    part_out = t_mm(mixed, d_attn).astype(bf16)
    d_mixed = mm_t(d_attn, w_out).reshape(n, NSEG, rows, cw)
    d_qkv, bias_rows = attention_back(
        qkv, d_mixed, diff, lse, doc_col, doc_row, side, blend_row, memory, norm_vec, heads
    )
    d_qkv = d_qkv.reshape(total, 3 * cw)
    bias_term = jnp.sum(bias_rows.reshape(heads, HEAD_DIM), axis=1) * blend * (1.0 - blend)

    d_hin = scatter(mm_t(d_qkv, wqkv).astype(bf16).reshape(n, own, width), 5)
    part_qkv = t_mm(h_in, d_qkv).astype(bf16).reshape(n, width // n, 3 * cw)
    (sum_out,), (sum_gu, sum_qkv) = line_sum([part_out], [part_gu, part_qkv], 6)
    grad_out = sum_out.astype(f32)
    grad_gate, grad_up = to_rows(sum_gu, 2)
    grad_q, grad_k, grad_v = to_rows(sum_qkv, 3)
    gain_in_term = jnp.sum(normed_in * d_hin, axis=0)
    grad_tokens = (d_resid + norm_back(d_hin * gain_in, normed_in, inv_in)).reshape(tokens.shape)

    gain_grads = lax.psum_scatter(
        jnp.stack([gain_in_term, gain_mid_term]), "fsdp", scatter_dimension=1, tiled=True
    )
    small = lax.psum(jnp.concatenate([gain_grads.reshape(-1), bias_term]), "seq")
    per = width // n
    return (
        block_out,
        grad_tokens,
        small[:per],
        grad_q,
        grad_k,
        grad_v,
        small[2 * per :],
        grad_out,
        small[per : 2 * per],
        grad_gate,
        grad_up,
        grad_down,
    )


def solution(mesh):
    whole = P("seq", None, "fsdp", None)
    matrix, vector = P("fsdp", None), P("fsdp")
    return jax.shard_map(
        shards,
        mesh=mesh,
        in_specs=(whole, P("seq", None), vector, matrix, matrix, matrix, vector, matrix, vector, matrix, matrix, matrix, whole),
        out_specs=(whole, whole, vector, matrix, matrix, matrix, vector, matrix, vector, matrix, matrix, matrix),
        check_vma=False,
    )
```

```python
import functools

import jax
import jax.numpy as jnp
from jax import lax
from jax.experimental import pallas as pl
from jax.experimental.pallas import tpu as pltpu
from jax.sharding import PartitionSpec as P

HEADS = 16
HEAD_DIM = 128
NSEG = 2

highest = lax.Precision.HIGHEST
norm_eps = 1e-05
f32 = jnp.float32
bf16 = jnp.bfloat16


def doc_number(start_row, places):
    return jnp.sum((start_row[None, :] <= places[:, None]).astype(jnp.int32), axis=1) - 1


def norm_back(grad_in, normed, inverse):
    return inverse * (grad_in - normed * jnp.mean(grad_in * normed, axis=-1, keepdims=True))


def mm(a, b):
    return lax.dot_general(a, b, (((1,), (0,)), ((), ())), preferred_element_type=f32)


def mm_t(a, b):
    return lax.dot_general(a, b, (((1,), (1,)), ((), ())), preferred_element_type=f32)


def t_mm(a, b):
    return lax.dot_general(a, b, (((0,), (0,)), ((), ())), preferred_element_type=f32)


def dots(a, b, ca, cb, precision=None):
    return lax.dot_general(a, b, (((ca,), (cb,)), ((), ())), preferred_element_type=f32, precision=precision)


def phi(u):
    return jnp.where(u > 0, u + 1.0, jnp.exp(jnp.minimum(u, 0.0)))


def phi_slope(u):
    return jnp.where(u > 0, 1.0, jnp.exp(jnp.minimum(u, 0.0)))


def attention_head(h, heads, segment, qkv_ref, doc_col, doc_row, side_ref, blend_ref, mixed_ref, diff_ref, lse_ref, mem_ref, nv_ref):
    n, _, rows, _ = qkv_ref.shape
    cw = heads * HEAD_DIM
    take = max(1, 256 // rows)
    block = take * rows
    scale = HEAD_DIM ** (-0.5)

    def part(kind, h, lo, hi):
        cols = slice(kind * cw + h * HEAD_DIM, kind * cw + (h + 1) * HEAD_DIM)
        return qkv_ref[lo:hi, 0, :, cols].reshape((hi - lo) * rows, HEAD_DIM)

    cols = slice(h * HEAD_DIM, (h + 1) * HEAD_DIM)

    @pl.when(segment == 0)
    def _():
        fk = phi(part(1, h, 0, n).astype(f32)) * side_ref[0]
        mem_ref[h] = dots(fk, part(2, h, 0, n).astype(f32), 0, 0, highest)
        nv_ref[h] = jnp.sum(fk, axis=0, keepdims=True)

    blend = blend_ref[:, cols]
    for i in range(n // take):
        lo, hi = i * take, (i + 1) * take
        span = (i + 1) * block
        q = part(0, h, lo, hi)
        s = dots(q, part(1, h, 0, hi), 1, 1) * scale
        at = lax.broadcasted_iota(jnp.int32, (block, span), 0) + i * block
        allowed = (lax.broadcasted_iota(jnp.int32, (block, span), 1) <= at) & (
            doc_row[0, :, :span] == doc_col[0, i * block : (i + 1) * block]
        )
        s = jnp.where(allowed, s, -1000000000.0)
        top = jnp.max(s, axis=1, keepdims=True)
        p = jnp.exp(s - top)
        tot = jnp.sum(p, axis=1, keepdims=True)
        lse_ref[h, 0, i * block : (i + 1) * block] = top + jnp.log(tot)
        direct = dots((p / tot).astype(bf16), part(2, h, 0, hi), 1, 0)
        shape = (take, rows, HEAD_DIM)

        @pl.when(segment == 0)
        def _():
            mixed_ref[lo:hi, 0, :, cols] = ((1.0 - blend) * direct).astype(bf16).reshape(shape)
            diff_ref[lo:hi, 0, :, cols] = (-direct).reshape(shape)

        @pl.when(segment != 0)
        def _():
            fq = phi(q.astype(f32))
            numer = dots(fq, mem_ref[h], 1, 0, highest)
            den = jnp.sum(fq * nv_ref[h], axis=1, keepdims=True) + 1.0
            ret = side_ref[0, i * block : (i + 1) * block] * numer / den
            mixed_ref[lo:hi, 0, :, cols] = (blend * ret + (1.0 - blend) * direct).astype(bf16).reshape(shape)
            diff_ref[lo:hi, 0, :, cols] = (ret - direct).reshape(shape)


def attention_kernel(heads, *refs):
    for h in range(heads):
        attention_head(h, heads, pl.program_id(0), *refs)


def attention_back_kernel(
    heads, qkv_ref, dmix_ref, diff_ref, lse_ref, doc_col, doc_row, side_ref, blend_ref, mem_ref, nv_ref,
    out_ref, bias_ref, dk_acc, dv_acc, dmem, dnv,
):
    n, _, rows, _ = qkv_ref.shape
    length = n * rows
    cw = heads * HEAD_DIM
    take = max(1, 256 // rows)
    block = take * rows
    scale = HEAD_DIM ** (-0.5)
    step = pl.program_id(0)
    shape = (take, rows, HEAD_DIM)

    def part(kind, h, lo, hi):
        cols = slice(kind * cw + h * HEAD_DIM, kind * cw + (h + 1) * HEAD_DIM)
        return qkv_ref[lo:hi, 0, :, cols].reshape((hi - lo) * rows, HEAD_DIM)

    @pl.when(step == 0)
    def _():
        bias_ref[...] = jnp.zeros_like(bias_ref)
        dmem[...] = jnp.zeros_like(dmem)
        dnv[...] = jnp.zeros_like(dnv)

    for h in range(heads):
        cols = slice(h * HEAD_DIM, (h + 1) * HEAD_DIM)
        blend = blend_ref[:, cols]
        dk_acc[...] = jnp.zeros_like(dk_acc)
        dv_acc[...] = jnp.zeros_like(dv_acc)
        for i in range(n // take):
            lo, hi = i * take, (i + 1) * take
            span = (i + 1) * block
            here = slice(i * block, (i + 1) * block)
            q, k, v = part(0, h, lo, hi), part(1, h, 0, hi), part(2, h, 0, hi)
            dmix = dmix_ref[lo:hi, 0, :, cols].reshape(block, HEAD_DIM)
            bias_ref[:, cols] += jnp.sum(dmix * diff_ref[lo:hi, 0, :, cols].reshape(block, HEAD_DIM), axis=0, keepdims=True)
            ddir = ((1.0 - blend) * dmix).astype(bf16)
            s = dots(q, k, 1, 1) * scale
            at = lax.broadcasted_iota(jnp.int32, (block, span), 0) + i * block
            allowed = (lax.broadcasted_iota(jnp.int32, (block, span), 1) <= at) & (
                doc_row[0, :, :span] == doc_col[0, here]
            )
            e = jnp.exp(jnp.where(allowed, s, -1000000000.0) - lse_ref[h, 0, here])
            dp = dots(ddir, v, 1, 1)
            bal = jnp.sum(e * dp, axis=1, keepdims=True)
            ds = (e * (dp - bal)).astype(bf16)
            dv_acc[:span] += dots(e.astype(bf16), ddir, 0, 0)
            dk_acc[:span] += dots(ds, q, 0, 0) * scale
            dq = dots(ds, k, 1, 0) * scale

            @pl.when(step != 0)
            def _():
                out_ref[lo:hi, 0, :, cols] = dq.astype(bf16).reshape(shape)

            @pl.when(step == 0)
            def _():
                q32 = q.astype(f32)
                fq = phi(q32)
                numer = dots(fq, mem_ref[h], 1, 0, highest)
                den = jnp.sum(fq * nv_ref[h], axis=1, keepdims=True) + 1.0
                dnum = side_ref[0, here] * (blend * dmix) / den
                dden = -jnp.sum(dnum * numer, axis=1, keepdims=True) / den
                dmem[h] += dots(fq, dnum, 0, 0, highest)
                dnv[h] += jnp.sum(dden * fq, axis=0, keepdims=True)
                dfq = dots(dnum, mem_ref[h], 1, 1, highest) + dden * nv_ref[h]
                out_ref[lo:hi, 0, :, cols] = (dq + dfq * phi_slope(q32)).astype(bf16).reshape(shape)

        whole = (n, rows, HEAD_DIM)
        kcols = slice(cw + h * HEAD_DIM, cw + (h + 1) * HEAD_DIM)
        vcols = slice(2 * cw + h * HEAD_DIM, 2 * cw + (h + 1) * HEAD_DIM)

        @pl.when(step == 0)
        def _():
            out_ref[:, 0, :, kcols] = dk_acc[...].astype(bf16).reshape(whole)
            out_ref[:, 0, :, vcols] = dv_acc[...].astype(bf16).reshape(whole)

        @pl.when(step != 0)
        def _():
            k32 = part(1, h, 0, n).astype(f32)
            v32 = part(2, h, 0, n).astype(f32)
            key_set = side_ref[0]
            mem_v = key_set * dots(phi(k32), dmem[h], 1, 0, highest)
            mem_k = key_set * (dots(v32, dmem[h], 1, 1, highest) + dnv[h]) * phi_slope(k32)
            out_ref[:, 0, :, kcols] = (dk_acc[...] + mem_k).astype(bf16).reshape(whole)
            out_ref[:, 0, :, vcols] = (dv_acc[...] + mem_v).astype(bf16).reshape(whole)


def attention_specs(n, rows, heads, pick):
    length = n * rows
    cw = heads * HEAD_DIM
    wide = pl.BlockSpec((n, 1, rows, 3 * cw), lambda g: (0, pick(g), 0, 0))
    narrow = pl.BlockSpec((n, 1, rows, cw), lambda g: (0, pick(g), 0, 0))
    lse = pl.BlockSpec((heads, 1, length, 1), lambda g: (0, pick(g), 0, 0))
    col = pl.BlockSpec((1, length, 1), lambda g: (pick(g), 0, 0))
    row = pl.BlockSpec((1, 1, length), lambda g: (pick(g), 0, 0))
    line = pl.BlockSpec((1, cw), lambda g: (0, 0))
    mem = pl.BlockSpec((heads, HEAD_DIM, HEAD_DIM), lambda g: (0, 0, 0))
    nv = pl.BlockSpec((heads, 1, HEAD_DIM), lambda g: (0, 0, 0))
    return wide, narrow, lse, col, row, line, mem, nv


def attention(qkv, doc_col, doc_row, side, blend, heads):
    n, _, rows, _ = qkv.shape
    length = n * rows
    cw = heads * HEAD_DIM
    wide, narrow, lse, col, row, line, mem, nv = attention_specs(n, rows, heads, lambda g: g)
    pairs = heads * NSEG * length * length // 2
    return pl.pallas_call(
        functools.partial(attention_kernel, heads),
        grid=(NSEG,),
        in_specs=[wide, col, row, col, line],
        out_specs=[narrow, narrow, lse, mem, nv],
        out_shape=[
            jax.ShapeDtypeStruct((n, NSEG, rows, cw), bf16),
            jax.ShapeDtypeStruct((n, NSEG, rows, cw), f32),
            jax.ShapeDtypeStruct((heads, NSEG, length, 1), f32),
            jax.ShapeDtypeStruct((heads, HEAD_DIM, HEAD_DIM), f32),
            jax.ShapeDtypeStruct((heads, 1, HEAD_DIM), f32),
        ],
        compiler_params=pltpu.CompilerParams(vmem_limit_bytes=48 << 20),
        cost_estimate=pl.CostEstimate(flops=pairs * 4 * HEAD_DIM, transcendentals=pairs, bytes_accessed=8 << 20),
        name="attention",
    )(qkv, doc_col, doc_row, side, blend)


def attention_back(qkv, dmix, diff, lse_rows, doc_col, doc_row, side, blend, mem_all, nv_all, heads):
    n, _, rows, _ = qkv.shape
    length = n * rows
    cw = heads * HEAD_DIM
    wide, narrow, lse, col, row, line, mem, nv = attention_specs(n, rows, heads, lambda g: NSEG - 1 - g)
    pairs = heads * NSEG * length * length // 2
    return pl.pallas_call(
        functools.partial(attention_back_kernel, heads),
        grid=(NSEG,),
        in_specs=[wide, narrow, narrow, lse, col, row, col, line, mem, nv],
        out_specs=[wide, line],
        out_shape=[
            jax.ShapeDtypeStruct((n, NSEG, rows, 3 * cw), bf16),
            jax.ShapeDtypeStruct((1, cw), f32),
        ],
        scratch_shapes=[
            pltpu.VMEM((length, HEAD_DIM), f32),
            pltpu.VMEM((length, HEAD_DIM), f32),
            pltpu.VMEM((heads, HEAD_DIM, HEAD_DIM), f32),
            pltpu.VMEM((heads, 1, HEAD_DIM), f32),
        ],
        compiler_params=pltpu.CompilerParams(vmem_limit_bytes=56 << 20),
        cost_estimate=pl.CostEstimate(flops=pairs * 10 * HEAD_DIM, transcendentals=pairs, bytes_accessed=16 << 20),
        name="attention_back",
    )(qkv, dmix, diff, lse_rows, doc_col, doc_row, side, blend, mem_all, nv_all)


def flip(index, bit):
    return index + bit - 2 * bit * lax.rem(lax.div(index, bit), 2)


def other(index, bits):
    for bit in (1, 2, 4):
        if bits & bit:
            index = flip(index, bit)
    return index


def link(src, dst, sems, slot, axis, peer):
    return pltpu.make_async_remote_copy(
        src_ref=src, dst_ref=dst, send_sem=sems[0].at[slot], recv_sem=sems[1].at[slot],
        device_id={axis: peer}, device_id_type=pl.DeviceIdType.MESH,
    )


def send(src, dst, sems, slot, peer):
    return link(src, dst, sems, slot, "fsdp", peer)


def greet(peers):
    barrier = pltpu.get_barrier_semaphore()
    for peer in peers:
        pl.semaphore_signal(barrier, inc=1, device_id={"fsdp": peer}, device_id_type=pl.DeviceIdType.MESH)
    pl.semaphore_wait(barrier, len(peers))


PIECES = 4
ORDER = (0, 1, 2, 4, 3, 5, 6, 7)
GATHER_SEMS = [pltpu.SemaphoreType.DMA] + [pltpu.SemaphoreType.DMA((PIECES,))] * 14


def gather_parts(x_ref, out_ref, local_sem, *sems):
    me = lax.axis_index("fsdp")
    sib, xn, yn, far_owner = flip(me, 1), flip(me, 2), flip(me, 4), other(me, 6)
    rows = x_ref.shape[0] // PIECES
    half = PIECES // 2
    own, over_x, over_y, far = sems[0:2], sems[2:4], sems[4:6], sems[6:8]
    side_x, side_y, side_far = sems[8:10], sems[10:12], sems[12:14]
    started = []

    def at(owner, c):
        return out_ref.at[owner, pl.ds(c * rows, rows)]

    def mine(c):
        return x_ref.at[pl.ds(c * rows, rows)]

    def go(make):
        make().start()
        started.append(make)

    def pass_on(owner, c, sems, peer):
        go(lambda: send(at(owner, c), at(owner, c), sems, c, peer))

    def arrived(owner, c, sems):
        send(at(owner, c), at(owner, c), sems, c, sib).wait_recv()

    local = pltpu.make_async_copy(x_ref, out_ref.at[me], local_sem)

    def begin_one(c, sems, peer):
        return send(mine(c), at(me, c), sems, c, peer)

    def begin():
        for j in range(PIECES):
            c, d = j, (j + half) % PIECES
            go(functools.partial(begin_one, c, over_x, xn))
            go(functools.partial(begin_one, d, over_y, yn))
        for c in range(PIECES):
            go(functools.partial(begin_one, c, own, sib))
        local.start()
        local.wait()

    def near(j):
        c, d = j, (j + half) % PIECES
        arrived(xn, c, over_x)
        if c < half:
            pass_on(xn, c, far, yn)
        pass_on(xn, c, side_x, sib)
        arrived(yn, d, over_y)
        if d >= half:
            pass_on(yn, d, far, xn)
        pass_on(yn, d, side_y, sib)

    def beyond(j):
        for c in (j, j + half):
            arrived(far_owner, c, far)
            pass_on(far_owner, c, side_far, sib)

    def wait_from(d):
        for c in range(PIECES):
            arrived(other(me, d), c, {1: own, 3: side_x, 5: side_y, 7: side_far}[d])

    def end():
        for make in started:
            make().wait_send()

    near_steps = [functools.partial(near, j) for j in range(PIECES)]
    far_steps = [functools.partial(beyond, j) for j in range(half)]
    return [begin, *near_steps, *far_steps, wait_from, end]


def gather_steps(x_ref, out_ref, *sems):
    *steps, wait_from, end = gather_parts(x_ref, out_ref, *sems)

    def finish():
        for d in (1, 3, 5, 7):
            wait_from(d)
        end()

    return [*steps, finish]


def params(collective_id, mib=32):
    return pltpu.CompilerParams(collective_id=collective_id, has_side_effects=True, vmem_limit_bytes=mib << 20)


ANYWHERE = pl.BlockSpec(memory_space=pl.ANY)


def move_steps(ins, out_ref, first, rows, sems, local_sem):
    me = lax.axis_index("fsdp")
    count = len(ins)
    c = out_ref.shape[1] // count

    def piece(kind, d):
        peer = other(me, d)
        src = ins[kind].at[pl.ds(first, rows), pl.ds(pl.multiple_of(peer * c, 128), c)]
        dst = out_ref.at[pl.ds(pl.multiple_of(me * rows, 16), rows), pl.ds(kind * c, c)]
        return src, dst, peer

    def moving(kind, d):
        src, dst, peer = piece(kind, d)
        return send(src, dst, sems, d * count + kind, peer)

    def local(kind):
        src, dst, _ = piece(kind, 0)
        return pltpu.make_async_copy(src, dst, local_sem.at[kind])

    def begin():
        for d in (6, 7, 2, 4, 3, 5, 1):
            for kind in range(count):
                moving(kind, d).start()
        for kind in range(count):
            local(kind).start()

    def end():
        for d in ORDER[1:]:
            for kind in range(count):
                there = out_ref.at[pl.ds(pl.multiple_of(other(me, d) * rows, 16), rows), pl.ds(kind * c, c)]
                send(there, there, sems, d * count + kind, other(me, d)).wait_recv()
                moving(kind, d).wait_send()
        for kind in range(count):
            local(kind).wait()

    return [begin, end]


def move_kernel(count, rows, *refs):
    ins, (out_ref, local_sem, *sems) = refs[:count], refs[count:]
    me = lax.axis_index("fsdp")
    greet([other(me, d) for d in range(1, 8)])
    for step in move_steps(ins, out_ref, lax.axis_index("seq") * rows, rows, sems, local_sem):
        step()


def to_columns(weights, first, rows):
    n = lax.axis_size("fsdp")
    cols = weights[0].shape[1]
    weights = [lax.dynamic_slice_in_dim(w, first, rows, 0) for w in weights]
    parts = jnp.stack([w.reshape(rows, n, cols // n) for w in weights], axis=2)
    parts = parts.reshape(rows, n, len(weights) * (cols // n))
    out = lax.all_to_all(parts, "fsdp", split_axis=1, concat_axis=0, tiled=True)
    return out.reshape(n * rows, len(weights) * (cols // n))


def to_columns_in_turns(weights, collective_id):
    n, s = lax.axis_size("fsdp"), lax.axis_size("seq")
    count = len(weights)
    share = weights[0].shape[0] // s
    width = count * (weights[0].shape[1] // n)
    if n != 8:
        part = to_columns(weights, lax.axis_index("seq") * share, share)
    else:
        part = pl.pallas_call(
            functools.partial(move_kernel, count, share),
            in_specs=[ANYWHERE] * count,
            out_specs=ANYWHERE,
            out_shape=jax.ShapeDtypeStruct((n * share, width), bf16),
            scratch_shapes=[pltpu.SemaphoreType.DMA((count,))] + [pltpu.SemaphoreType.DMA((n * count,))] * 2,
            compiler_params=params(collective_id),
            name="move",
        )(*weights)
    part = part.reshape(n, share, width)
    return lax.all_gather(part, "seq", axis=1, tiled=True).reshape(n * share * s, width)


def front_kernel(count, *refs):
    x_ref, gain_ref, *refs = refs
    ins, refs = refs[:count], refs[count:]
    out_ref, gains_ref, w_ref, *sems = refs
    gain_sems, sems = sems[:3], sems[3:]
    move_sems, sems = sems[:3], sems[3:]
    me = lax.axis_index("fsdp")
    greet([other(me, d) for d in range(1, 8)])

    def gain(d):
        return send(gain_ref, gains_ref.at[me], gain_sems[1:], d, other(me, d))

    own = pltpu.make_async_copy(gain_ref, gains_ref.at[me], gain_sems[0])
    own.start()
    for d in range(1, 8):
        gain(d).start()
    first, *steps = gather_steps(x_ref, out_ref, *sems)
    begin, end = move_steps(ins, w_ref, 0, ins[0].shape[0], move_sems[1:], move_sems[0])
    first()
    begin()
    for step in steps:
        step()
    end()
    own.wait()
    for d in range(1, 8):
        there = gains_ref.at[other(me, d)]
        send(there, there, gain_sems[1:], d, other(me, d)).wait_recv()
        gain(d).wait_send()


def front(x, gains, weights, collective_id):
    n = lax.axis_size("fsdp")
    if n != 8:
        return (
            lax.all_gather(x, "fsdp", axis=0),
            lax.all_gather(gains, "fsdp", axis=1, tiled=True),
            to_columns(weights, 0, weights[0].shape[0]),
        )
    count = len(weights)
    kinds, c = gains.shape
    gains = jnp.concatenate([gains, jnp.zeros((8 - kinds, c), f32)])
    rows, cols = weights[0].shape
    sems = pltpu.SemaphoreType.DMA
    x, gains, w = pl.pallas_call(
        functools.partial(front_kernel, count),
        in_specs=[ANYWHERE] * (2 + count),
        out_specs=[ANYWHERE] * 3,
        out_shape=[
            jax.ShapeDtypeStruct((n, *x.shape), x.dtype),
            jax.ShapeDtypeStruct((n, 8, c), f32),
            jax.ShapeDtypeStruct((n * rows, count * (cols // n)), bf16),
        ],
        scratch_shapes=[sems, sems((8,)), sems((8,)), sems((count,)), sems((8 * count,)), sems((8 * count,)), *GATHER_SEMS],
        compiler_params=params(collective_id),
        name="front",
    )(x, gains, *weights)
    return x, gains[:, :kinds].transpose(1, 0, 2).reshape(kinds, n * c), w


def attend_kernel(heads, all_ref, gain_ref, w_ref, dy_ref, doc_col, doc_row, side_ref, blend_ref, *refs):
    h_out, qkv_out, dy_out, mixed_ref, diff_ref, lse_ref, mem_ref, nv_ref, x, w, hid, qkv, load_sems, x_sems, h_sems, q_sems, *sems = refs
    n, tokens, width = all_ref.shape
    rows = tokens // NSEG
    me = lax.axis_index("fsdp")
    weights = pltpu.make_async_copy(w_ref, w, load_sems.at[0])
    weights.start()

    def load(i):
        return pltpu.make_async_copy(all_ref.at[i], x.at[rest(i, 2)], x_sems.at[rest(i, 2)])

    def store(i):
        return pltpu.make_async_copy(hid.at[rest(i, 2)], h_out.at[i], h_sems.at[rest(i, 2)])

    load(0).start()
    greet([other(me, d) for d in (1, 2, 4)])
    begin, near0, near1, near2, near3, far0, far1, wait_from, end = gather_parts(dy_ref, dy_out, *sems)
    begin()
    weights.wait()

    def project(i, _):
        slot = rest(i, 2)
        for at, fn in ((3, near0), (6, near1)):

            @pl.when(i == at)
            def _():
                fn()

        @pl.when(i < n - 1)
        def _():
            load(i + 1).start()

        @pl.when(i > 1)
        def _():
            store(i - 2).wait()

        load(i).wait()
        for r in range(0, tokens, 64):
            here = x[slot, r : r + 64].astype(f32)
            inverse = lax.rsqrt(jnp.mean(here * here, axis=1, keepdims=True) + norm_eps)
            hid[slot, r : r + 64] = (here * inverse * gain_ref[...]).astype(bf16)
        store(i).start()
        made = jnp.dot(hid[slot], w[...], preferred_element_type=f32).astype(bf16)
        qkv[i] = made.reshape(NSEG, rows, made.shape[1])
        return 0

    lax.fori_loop(0, n, project, 0)
    store(n - 2).wait()
    store(n - 1).wait()
    keep = pltpu.make_async_copy(qkv, qkv_out, q_sems.at[0])
    keep.start()
    hooks = {(0, 0): near2, (0, heads - 1): near3, (1, 0): far0, (1, heads - 1): far1} if heads > 1 else {}

    def segment(i, _):
        here = pl.ds(i, 1)
        for h in range(heads):
            for (seg, at), fn in hooks.items():
                if at == h:

                    @pl.when(i == seg)
                    def _():
                        fn()

            attention_head(
                h, heads, i, qkv.at[:, here], doc_col.at[here], doc_row.at[here], side_ref.at[here], blend_ref,
                mixed_ref.at[:, here], diff_ref.at[:, here], lse_ref.at[:, here], mem_ref, nv_ref,
            )
        return 0

    lax.fori_loop(0, NSEG, segment, 0)
    for d in (1, 3, 5, 7):
        wait_from(d)
    end()
    keep.wait()


def attend(x_all, gain, wqkv, dy, doc_col, doc_row, side, blend, heads, collective_id):
    n, tokens, width = x_all.shape
    rows = tokens // NSEG
    cw = heads * HEAD_DIM
    if n != 8 or heads == 1:
        here = x_all.reshape(n * tokens, width).astype(f32)
        inverse = lax.rsqrt(jnp.mean(here * here, axis=1, keepdims=True) + norm_eps)
        h_in = (here * inverse * gain).astype(bf16)
        qkv = mm(h_in, wqkv).astype(bf16).reshape(n, NSEG, rows, 3 * cw)
        dy = lax.all_gather(dy, "fsdp", axis=0)
        return h_in.reshape(x_all.shape), qkv, dy, *attention(qkv, doc_col, doc_row, side, blend, heads)
    length = n * rows
    sems = pltpu.SemaphoreType.DMA
    inside = pl.BlockSpec(memory_space=pltpu.VMEM)
    pairs = heads * NSEG * length * length // 2
    return pl.pallas_call(
        functools.partial(attend_kernel, heads),
        in_specs=[ANYWHERE, inside, ANYWHERE, ANYWHERE] + [inside] * 4,
        out_specs=[ANYWHERE] * 3 + [inside] * 5,
        out_shape=[
            jax.ShapeDtypeStruct(x_all.shape, bf16),
            jax.ShapeDtypeStruct((n, NSEG, rows, 3 * cw), bf16),
            jax.ShapeDtypeStruct((n, *dy.shape), bf16),
            jax.ShapeDtypeStruct((n, NSEG, rows, cw), bf16),
            jax.ShapeDtypeStruct((n, NSEG, rows, cw), f32),
            jax.ShapeDtypeStruct((heads, NSEG, length, 1), f32),
            jax.ShapeDtypeStruct((heads, HEAD_DIM, HEAD_DIM), f32),
            jax.ShapeDtypeStruct((heads, 1, HEAD_DIM), f32),
        ],
        scratch_shapes=[
            pltpu.VMEM((2, tokens, width), bf16),
            pltpu.VMEM(wqkv.shape, bf16),
            pltpu.VMEM((2, tokens, width), bf16),
            pltpu.VMEM((n, NSEG, rows, 3 * cw), bf16),
            *[sems((k,)) for k in (1, 2, 2, 1)],
            *GATHER_SEMS,
        ],
        compiler_params=params(collective_id, 48),
        cost_estimate=pl.CostEstimate(
            flops=pairs * 4 * HEAD_DIM + 6 * n * tokens * width * cw, transcendentals=pairs, bytes_accessed=32 << 20
        ),
        name="attend",
    )(x_all, gain, wqkv, dy, doc_col, doc_row, side, blend)


def quotient(a, b):
    return a // b if isinstance(a, int) else lax.div(a, b)


def rest(a, b):
    return a % b if isinstance(a, int) else lax.rem(a, b)


def xor(index, bits):
    total = 0
    for bit in (1, 2, 4):
        a, b = rest(quotient(index, bit), 2), rest(quotient(bits, bit), 2)
        total = total + bit * (a + b - 2 * a * b)
    return total


def nth_block(i):
    return i + quotient(i, 4) * (2 - 4 * rest(quotient(i, 2), 2))


def mlp_kernel(own_ref, wgu_ref, wd_ref, dy_ref, h_out, inner_out, dgu_out, out_ref, *refs):
    wgu, wd, h, dy, inner, dgu, mine, side, near, last, weight_sems, dy_sems, h_sems, inner_sems, dgu_sems, *sems = refs
    gather_sems, sems = sems[:15], sems[15:]
    me = lax.axis_index("fsdp")
    sib, xn, yn = flip(me, 1), flip(me, 2), flip(me, 4)
    tokens, width = own_ref.shape
    fw = wd.shape[0]
    begin, near0, near1, near2, near3, far0, far1, wait_from, gather_end = gather_parts(own_ref, h, *gather_sems)
    back = scatter_parts(mine, side, near, last, out_ref, sems)
    loads = [
        pltpu.make_async_copy(wgu_ref, wgu, weight_sems.at[0]),
        pltpu.make_async_copy(wd_ref, wd, weight_sems.at[1]),
    ]
    for load in loads:
        load.start()

    def load_dy(i):
        return pltpu.make_async_copy(dy_ref.at[xor(me, nth_block(i))], dy.at[rest(i, 2)], dy_sems.at[rest(i, 2)])

    load_dy(0).start()
    greet([sib, xn, yn])
    begin()
    back_x, back_far = back["combine"](2), back["combine"](6)
    hooks = {
        (0, 6): [near0],
        (1, 0): [lambda: wait_from(1)],
        (1, 2): [near1],
        (1, 6): [near2],
        (2, 0): [near3],
        (2, 6): [far0],
        (3, 0): [lambda: wait_from(3)],
        (3, 4): [far1],
        (4, 3): [back_x],
        (5, 0): [lambda: wait_from(7)],
        (6, 3): [back_far],
        (7, 0): [lambda: wait_from(5)],
        (7, 4): [lambda: back["onward"](0)],
        (7, 6): [lambda: back["onward"](1)],
    }
    loads[0].wait()
    loads[1].wait()
    tile = fw // 4
    wide = width // 4

    def store(i, ref, out, store_sems):
        slot = rest(i, 2)
        return pltpu.make_async_copy(ref.at[slot], out.at[xor(me, nth_block(i))], store_sems.at[slot])

    def keep(i):
        owner = xor(me, nth_block(i))
        return pltpu.make_async_copy(h.at[owner], h_out.at[owner], h_sems.at[i])

    def body(i, _):
        slot = rest(i, 2)
        block = nth_block(i)
        owner = xor(me, block)

        def point(p):
            for (step, at), fns in hooks.items():
                if at == p:

                    @pl.when(i == step)
                    def _():
                        for fn in fns:
                            fn()

        @pl.when(i < 7)
        def _():
            load_dy(i + 1).start()

        @pl.when(i > 1)
        def _():
            store(i - 2, inner, inner_out, inner_sems).wait()
            store(i - 2, dgu, dgu_out, dgu_sems).wait()

        for t in range(4):
            point(t)
            if t == 0:
                keep(i).start()
                load_dy(i).wait()
            left = h[owner]
            cols = slice(t * tile, (t + 1) * tile)
            gate = jnp.dot(left, wgu[:, cols], preferred_element_type=f32)
            up = jnp.dot(left, wgu[:, fw + t * tile : fw + (t + 1) * tile], preferred_element_type=f32)
            back_in = dots(dy[slot], wd[cols], 1, 1)
            sig = jax.nn.sigmoid(gate)
            act = gate * sig
            inner[slot, :, cols] = (act * up).astype(bf16)
            dgu[slot, :, cols] = (back_in * up * (sig * (1.0 + gate * (1.0 - sig)))).astype(bf16)
            dgu[slot, :, fw + t * tile : fw + (t + 1) * tile] = (back_in * act).astype(bf16)
        store(i, inner, inner_out, inner_sems).start()
        store(i, dgu, dgu_out, dgu_sems).start()
        for t in range(4):
            point(4 + t)
            cols = slice(t * wide, (t + 1) * wide)
            mine[block, :, cols] = dots(dgu[slot], wgu[cols], 1, 1).astype(bf16)

        @pl.when(lax.rem(block, 2) == 1)
        def _():
            back["to_core"](block).start()

        return 0

    lax.fori_loop(0, 8, body, 0)
    back["combine"](4)()
    back["onward"](2)
    back["combine"](0)()
    back["finish"]()
    for i in (6, 7):
        store(i, inner, inner_out, inner_sems).wait()
        store(i, dgu, dgu_out, dgu_sems).wait()
    for i in range(8):
        keep(i).wait()
    gather_end()


def scatter_parts(mine, side, near, last, out_ref, sems):
    me = lax.axis_index("fsdp")
    sib, xn, yn = flip(me, 1), flip(me, 2), flip(me, 4)
    rows = out_ref.shape[0] // PIECES
    half = PIECES // 2
    core, sems = sems[:2], sems[2:]
    hop = {"xf": sems[0:2], "xo": sems[2:4], "yf": sems[4:6], "yo": sems[6:8], "last": sems[8:10]}

    def to_core(d):
        kind = quotient(d, 2)
        return send(mine.at[d], side.at[kind], core, kind, sib)

    def span(c):
        return pl.ds(c * rows, rows)

    def go(copy):
        copy.start()

    def travel(d, c):
        if d == 6:
            return send(mine.at[6, span(c)], near.at[0, span(c)], hop["xf" if c < half else "yf"], c, xn if c < half else yn)
        if d == 2:
            return send(mine.at[2, span(c)], near.at[1, span(c)], hop["xo"], c, xn)
        return send(mine.at[4, span(c)], near.at[1, span(c)], hop["yo"], c, yn)

    def leaves(d, c):
        return d == 6 or (d == 2 and c < half) or (d == 4 and c >= half)

    def step_on(c):
        return send(mine.at[4 if c < half else 2, span(c)], last.at[span(c)], hop["last"], c, yn if c < half else xn)

    def add(d, c, ref):
        total = mine.at[d]

        def body(i, _):
            here = pl.ds(pl.multiple_of(c * rows + i * 16, 16), 16)
            total[here] = (total[here].astype(f32) + ref[here].astype(f32)).astype(bf16)
            return 0

        lax.fori_loop(0, rows // 16, body, 0)

    def combine(d):
        def run():
            send(side.at[d // 2], side.at[d // 2], core, d // 2, sib).wait_recv()
            for c in range(PIECES):
                add(d, c, side.at[d // 2])
                if leaves(d, c):
                    go(travel(d, c))

        return run

    def onward(which):
        for c in range(half) if which == 2 else [half + which]:
            d = 4 if c < half else 2
            send(near.at[0, span(c)], near.at[0, span(c)], hop["xf" if c < half else "yf"], c, xn).wait_recv()
            add(d, c, near.at[0])
            go(step_on(c))

    def finish():
        total, came = mine.at[0], near.at[1]
        for j in range(half):
            for c in (j + half, j):
                send(near.at[1, span(c)], near.at[1, span(c)], hop["xo" if c < half else "yo"], c, xn).wait_recv()
                send(last.at[span(c)], last.at[span(c)], hop["last"], c, xn).wait_recv()

                def body(i, _):
                    here = pl.ds(pl.multiple_of(c * rows + i * 16, 16), 16)
                    out_ref[here] = total[here].astype(f32) + came[here].astype(f32) + last[here].astype(f32)
                    return 0

                lax.fori_loop(0, rows // 16, body, 0)
        for d in (1, 3, 5, 7):
            to_core(d).wait_send()
        for d in (2, 4, 6):
            for c in range(PIECES):
                if leaves(d, c):
                    travel(d, c).wait_send()
        for c in range(PIECES):
            step_on(c).wait_send()

    return {"to_core": to_core, "combine": combine, "onward": onward, "finish": finish}


SCATTER_SEMS = [pltpu.SemaphoreType.DMA((4,))] * 2 + [pltpu.SemaphoreType.DMA((PIECES,))] * 10


def scatter_boxes(rows, columns):
    return [pltpu.VMEM((k, rows, columns), bf16) for k in (8, 4, 2)] + [pltpu.VMEM((rows, columns), bf16)]


def mlp(h_own, wgu, w_down, dy, collective_id):
    n, rows, width = dy.shape
    fw = w_down.shape[0]
    if n != 8:
        h = lax.all_gather(h_own, "fsdp", axis=0)
        gate_up = mm(h.reshape(n * rows, width), wgu)
        gate, up = gate_up[:, :fw], gate_up[:, fw:]
        sig = jax.nn.sigmoid(gate)
        inner = (gate * sig * up).astype(bf16)
        back_in = mm_t(dy.reshape(n * rows, width), w_down)
        d_gate = (back_in * up * (sig * (1.0 + gate * (1.0 - sig)))).astype(bf16)
        d_gu = jnp.concatenate([d_gate, (back_in * (gate * sig)).astype(bf16)], axis=1)
        d_h = lax.psum_scatter(mm_t(d_gu, wgu).astype(bf16), "fsdp", scatter_dimension=0, tiled=True).astype(f32)
        return h, inner.reshape(n, rows, fw), d_gu.reshape(n, rows, 2 * fw), d_h
    sems = pltpu.SemaphoreType.DMA
    return pl.pallas_call(
        mlp_kernel,
        in_specs=[ANYWHERE] * 4,
        out_specs=[ANYWHERE] * 3 + [pl.BlockSpec(memory_space=pltpu.VMEM)],
        out_shape=[
            jax.ShapeDtypeStruct((n, rows, width), bf16),
            jax.ShapeDtypeStruct((n, rows, fw), bf16),
            jax.ShapeDtypeStruct((n, rows, 2 * fw), bf16),
            jax.ShapeDtypeStruct((rows, width), f32),
        ],
        scratch_shapes=[
            pltpu.VMEM(wgu.shape, bf16),
            pltpu.VMEM(w_down.shape, bf16),
            pltpu.VMEM((n, rows, width), bf16),
            pltpu.VMEM((2, rows, width), bf16),
            pltpu.VMEM((2, rows, fw), bf16),
            pltpu.VMEM((2, rows, 2 * fw), bf16),
            *scatter_boxes(rows, width),
            *[sems((k,)) for k in (2, 2, 8, 2, 2)],
            *GATHER_SEMS,
            *SCATTER_SEMS,
        ],
        compiler_params=params(collective_id, 60),
        cost_estimate=pl.CostEstimate(flops=10 * n * rows * width * fw, transcendentals=n * rows * fw, bytes_accessed=64 << 20),
        name="mlp",
    )(h_own, wgu, w_down, dy)


def product_tiles(lhs, rhs, box, out_ref, sems, over_rows, hooks):
    columns = rhs.shape[1]
    count = out_ref.shape[0] // 256

    def rows(i):
        return pl.ds(pl.multiple_of(i * 256, 256), 256)

    def store(i):
        return pltpu.make_async_copy(
            box.at[rest(i, 2), :, pl.ds(0, columns)], out_ref.at[rows(i)], sems.at[rest(i, 2)]
        )

    def body(i, _):
        for step, fns in hooks.items():

            @pl.when(i == step)
            def _():
                for fn in fns:
                    fn()

        @pl.when(i > 1)
        def _():
            store(i - 2).wait()

        left = lhs[:, rows(i)] if over_rows else lhs[rows(i)]
        for at in range(0, columns, 512):
            here = slice(at, min(at + 512, columns))
            box[rest(i, 2), :, here] = dots(left, rhs[:, here], 0 if over_rows else 1, 0).astype(bf16)
        store(i).start()
        return 0

    lax.fori_loop(0, count, body, 0)
    for i in range(max(0, count - 2), count):
        store(i).wait()


def gather_grads_kernel(x_ref, inner_ref, dy_ref, h_ref, dgu_ref, out_ref, down_ref, gu_ref, inner, dy, h, dgu, box, load_sems, sems, *refs):
    loads = [
        pltpu.make_async_copy(src, dst, load_sems.at[i])
        for i, (src, dst) in enumerate(((inner_ref, inner), (dy_ref, dy), (h_ref, h), (dgu_ref, dgu)))
    ]
    for load in loads:
        load.start()
    me = lax.axis_index("fsdp")
    greet([other(me, d) for d in (1, 2, 4)])
    begin, near0, near1, near2, near3, far0, far1, wait_from, end = gather_parts(x_ref, out_ref, *refs)
    begin()
    loads[0].wait()
    loads[1].wait()
    product_tiles(inner, dy, box, down_ref, sems, True, {1: [near0], 3: [near1]})
    loads[2].wait()
    loads[3].wait()
    product_tiles(h, dgu, box, gu_ref, sems, True, {1: [near2], 3: [near3], 5: [far0], 7: [far1]})
    for d in (1, 3, 5, 7):
        wait_from(d)
    end()


def gather_grads(x, inner, dy, h, dgu, collective_id):
    n = lax.axis_size("fsdp")
    if n != 8:
        return lax.all_gather(x, "fsdp", axis=0), t_mm(inner, dy).astype(bf16), t_mm(h, dgu).astype(bf16)
    total, width = dy.shape
    sems = pltpu.SemaphoreType.DMA
    return pl.pallas_call(
        gather_grads_kernel,
        in_specs=[ANYWHERE] * 5,
        out_specs=[ANYWHERE] * 3,
        out_shape=[
            jax.ShapeDtypeStruct((n, *x.shape), bf16),
            jax.ShapeDtypeStruct((inner.shape[1], width), bf16),
            jax.ShapeDtypeStruct((width, dgu.shape[1]), bf16),
        ],
        scratch_shapes=[pltpu.VMEM(a.shape, bf16) for a in (inner, dy, h, dgu)]
        + [pltpu.VMEM((2, 256, max(width, dgu.shape[1])), bf16), sems((4,)), sems((2,)), *GATHER_SEMS],
        compiler_params=params(collective_id, 56),
        cost_estimate=pl.CostEstimate(
            flops=2 * total * width * (inner.shape[1] + dgu.shape[1]), transcendentals=0, bytes_accessed=48 << 20
        ),
        name="gather_grads",
    )(x, inner, dy, h, dgu)


def product_scatter_kernel(turned, tasks, *refs):
    (lhs_ref, rhs_ref), refs = refs[:2], refs[2:]
    task_ins, refs = refs[: 2 * len(tasks)], refs[2 * len(tasks) :]
    out_ref, refs = refs[0], refs[1:]
    task_outs, refs = refs[: len(tasks)], refs[len(tasks) :]
    (lhs, rhs, mine, side, near, last), refs = refs[:6], refs[6:]
    task_boxes, refs = refs[: 2 * len(tasks)], refs[2 * len(tasks) :]
    if tasks:
        box, store_sems, task_sems, *refs = refs
    load_sems, *sems = refs
    me = lax.axis_index("fsdp")
    loads = [pltpu.make_async_copy(lhs_ref, lhs, load_sems.at[0]), pltpu.make_async_copy(rhs_ref, rhs, load_sems.at[1])]
    task_loads = [pltpu.make_async_copy(task_ins[i], task_boxes[i], task_sems.at[i]) for i in range(2 * len(tasks))]
    for load in loads + task_loads:
        load.start()
    greet([other(me, d) for d in (1, 2, 4)])
    back = scatter_parts(mine, side, near, last, out_ref, sems)
    width = out_ref.shape[1]
    wide = width // 4
    combined = {2: back["combine"](6), 4: back["combine"](4), 6: back["combine"](2)}
    for load in loads:
        load.wait()

    def body(i, _):
        block = 6 - 2 * lax.div(i, 2) + lax.rem(i, 2)
        owner = xor(me, block)
        left = lhs[owner]
        for t in range(4):
            cols = slice(t * wide, (t + 1) * wide)
            made = dots(left, rhs[cols], 1, 1) if turned else dots(left, rhs[:, cols], 1, 0)
            mine[block, :, cols] = made.astype(bf16)

        @pl.when(lax.rem(block, 2) == 1)
        def _():
            back["to_core"](block).start()

        for step, fn in combined.items():

            @pl.when(i == step)
            def _():
                fn()

        return 0

    lax.fori_loop(0, 8, body, 0)
    todo = [lambda: back["combine"](0)(), lambda: back["onward"](0), lambda: back["onward"](1), lambda: back["onward"](2)]
    for k, (over_rows, places) in enumerate(tasks):
        task_loads[2 * k].wait()
        task_loads[2 * k + 1].wait()
        hooks = {place: [todo.pop(0)] for place in places}
        product_tiles(task_boxes[2 * k], task_boxes[2 * k + 1], box, task_outs[k], store_sems, over_rows, hooks)
    for fn in todo:
        fn()
    back["finish"]()


def product_scatter(lhs, rhs, turned, tasks, collective_id):
    n, rows, depth = lhs.shape
    width = rhs.shape[0] if turned else rhs.shape[1]
    if n != 8:
        made = (mm_t if turned else mm)(lhs.reshape(n * rows, depth), rhs).astype(bf16)
        made = lax.psum_scatter(made, "fsdp", scatter_dimension=0, tiled=True).astype(f32)
        return made, [(t_mm if over else mm)(a, b).astype(bf16) for a, b, over, _ in tasks]
    sems = pltpu.SemaphoreType.DMA
    pairs = [x for a, b, _, _ in tasks for x in (a, b)]
    results = [jax.ShapeDtypeStruct((a.shape[1] if over else a.shape[0], b.shape[1]), bf16) for a, b, over, _ in tasks]
    flops = 2 * n * rows * depth * width + sum(2 * a.size * b.shape[1] for a, b, _, _ in tasks)
    scratch = [pltpu.VMEM(lhs.shape, bf16), pltpu.VMEM(rhs.shape, bf16), *scatter_boxes(rows, width)]
    if tasks:
        scratch += [pltpu.VMEM(x.shape, bf16) for x in pairs]
        scratch += [pltpu.VMEM((2, 256, max(b.shape[1] for _, b, _, _ in tasks)), bf16), sems((2,)), sems((len(pairs),))]
    out, *made = pl.pallas_call(
        functools.partial(product_scatter_kernel, turned, [(over, places) for _, _, over, places in tasks]),
        in_specs=[ANYWHERE] * (2 + len(pairs)),
        out_specs=[pl.BlockSpec(memory_space=pltpu.VMEM)] + [ANYWHERE] * len(tasks),
        out_shape=[jax.ShapeDtypeStruct((rows, width), f32), *results],
        scratch_shapes=[*scratch, sems((2,)), *SCATTER_SEMS],
        compiler_params=params(collective_id, 60),
        cost_estimate=pl.CostEstimate(flops=flops, transcendentals=0, bytes_accessed=48 << 20),
        name="product_scatter",
    )(lhs, rhs, *pairs)
    return out, made


SLOTS = 4


def chunks_of(still, moved):
    out = []
    for t, rows in enumerate(still):
        out += [(t, None, r, 128) for r in range(0, rows, 128)]
    for t, (rows, size) in enumerate(moved):
        out += [(len(still) + t, d, r, size) for d in ORDER for r in range(0, rows, size)]
    return out


def line_kernel(still, moved, *refs):
    kinds = len(still) + len(moved)
    small_ref, refs = refs[0], refs[1:]
    ins, refs = refs[:kinds], refs[kinds:]
    small_out, refs = refs[0], refs[1:]
    outs, refs = refs[:kinds], refs[kinds:]
    first, refs = refs[:kinds], refs[kinds:]
    second, refs = refs[:kinds], refs[kinds:]
    come, refs = refs[: len(moved)], refs[len(moved) :]
    small_come, small_sum, small_in, small_back, small_sems, small_line, *refs = refs
    small_line_sems, refs = (small_line, refs[0]), refs[1:]
    small_move, refs = (small_sems, refs[0]), refs[1:]
    g_buf, a_buf, t_buf, b_buf, u_buf, loads, stores, *sems = refs
    move = [sems[2 * t : 2 * t + 2] for t in range(len(moved))]
    sems = sems[2 * len(moved) :]
    go_in, cross, back = sems[0:2], sems[2:4], sems[4:6]
    me, place = lax.axis_index("fsdp"), lax.axis_index("seq")
    is_end = (place == 0) | (place == 3)
    chunks = chunks_of(still, moved)
    inward = jnp.where(place < 2, 1, 2)
    outward = jnp.where(place < 2, 0, 3)
    opposite = 3 - inward
    barrier = pltpu.get_barrier_semaphore()
    for d in range(1, 8):
        pl.semaphore_signal(barrier, inc=1, device_id={"fsdp": other(me, d)}, device_id_type=pl.DeviceIdType.MESH)

    @pl.when(is_end)
    def _():
        pl.semaphore_signal(barrier, inc=1, device_id={"seq": inward}, device_id_type=pl.DeviceIdType.MESH)
        pl.semaphore_wait(barrier, 8)

    @pl.when(jnp.logical_not(is_end))
    def _():
        for peer in (outward, opposite):
            pl.semaphore_signal(barrier, inc=1, device_id={"seq": peer}, device_id_type=pl.DeviceIdType.MESH)
        pl.semaphore_wait(barrier, 9)

    def moving(t, d):
        ref = ins[len(still) + t]
        return link(ref.at[other(me, d)], come[t].at[me], move[t], d, "fsdp", other(me, d))

    def arrival(t, d):
        owner = other(me, d)
        return link(come[t].at[owner], come[t].at[owner], move[t], d, "fsdp", owner)

    def small_moving(d):
        return link(small_ref.at[other(me, d)], small_come.at[me], small_move, d, "fsdp", other(me, d))

    def small_arrival(d):
        there = small_come.at[other(me, d)]
        return link(there, there, small_move, d, "fsdp", other(me, d))

    def small_hop(src, dst, slot, peer):
        return link(src, dst, small_line_sems, slot, "seq", peer)

    for d in range(1, 8):
        small_moving(d).start()
    small_come[me] = small_ref[me]
    plan = [(t, d) for t in range(len(moved)) for d in ORDER[1:]]
    begun = []

    def feed(count):
        while plan and count:
            t, d = plan.pop(0)
            moving(t, d).start()
            begun.append((t, d))
            count -= 1

    def view(refs, k):
        t, d, r, rows = chunks[k]
        if d is None:
            return refs[t].at[pl.ds(r, rows)]
        return refs[t].at[other(me, d), pl.ds(r, rows)]

    def windows(k):
        t, d, r, rows = chunks[k]
        buf = box(u_buf, k, SLOTS)
        if d is None:
            return [(buf, outs[t].at[pl.ds(r, rows)])]
        kinds = outs[t].shape[0]
        c = ins[t].shape[2] // kinds
        columns = pl.ds(pl.multiple_of(other(me, d) * c, 128), c)
        return [(buf.at[:, pl.ds(i * c, c)], outs[t].at[i, pl.ds(r, rows), columns]) for i in range(kinds)]

    def source(k):
        t, d, r, rows = chunks[k]
        if d is None:
            return ins[t].at[pl.ds(r, rows)]
        if d == 0:
            return ins[t].at[me, pl.ds(r, rows)]
        return come[t - len(still)].at[other(me, d), pl.ds(r, rows)]

    def await_source(k):
        t, d, r, rows = chunks[k]
        if d and r == 0:
            arrival(t - len(still), d).wait_recv()

    def box(buf, k, depth):
        t, d, r, rows = chunks[k]
        return buf.at[k % depth, pl.ds(0, rows), pl.ds(0, ins[t].shape[-1])]

    def add(dst, left, right):
        rows = dst.shape[0]

        def body(i, _):
            here = pl.ds(pl.multiple_of(i * 16, 16), 16)
            dst[here] = (left[here].astype(f32) + right[here].astype(f32)).astype(bf16)
            return 0

        lax.fori_loop(0, rows // 16, body, 0)

    def end_send(k):
        return link(source(k), view(first, k), go_in, k, "seq", inward)

    def mid_cross(k):
        return link(box(t_buf, k, SLOTS), view(second, k), cross, k, "seq", opposite)

    def mid_back(k):
        return [link(src, dst, back, k, "seq", outward) for src, dst in windows(k)]

    def store(k):
        return [pltpu.make_async_copy(src, dst, stores.at[k % SLOTS]) for src, dst in windows(k)]

    def all_back(k):
        return link(box(u_buf, k, SLOTS), box(u_buf, k, SLOTS), back, k, "seq", outward)

    def all_stored(k):
        return pltpu.make_async_copy(box(u_buf, k, SLOTS), box(u_buf, k, SLOTS), stores.at[k % SLOTS])

    def finish(k):
        link(view(second, k), view(second, k), cross, k, "seq", opposite).wait_recv()
        load = pltpu.make_async_copy(view(second, k), box(b_buf, k, 2), loads.at[2])
        load.start()
        if k >= SLOTS:
            all_back(k - SLOTS).wait_send()
            all_stored(k - SLOTS).wait()
        load.wait()
        add(box(u_buf, k, SLOTS), box(t_buf, k, SLOTS), box(b_buf, k, 2))
        for copy in mid_back(k) + store(k):
            copy.start()

    count = len(chunks)
    feed(3)
    for d in range(1, 8):
        small_arrival(d).wait_recv()
    small_sum[...] = jnp.sum(small_come[...], axis=0)

    @pl.when(is_end)
    def _():
        small_hop(small_sum, small_in, 0, inward).start()

    @pl.when(jnp.logical_not(is_end))
    def _():
        small_hop(small_in, small_in, 0, outward).wait_recv()
        small_sum[...] = small_sum[...] + small_in[...]
        small_hop(small_sum, small_back, 1, opposite).start()

    for k in range(count):
        if k % 2 == 1:
            feed(1)
        await_source(k)

        @pl.when(is_end)
        def _():
            end_send(k).start()

        @pl.when(jnp.logical_not(is_end))
        def _():
            own = pltpu.make_async_copy(source(k), box(g_buf, k, 2), loads.at[0])
            own.start()
            link(view(first, k), view(first, k), go_in, k, "seq", outward).wait_recv()
            got = pltpu.make_async_copy(view(first, k), box(a_buf, k, 2), loads.at[1])
            got.start()
            if k >= SLOTS:
                mid_cross(k - SLOTS).wait_send()
            own.wait()
            got.wait()
            add(box(t_buf, k, SLOTS), box(g_buf, k, 2), box(a_buf, k, 2))
            mid_cross(k).start()
            if k >= 1:
                finish(k - 1)

    @pl.when(jnp.logical_not(is_end))
    def _():
        small_hop(small_back, small_back, 1, opposite).wait_recv()
        small_hop(small_sum, small_back, 1, opposite).wait_send()
        small_out[...] = small_sum[...] + small_back[...]
        small_hop(small_out, small_out, 2, outward).start()

    @pl.when(is_end)
    def _():
        small_hop(small_out, small_out, 2, inward).wait_recv()
        small_hop(small_sum, small_in, 0, inward).wait_send()
        for k in range(count):
            all_back(k).wait_recv()
            end_send(k).wait_send()

    @pl.when(jnp.logical_not(is_end))
    def _():
        finish(count - 1)
        small_hop(small_out, small_out, 2, outward).wait_send()
        for k in range(max(0, count - SLOTS), count):
            mid_cross(k).wait_send()
            all_back(k).wait_send()
            all_stored(k).wait()

    for t, d in begun:
        moving(t, d).wait_send()
    for d in range(1, 8):
        small_moving(d).wait_send()


def line_sum(small, still, moved, kinds, collective_id):
    if lax.axis_size("seq") != 4 or lax.axis_size("fsdp") != 8:
        out = []
        for x, count in zip(moved, kinds):
            n, rows, c = x.shape
            x = lax.psum(lax.all_to_all(x, "fsdp", split_axis=0, concat_axis=0, tiled=True), "seq")
            out.append(x.reshape(n, rows, count, c // count).transpose(2, 1, 0, 3).reshape(count, rows, n * (c // count)))
        small = lax.psum(lax.psum_scatter(small, "fsdp", scatter_dimension=0), "seq")
        return small, [lax.psum(x, "seq") for x in still], out
    still_rows = [x.shape[0] for x in still]
    moved_rows = [(x.shape[1], 128 if x.shape[2] > 1024 else 256) for x in moved]
    arrays = [*still, *moved]
    shapes = [jax.ShapeDtypeStruct(x.shape, bf16) for x in arrays]
    results = shapes[: len(still)] + [
        jax.ShapeDtypeStruct((count, x.shape[1], x.shape[0] * (x.shape[2] // count)), bf16) for x, count in zip(moved, kinds)
    ]
    count = len(chunks_of(still_rows, moved_rows))
    inside = pl.BlockSpec(memory_space=pltpu.VMEM)
    rows = max([128] + [size for _, size in moved_rows])
    width = max(x.shape[-1] for x in arrays)
    outs = pl.pallas_call(
        functools.partial(line_kernel, still_rows, moved_rows),
        in_specs=[inside] + [ANYWHERE] * len(arrays),
        out_specs=[inside] + [ANYWHERE] * (3 * len(arrays) + len(moved)),
        out_shape=[jax.ShapeDtypeStruct(small.shape[1:], f32)] + results + shapes * 2 + shapes[len(still) :],
        scratch_shapes=[pltpu.VMEM(small.shape, f32)]
        + [pltpu.VMEM(small.shape[1:], f32)] * 3
        + [pltpu.SemaphoreType.DMA((8,)), pltpu.SemaphoreType.DMA((3,)), pltpu.SemaphoreType.DMA((3,)), pltpu.SemaphoreType.DMA((8,))]
        + [pltpu.VMEM((depth, rows, width), bf16) for depth in (2, 2, SLOTS, 2, SLOTS)]
        + [pltpu.SemaphoreType.DMA((3,)), pltpu.SemaphoreType.DMA((SLOTS,))]
        + [pltpu.SemaphoreType.DMA((8,))] * (2 * len(moved))
        + [pltpu.SemaphoreType.DMA((count,))] * 6,
        compiler_params=params(collective_id, 40),
        name="line_sum",
    )(small, *arrays)
    small, *outs = outs
    return small, outs[: len(still)], outs[len(still) : len(arrays)]


def shards(
    tokens,
    doc_starts,
    norm_in,
    w_query,
    w_key,
    w_value,
    mix_bias,
    w_out,
    norm_mid,
    w_gate,
    w_up,
    w_down,
    cotangent,
):
    rows = tokens.shape[2]
    width = tokens.shape[3]
    n = lax.axis_size("fsdp")
    s = lax.axis_size("seq")
    own = NSEG * rows
    total = n * own
    seg_len = rows * n
    heads = HEADS // n
    cw = heads * HEAD_DIM
    fw = w_gate.shape[1] // n

    wgu = to_columns_in_turns([w_gate, w_up], 7)
    flat_in = tokens.reshape(own, width)
    all_in, gains, wqkv = front(flat_in, jnp.stack([norm_in, norm_mid]), [w_query, w_key, w_value], 0)
    gain_in, gain_mid = gains[0][None], gains[1][None]

    def normed(rows_in):
        rows_in = rows_in.astype(f32)
        inverse = lax.rsqrt(jnp.mean(rows_in * rows_in, axis=1, keepdims=True) + norm_eps)
        return rows_in * inverse, inverse

    flat_in = flat_in.astype(f32)
    normed_in, inv_in = normed(flat_in)
    start_row = doc_starts[0]
    docs = doc_number(start_row, jnp.arange(NSEG * seg_len, dtype=jnp.int32)).reshape(NSEG, seg_len)
    side = (docs == docs[1, 0]).astype(f32)[:, :, None]
    doc_col, doc_row = docs[:, :, None], docs[:, None, :]
    blend = jax.nn.sigmoid(mix_bias)
    blend_row = jnp.repeat(blend, HEAD_DIM)[None]
    h_in, qkv, dy, mixed, diff, lse, memory, norm_vec = attend(
        all_in, gain_in, wqkv, cotangent.reshape(own, width), doc_col, doc_row, side, blend_row, heads, 4
    )
    h_in, dy = h_in.reshape(total, width), dy.reshape(total, width)
    mixed = mixed.reshape(total, cw)

    attn_sum, _ = product_scatter(mixed.reshape(n, own, cw), w_out, False, [], 3)
    residual = flat_in + attn_sum
    inv_mid = lax.rsqrt(jnp.mean(residual * residual, axis=1, keepdims=True) + norm_eps)
    normed_mid = residual * inv_mid
    h_mid = (normed_mid * gain_mid).astype(bf16)
    h_mid, inner, d_gu, d_hmid = mlp(h_mid, wgu, w_down, dy.reshape(n, own, width), 1)
    h_mid, inner, d_gu = (x.reshape(total, x.shape[2]) for x in (h_mid, inner, d_gu))

    gain_mid_term = jnp.sum(normed_mid * d_hmid, axis=0)
    d_resid = cotangent.reshape(own, width).astype(f32) + norm_back(d_hmid * gain_mid, normed_mid, inv_mid)
    d_attn, part_down, part_gu = gather_grads(d_resid.astype(bf16), inner, dy, h_mid, d_gu, 2)
    d_attn = d_attn.reshape(total, width)
    part_gu = part_gu.reshape(n, width // n, 2 * fw)
    grad_down = lax.psum(part_down, "seq").astype(f32)

    d_mixed = mm_t(d_attn, w_out).reshape(n, NSEG, rows, cw)
    d_qkv, bias_rows = attention_back(
        qkv, d_mixed, diff, lse, doc_col, doc_row, side, blend_row, memory, norm_vec, heads
    )
    d_qkv = d_qkv.reshape(total, 3 * cw)
    bias_term = jnp.sum(bias_rows.reshape(heads, HEAD_DIM), axis=1) * blend * (1.0 - blend)

    d_hin, (part_mlp, part_out, part_qkv) = product_scatter(
        d_qkv.reshape(n, own, 3 * cw),
        wqkv,
        True,
        [(inner, w_down, False, (1, 4, 5, 6)), (mixed, d_attn, True, ()), (h_in, d_qkv, True, ())],
        5,
    )
    mlp_sum = lax.psum_scatter(part_mlp, "fsdp", scatter_dimension=0, tiled=True)
    block_out = (residual + mlp_sum.astype(f32)).astype(bf16).reshape(tokens.shape)
    part_qkv = part_qkv.reshape(n, width // n, 3 * cw)
    gain_in_term = jnp.sum(normed_in * d_hin, axis=0)
    per = width // n
    terms = jnp.stack([gain_in_term.reshape(n, per), gain_mid_term.reshape(n, per)], axis=1)
    mine = (jnp.arange(n) == lax.axis_index("fsdp"))[:, None, None]
    bias = jnp.where(mine, jnp.pad(bias_term, (0, per - heads))[None, None], 0.0)
    terms = jnp.concatenate([terms, bias, jnp.zeros((n, 5, per), f32)], axis=1)
    small, (sum_out,), (sum_gu, sum_qkv) = line_sum(terms, [part_out], [part_gu, part_qkv], [2, 3], 6)
    grad_out = sum_out.astype(f32)
    grad_gate, grad_up = sum_gu[0].astype(f32), sum_gu[1].astype(f32)
    grad_q, grad_k, grad_v = (sum_qkv[i].astype(f32) for i in range(3))
    grad_tokens = (d_resid + norm_back(d_hin * gain_in, normed_in, inv_in)).reshape(tokens.shape)

    return (
        block_out,
        grad_tokens,
        small[0],
        grad_q,
        grad_k,
        grad_v,
        small[2, :heads],
        grad_out,
        small[1],
        grad_gate,
        grad_up,
        grad_down,
    )


def solution(mesh):
    whole = P("seq", None, "fsdp", None)
    matrix, vector = P("fsdp", None), P("fsdp")
    return jax.shard_map(
        shards,
        mesh=mesh,
        in_specs=(whole, P("seq", None), vector, matrix, matrix, matrix, vector, matrix, vector, matrix, matrix, matrix, whole),
        out_specs=(whole, whole, vector, matrix, matrix, matrix, vector, matrix, vector, matrix, matrix, matrix),
        check_vma=False,
    )
```

```python
import functools

import jax
import jax.numpy as jnp
from jax import lax
from jax.experimental import pallas as pl
from jax.experimental.pallas import tpu as pltpu
from jax.sharding import PartitionSpec as P

HEADS = 16
HEAD_DIM = 128
NSEG = 2

highest = lax.Precision.HIGHEST
norm_eps = 1e-05
f32 = jnp.float32
bf16 = jnp.bfloat16


def doc_number(start_row, places):
    return jnp.sum((start_row[None, :] <= places[:, None]).astype(jnp.int32), axis=1) - 1


def norm_back(grad_in, normed, inverse):
    return inverse * (grad_in - normed * jnp.mean(grad_in * normed, axis=-1, keepdims=True))


def mm(a, b):
    return lax.dot_general(a, b, (((1,), (0,)), ((), ())), preferred_element_type=f32)


def mm_t(a, b):
    return lax.dot_general(a, b, (((1,), (1,)), ((), ())), preferred_element_type=f32)


def t_mm(a, b):
    return lax.dot_general(a, b, (((0,), (0,)), ((), ())), preferred_element_type=f32)


def dots(a, b, ca, cb, precision=None):
    return lax.dot_general(a, b, (((ca,), (cb,)), ((), ())), preferred_element_type=f32, precision=precision)


def phi(u):
    return jnp.where(u > 0, u + 1.0, jnp.exp(jnp.minimum(u, 0.0)))


def phi_slope(u):
    return jnp.where(u > 0, 1.0, jnp.exp(jnp.minimum(u, 0.0)))


def attention_head(h, heads, segment, qkv_ref, doc_col, doc_row, side_ref, blend_ref, mixed_ref, diff_ref, lse_ref, mem_ref, nv_ref):
    n, _, rows, _ = qkv_ref.shape
    cw = heads * HEAD_DIM
    take = max(1, 256 // rows)
    block = take * rows
    scale = HEAD_DIM ** (-0.5)

    def part(kind, h, lo, hi):
        cols = slice(kind * cw + h * HEAD_DIM, kind * cw + (h + 1) * HEAD_DIM)
        return qkv_ref[lo:hi, 0, :, cols].reshape((hi - lo) * rows, HEAD_DIM)

    cols = slice(h * HEAD_DIM, (h + 1) * HEAD_DIM)

    @pl.when(segment == 0)
    def _():
        fk = phi(part(1, h, 0, n).astype(f32)) * side_ref[0]
        mem_ref[h] = dots(fk, part(2, h, 0, n).astype(f32), 0, 0, highest)
        nv_ref[h] = jnp.sum(fk, axis=0, keepdims=True)

    blend = blend_ref[:, cols]
    for i in range(n // take):
        lo, hi = i * take, (i + 1) * take
        span = (i + 1) * block
        q = part(0, h, lo, hi)
        s = dots(q, part(1, h, 0, hi), 1, 1) * scale
        at = lax.broadcasted_iota(jnp.int32, (block, span), 0) + i * block
        allowed = (lax.broadcasted_iota(jnp.int32, (block, span), 1) <= at) & (
            doc_row[0, :, :span] == doc_col[0, i * block : (i + 1) * block]
        )
        s = jnp.where(allowed, s, -1000000000.0)
        top = jnp.max(s, axis=1, keepdims=True)
        p = jnp.exp(s - top)
        tot = jnp.sum(p, axis=1, keepdims=True)
        lse_ref[h, 0, i * block : (i + 1) * block] = top + jnp.log(tot)
        direct = dots((p / tot).astype(bf16), part(2, h, 0, hi), 1, 0)
        shape = (take, rows, HEAD_DIM)

        @pl.when(segment == 0)
        def _():
            mixed_ref[lo:hi, 0, :, cols] = ((1.0 - blend) * direct).astype(bf16).reshape(shape)
            diff_ref[lo:hi, 0, :, cols] = (-direct).reshape(shape)

        @pl.when(segment != 0)
        def _():
            fq = phi(q.astype(f32))
            numer = dots(fq, mem_ref[h], 1, 0, highest)
            den = jnp.sum(fq * nv_ref[h], axis=1, keepdims=True) + 1.0
            ret = side_ref[0, i * block : (i + 1) * block] * numer / den
            mixed_ref[lo:hi, 0, :, cols] = (blend * ret + (1.0 - blend) * direct).astype(bf16).reshape(shape)
            diff_ref[lo:hi, 0, :, cols] = (ret - direct).reshape(shape)


def attention_kernel(heads, *refs):
    for h in range(heads):
        attention_head(h, heads, pl.program_id(0), *refs)


def attention_back_kernel(
    heads, qkv_ref, dmix_ref, diff_ref, lse_ref, doc_col, doc_row, side_ref, blend_ref, mem_ref, nv_ref,
    out_ref, bias_ref, dk_acc, dv_acc, dmem, dnv,
):
    n, _, rows, _ = qkv_ref.shape
    length = n * rows
    cw = heads * HEAD_DIM
    take = max(1, 256 // rows)
    block = take * rows
    scale = HEAD_DIM ** (-0.5)
    step = pl.program_id(0)
    shape = (take, rows, HEAD_DIM)

    def part(kind, h, lo, hi):
        cols = slice(kind * cw + h * HEAD_DIM, kind * cw + (h + 1) * HEAD_DIM)
        return qkv_ref[lo:hi, 0, :, cols].reshape((hi - lo) * rows, HEAD_DIM)

    @pl.when(step == 0)
    def _():
        bias_ref[...] = jnp.zeros_like(bias_ref)
        dmem[...] = jnp.zeros_like(dmem)
        dnv[...] = jnp.zeros_like(dnv)

    for h in range(heads):
        cols = slice(h * HEAD_DIM, (h + 1) * HEAD_DIM)
        blend = blend_ref[:, cols]
        dk_acc[...] = jnp.zeros_like(dk_acc)
        dv_acc[...] = jnp.zeros_like(dv_acc)
        for i in range(n // take):
            lo, hi = i * take, (i + 1) * take
            span = (i + 1) * block
            here = slice(i * block, (i + 1) * block)
            q, k, v = part(0, h, lo, hi), part(1, h, 0, hi), part(2, h, 0, hi)
            dmix = dmix_ref[lo:hi, 0, :, cols].reshape(block, HEAD_DIM)
            bias_ref[:, cols] += jnp.sum(dmix * diff_ref[lo:hi, 0, :, cols].reshape(block, HEAD_DIM), axis=0, keepdims=True)
            ddir = ((1.0 - blend) * dmix).astype(bf16)
            s = dots(q, k, 1, 1) * scale
            at = lax.broadcasted_iota(jnp.int32, (block, span), 0) + i * block
            allowed = (lax.broadcasted_iota(jnp.int32, (block, span), 1) <= at) & (
                doc_row[0, :, :span] == doc_col[0, here]
            )
            e = jnp.exp(jnp.where(allowed, s, -1000000000.0) - lse_ref[h, 0, here])
            dp = dots(ddir, v, 1, 1)
            bal = jnp.sum(e * dp, axis=1, keepdims=True)
            ds = (e * (dp - bal)).astype(bf16)
            dv_acc[:span] += dots(e.astype(bf16), ddir, 0, 0)
            dk_acc[:span] += dots(ds, q, 0, 0) * scale
            dq = dots(ds, k, 1, 0) * scale

            @pl.when(step != 0)
            def _():
                out_ref[lo:hi, 0, :, cols] = dq.astype(bf16).reshape(shape)

            @pl.when(step == 0)
            def _():
                q32 = q.astype(f32)
                fq = phi(q32)
                numer = dots(fq, mem_ref[h], 1, 0, highest)
                den = jnp.sum(fq * nv_ref[h], axis=1, keepdims=True) + 1.0
                dnum = side_ref[0, here] * (blend * dmix) / den
                dden = -jnp.sum(dnum * numer, axis=1, keepdims=True) / den
                dmem[h] += dots(fq, dnum, 0, 0, highest)
                dnv[h] += jnp.sum(dden * fq, axis=0, keepdims=True)
                dfq = dots(dnum, mem_ref[h], 1, 1, highest) + dden * nv_ref[h]
                out_ref[lo:hi, 0, :, cols] = (dq + dfq * phi_slope(q32)).astype(bf16).reshape(shape)

        whole = (n, rows, HEAD_DIM)
        kcols = slice(cw + h * HEAD_DIM, cw + (h + 1) * HEAD_DIM)
        vcols = slice(2 * cw + h * HEAD_DIM, 2 * cw + (h + 1) * HEAD_DIM)

        @pl.when(step == 0)
        def _():
            out_ref[:, 0, :, kcols] = dk_acc[...].astype(bf16).reshape(whole)
            out_ref[:, 0, :, vcols] = dv_acc[...].astype(bf16).reshape(whole)

        @pl.when(step != 0)
        def _():
            k32 = part(1, h, 0, n).astype(f32)
            v32 = part(2, h, 0, n).astype(f32)
            key_set = side_ref[0]
            mem_v = key_set * dots(phi(k32), dmem[h], 1, 0, highest)
            mem_k = key_set * (dots(v32, dmem[h], 1, 1, highest) + dnv[h]) * phi_slope(k32)
            out_ref[:, 0, :, kcols] = (dk_acc[...] + mem_k).astype(bf16).reshape(whole)
            out_ref[:, 0, :, vcols] = (dv_acc[...] + mem_v).astype(bf16).reshape(whole)


def attention_specs(n, rows, heads, pick):
    length = n * rows
    cw = heads * HEAD_DIM
    wide = pl.BlockSpec((n, 1, rows, 3 * cw), lambda g: (0, pick(g), 0, 0))
    narrow = pl.BlockSpec((n, 1, rows, cw), lambda g: (0, pick(g), 0, 0))
    lse = pl.BlockSpec((heads, 1, length, 1), lambda g: (0, pick(g), 0, 0))
    col = pl.BlockSpec((1, length, 1), lambda g: (pick(g), 0, 0))
    row = pl.BlockSpec((1, 1, length), lambda g: (pick(g), 0, 0))
    line = pl.BlockSpec((1, cw), lambda g: (0, 0))
    mem = pl.BlockSpec((heads, HEAD_DIM, HEAD_DIM), lambda g: (0, 0, 0))
    nv = pl.BlockSpec((heads, 1, HEAD_DIM), lambda g: (0, 0, 0))
    return wide, narrow, lse, col, row, line, mem, nv


def attention(qkv, doc_col, doc_row, side, blend, heads):
    n, _, rows, _ = qkv.shape
    length = n * rows
    cw = heads * HEAD_DIM
    wide, narrow, lse, col, row, line, mem, nv = attention_specs(n, rows, heads, lambda g: g)
    pairs = heads * NSEG * length * length // 2
    return pl.pallas_call(
        functools.partial(attention_kernel, heads),
        grid=(NSEG,),
        in_specs=[wide, col, row, col, line],
        out_specs=[narrow, narrow, lse, mem, nv],
        out_shape=[
            jax.ShapeDtypeStruct((n, NSEG, rows, cw), bf16),
            jax.ShapeDtypeStruct((n, NSEG, rows, cw), f32),
            jax.ShapeDtypeStruct((heads, NSEG, length, 1), f32),
            jax.ShapeDtypeStruct((heads, HEAD_DIM, HEAD_DIM), f32),
            jax.ShapeDtypeStruct((heads, 1, HEAD_DIM), f32),
        ],
        compiler_params=pltpu.CompilerParams(vmem_limit_bytes=48 << 20),
        cost_estimate=pl.CostEstimate(flops=pairs * 4 * HEAD_DIM, transcendentals=pairs, bytes_accessed=8 << 20),
        name="attention",
    )(qkv, doc_col, doc_row, side, blend)


def attention_back(qkv, dmix, diff, lse_rows, doc_col, doc_row, side, blend, mem_all, nv_all, heads):
    n, _, rows, _ = qkv.shape
    length = n * rows
    cw = heads * HEAD_DIM
    wide, narrow, lse, col, row, line, mem, nv = attention_specs(n, rows, heads, lambda g: NSEG - 1 - g)
    pairs = heads * NSEG * length * length // 2
    return pl.pallas_call(
        functools.partial(attention_back_kernel, heads),
        grid=(NSEG,),
        in_specs=[wide, narrow, narrow, lse, col, row, col, line, mem, nv],
        out_specs=[wide, line],
        out_shape=[
            jax.ShapeDtypeStruct((n, NSEG, rows, 3 * cw), bf16),
            jax.ShapeDtypeStruct((1, cw), f32),
        ],
        scratch_shapes=[
            pltpu.VMEM((length, HEAD_DIM), f32),
            pltpu.VMEM((length, HEAD_DIM), f32),
            pltpu.VMEM((heads, HEAD_DIM, HEAD_DIM), f32),
            pltpu.VMEM((heads, 1, HEAD_DIM), f32),
        ],
        compiler_params=pltpu.CompilerParams(vmem_limit_bytes=56 << 20),
        cost_estimate=pl.CostEstimate(flops=pairs * 10 * HEAD_DIM, transcendentals=pairs, bytes_accessed=16 << 20),
        name="attention_back",
    )(qkv, dmix, diff, lse_rows, doc_col, doc_row, side, blend, mem_all, nv_all)


def flip(index, bit):
    return index + bit - 2 * bit * lax.rem(lax.div(index, bit), 2)


def other(index, bits):
    for bit in (1, 2, 4):
        if bits & bit:
            index = flip(index, bit)
    return index


def link(src, dst, sems, slot, axis, peer):
    return pltpu.make_async_remote_copy(
        src_ref=src, dst_ref=dst, send_sem=sems[0].at[slot], recv_sem=sems[1].at[slot],
        device_id={axis: peer}, device_id_type=pl.DeviceIdType.MESH,
    )


def send(src, dst, sems, slot, peer):
    return link(src, dst, sems, slot, "fsdp", peer)


def greet(peers):
    barrier = pltpu.get_barrier_semaphore()
    for peer in peers:
        pl.semaphore_signal(barrier, inc=1, device_id={"fsdp": peer}, device_id_type=pl.DeviceIdType.MESH)
    pl.semaphore_wait(barrier, len(peers))


PIECES = 4
ORDER = (0, 1, 2, 4, 3, 5, 6, 7)
GATHER_SEMS = [pltpu.SemaphoreType.DMA] + [pltpu.SemaphoreType.DMA((PIECES,))] * 14


def gather_parts(x_ref, out_ref, local_sem, *sems, own_first=False):
    me = lax.axis_index("fsdp")
    sib, xn, yn, far_owner = flip(me, 1), flip(me, 2), flip(me, 4), other(me, 6)
    rows = x_ref.shape[0] // PIECES
    half = PIECES // 2
    own, over_x, over_y, far = sems[0:2], sems[2:4], sems[4:6], sems[6:8]
    side_x, side_y, side_far = sems[8:10], sems[10:12], sems[12:14]
    started = []

    def at(owner, c):
        return out_ref.at[owner, pl.ds(c * rows, rows)]

    def mine(c):
        return x_ref.at[pl.ds(c * rows, rows)]

    def go(make):
        make().start()
        started.append(make)

    def pass_on(owner, c, sems, peer):
        go(lambda: send(at(owner, c), at(owner, c), sems, c, peer))

    def arrived(owner, c, sems):
        send(at(owner, c), at(owner, c), sems, c, sib).wait_recv()

    local = pltpu.make_async_copy(x_ref, out_ref.at[me], local_sem)

    def begin_one(c, sems, peer):
        return send(mine(c), at(me, c), sems, c, peer)

    def begin():
        local.start()
        for j in range(PIECES):
            c, d = j, (j + half) % PIECES
            go(functools.partial(begin_one, c, over_x, xn))
            go(functools.partial(begin_one, d, over_y, yn))
        for c in range(PIECES):
            go(functools.partial(begin_one, c, own, sib))
        if own_first:
            local.wait()

    def near(j):
        c, d = j, (j + half) % PIECES
        arrived(xn, c, over_x)
        if c < half:
            pass_on(xn, c, far, yn)
        pass_on(xn, c, side_x, sib)
        arrived(yn, d, over_y)
        if d >= half:
            pass_on(yn, d, far, xn)
        pass_on(yn, d, side_y, sib)

    def beyond(j):
        for c in (j, j + half):
            arrived(far_owner, c, far)
            pass_on(far_owner, c, side_far, sib)

    def wait_from(d):
        for c in range(PIECES):
            arrived(other(me, d), c, {1: own, 3: side_x, 5: side_y, 7: side_far}[d])

    def end():
        for make in started:
            make().wait_send()
        if not own_first:
            local.wait()

    near_steps = [functools.partial(near, j) for j in range(PIECES)]
    far_steps = [functools.partial(beyond, j) for j in range(half)]
    return [begin, *near_steps, *far_steps, wait_from, end]


def gather_steps(x_ref, out_ref, *sems):
    *steps, wait_from, end = gather_parts(x_ref, out_ref, *sems)

    def finish():
        for d in (1, 3, 5, 7):
            wait_from(d)
        end()

    return [*steps, finish]


def params(collective_id, mib=32):
    return pltpu.CompilerParams(collective_id=collective_id, has_side_effects=True, vmem_limit_bytes=mib << 20)


ANYWHERE = pl.BlockSpec(memory_space=pltpu.HBM)


def move_steps(ins, out_ref, first, rows, sems, local_sem):
    me = lax.axis_index("fsdp")
    count = len(ins)
    c = out_ref.shape[1] // count

    def piece(kind, d):
        peer = other(me, d)
        src = ins[kind].at[pl.ds(first, rows), pl.ds(pl.multiple_of(peer * c, 128), c)]
        dst = out_ref.at[pl.ds(pl.multiple_of(me * rows, 16), rows), pl.ds(kind * c, c)]
        return src, dst, peer

    def moving(kind, d):
        src, dst, peer = piece(kind, d)
        return send(src, dst, sems, d * count + kind, peer)

    def local(kind):
        src, dst, _ = piece(kind, 0)
        return pltpu.make_async_copy(src, dst, local_sem.at[kind])

    def begin():
        for d in (6, 7, 2, 4, 3, 5, 1):
            for kind in range(count):
                moving(kind, d).start()
        for kind in range(count):
            local(kind).start()

    def end():
        for d in ORDER[1:]:
            for kind in range(count):
                there = out_ref.at[pl.ds(pl.multiple_of(other(me, d) * rows, 16), rows), pl.ds(kind * c, c)]
                send(there, there, sems, d * count + kind, other(me, d)).wait_recv()
                moving(kind, d).wait_send()
        for kind in range(count):
            local(kind).wait()

    return [begin, end]


def move_kernel(count, rows, *refs):
    ins, (out_ref, local_sem, *sems) = refs[:count], refs[count:]
    me = lax.axis_index("fsdp")
    greet([other(me, d) for d in range(1, 8)])
    for step in move_steps(ins, out_ref, lax.axis_index("seq") * rows, rows, sems, local_sem):
        step()


def to_columns(weights, first, rows):
    n = lax.axis_size("fsdp")
    cols = weights[0].shape[1]
    weights = [lax.dynamic_slice_in_dim(w, first, rows, 0) for w in weights]
    parts = jnp.stack([w.reshape(rows, n, cols // n) for w in weights], axis=2)
    parts = parts.reshape(rows, n, len(weights) * (cols // n))
    out = lax.all_to_all(parts, "fsdp", split_axis=1, concat_axis=0, tiled=True)
    return out.reshape(n * rows, len(weights) * (cols // n))


def to_columns_in_turns(weights, collective_id):
    n, s = lax.axis_size("fsdp"), lax.axis_size("seq")
    count = len(weights)
    share = weights[0].shape[0] // s
    width = count * (weights[0].shape[1] // n)
    if n != 8:
        part = to_columns(weights, lax.axis_index("seq") * share, share)
    else:
        part = pl.pallas_call(
            functools.partial(move_kernel, count, share),
            in_specs=[ANYWHERE] * count,
            out_specs=ANYWHERE,
            out_shape=jax.ShapeDtypeStruct((n * share, width), bf16),
            scratch_shapes=[pltpu.SemaphoreType.DMA((count,))] + [pltpu.SemaphoreType.DMA((n * count,))] * 2,
            compiler_params=params(collective_id),
            name="move",
        )(*weights)
    part = part.reshape(n, share, width)
    return lax.all_gather(part, "seq", axis=1, tiled=True).reshape(n * share * s, width)


def front_kernel(count, *refs):
    x_ref, gain_ref, *refs = refs
    ins, refs = refs[:count], refs[count:]
    out_ref, gains_ref, w_ref, *sems = refs
    gain_sems, sems = sems[:3], sems[3:]
    move_sems, sems = sems[:3], sems[3:]
    me = lax.axis_index("fsdp")
    greet([other(me, d) for d in range(1, 8)])

    def gain(d):
        return send(gain_ref, gains_ref.at[me], gain_sems[1:], d, other(me, d))

    own = pltpu.make_async_copy(gain_ref, gains_ref.at[me], gain_sems[0])
    own.start()
    for d in range(1, 8):
        gain(d).start()
    first, *steps = gather_steps(x_ref, out_ref, *sems)
    begin, end = move_steps(ins, w_ref, 0, ins[0].shape[0], move_sems[1:], move_sems[0])
    first()
    begin()
    for step in steps:
        step()
    end()
    own.wait()
    for d in range(1, 8):
        there = gains_ref.at[other(me, d)]
        send(there, there, gain_sems[1:], d, other(me, d)).wait_recv()
        gain(d).wait_send()


def front(x, gains, weights, collective_id):
    n = lax.axis_size("fsdp")
    if n != 8:
        return (
            lax.all_gather(x, "fsdp", axis=0),
            lax.all_gather(gains, "fsdp", axis=1, tiled=True),
            to_columns(weights, 0, weights[0].shape[0]),
        )
    count = len(weights)
    kinds, c = gains.shape
    gains = jnp.concatenate([gains, jnp.zeros((8 - kinds, c), f32)])
    rows, cols = weights[0].shape
    sems = pltpu.SemaphoreType.DMA
    x, gains, w = pl.pallas_call(
        functools.partial(front_kernel, count),
        in_specs=[ANYWHERE] * (2 + count),
        out_specs=[ANYWHERE] * 3,
        out_shape=[
            jax.ShapeDtypeStruct((n, *x.shape), x.dtype),
            jax.ShapeDtypeStruct((n, 8, c), f32),
            jax.ShapeDtypeStruct((n * rows, count * (cols // n)), bf16),
        ],
        scratch_shapes=[sems, sems((8,)), sems((8,)), sems((count,)), sems((8 * count,)), sems((8 * count,)), *GATHER_SEMS],
        compiler_params=params(collective_id),
        name="front",
    )(x, gains, *weights)
    return x, gains[:, :kinds].transpose(1, 0, 2).reshape(kinds, n * c), w


def attend_kernel(heads, all_ref, gain_ref, w_ref, dy_ref, doc_col, doc_row, side_ref, blend_ref, *refs):
    h_out, qkv_out, dy_out, mixed_ref, diff_ref, lse_ref, mem_ref, nv_ref, x, w, hid, qkv, load_sems, x_sems, h_sems, q_sems, *sems = refs
    n, tokens, width = all_ref.shape
    rows = tokens // NSEG
    me = lax.axis_index("fsdp")
    weights = pltpu.make_async_copy(w_ref, w, load_sems.at[0])
    weights.start()

    def load(i):
        return pltpu.make_async_copy(all_ref.at[i], x.at[rest(i, 2)], x_sems.at[rest(i, 2)])

    def store(i):
        return pltpu.make_async_copy(hid.at[rest(i, 2)], h_out.at[i], h_sems.at[rest(i, 2)])

    load(0).start()
    greet([other(me, d) for d in (1, 2, 4)])
    begin, near0, near1, near2, near3, far0, far1, wait_from, end = gather_parts(dy_ref, dy_out, *sems)
    begin()
    weights.wait()

    def project(i, _):
        slot = rest(i, 2)
        for at, fn in ((3, near0), (6, near1)):

            @pl.when(i == at)
            def _():
                fn()

        @pl.when(i < n - 1)
        def _():
            load(i + 1).start()

        @pl.when(i > 1)
        def _():
            store(i - 2).wait()

        load(i).wait()
        for r in range(0, tokens, 64):
            here = x[slot, r : r + 64].astype(f32)
            inverse = lax.rsqrt(jnp.mean(here * here, axis=1, keepdims=True) + norm_eps)
            hid[slot, r : r + 64] = (here * inverse * gain_ref[...]).astype(bf16)
        store(i).start()
        made = jnp.dot(hid[slot], w[...], preferred_element_type=f32).astype(bf16)
        qkv[i] = made.reshape(NSEG, rows, made.shape[1])
        return 0

    lax.fori_loop(0, n, project, 0)
    store(n - 2).wait()
    store(n - 1).wait()
    keep = pltpu.make_async_copy(qkv, qkv_out, q_sems.at[0])
    keep.start()
    hooks = {(0, 0): near2, (0, heads - 1): near3, (1, 0): far0, (1, heads - 1): far1} if heads > 1 else {}

    def segment(i, _):
        here = pl.ds(i, 1)
        for h in range(heads):
            for (seg, at), fn in hooks.items():
                if at == h:

                    @pl.when(i == seg)
                    def _():
                        fn()

            attention_head(
                h, heads, i, qkv.at[:, here], doc_col.at[here], doc_row.at[here], side_ref.at[here], blend_ref,
                mixed_ref.at[:, here], diff_ref.at[:, here], lse_ref.at[:, here], mem_ref, nv_ref,
            )
        return 0

    lax.fori_loop(0, NSEG, segment, 0)
    for d in (1, 3, 5, 7):
        wait_from(d)
    end()
    keep.wait()


def attend(x_all, gain, wqkv, dy, doc_col, doc_row, side, blend, heads, collective_id):
    n, tokens, width = x_all.shape
    rows = tokens // NSEG
    cw = heads * HEAD_DIM
    if n != 8 or heads == 1:
        here = x_all.reshape(n * tokens, width).astype(f32)
        inverse = lax.rsqrt(jnp.mean(here * here, axis=1, keepdims=True) + norm_eps)
        h_in = (here * inverse * gain).astype(bf16)
        qkv = mm(h_in, wqkv).astype(bf16).reshape(n, NSEG, rows, 3 * cw)
        dy = lax.all_gather(dy, "fsdp", axis=0)
        return h_in.reshape(x_all.shape), qkv, dy, *attention(qkv, doc_col, doc_row, side, blend, heads)
    length = n * rows
    sems = pltpu.SemaphoreType.DMA
    inside = pl.BlockSpec(memory_space=pltpu.VMEM)
    pairs = heads * NSEG * length * length // 2
    return pl.pallas_call(
        functools.partial(attend_kernel, heads),
        in_specs=[ANYWHERE, inside, ANYWHERE, ANYWHERE] + [inside] * 4,
        out_specs=[ANYWHERE] * 3 + [inside] * 5,
        out_shape=[
            jax.ShapeDtypeStruct(x_all.shape, bf16),
            jax.ShapeDtypeStruct((n, NSEG, rows, 3 * cw), bf16),
            jax.ShapeDtypeStruct((n, *dy.shape), bf16),
            jax.ShapeDtypeStruct((n, NSEG, rows, cw), bf16),
            jax.ShapeDtypeStruct((n, NSEG, rows, cw), f32),
            jax.ShapeDtypeStruct((heads, NSEG, length, 1), f32),
            jax.ShapeDtypeStruct((heads, HEAD_DIM, HEAD_DIM), f32),
            jax.ShapeDtypeStruct((heads, 1, HEAD_DIM), f32),
        ],
        scratch_shapes=[
            pltpu.VMEM((2, tokens, width), bf16),
            pltpu.VMEM(wqkv.shape, bf16),
            pltpu.VMEM((2, tokens, width), bf16),
            pltpu.VMEM((n, NSEG, rows, 3 * cw), bf16),
            *[sems((k,)) for k in (1, 2, 2, 1)],
            *GATHER_SEMS,
        ],
        compiler_params=params(collective_id, 48),
        cost_estimate=pl.CostEstimate(
            flops=pairs * 4 * HEAD_DIM + 6 * n * tokens * width * cw, transcendentals=pairs, bytes_accessed=32 << 20
        ),
        name="attend",
    )(x_all, gain, wqkv, dy, doc_col, doc_row, side, blend)


def quotient(a, b):
    return a // b if isinstance(a, int) else lax.div(a, b)


def rest(a, b):
    return a % b if isinstance(a, int) else lax.rem(a, b)


def xor(index, bits):
    total = 0
    for bit in (1, 2, 4):
        a, b = rest(quotient(index, bit), 2), rest(quotient(bits, bit), 2)
        total = total + bit * (a + b - 2 * a * b)
    return total


def nth_block(i):
    return i + quotient(i, 4) * (2 - 4 * rest(quotient(i, 2), 2))


def mlp_kernel(own_ref, wgu_ref, wd_ref, dy_ref, h_out, inner_out, dgu_out, down_out, out_ref, *refs):
    wgu, wd, h, dy, inner, dgu, mine, side, near, last, weight_sems, dy_sems, h_sems, inner_sems, dgu_sems, *sems = refs
    gather_sems, sems = sems[:15], sems[15:]
    me = lax.axis_index("fsdp")
    sib, xn, yn = flip(me, 1), flip(me, 2), flip(me, 4)
    tokens, width = own_ref.shape
    fw = wd.shape[0]
    begin, near0, near1, near2, near3, far0, far1, wait_from, gather_end = gather_parts(own_ref, h, *gather_sems, own_first=True)
    back = scatter_parts(mine, side, near, last, out_ref, sems)
    loads = [
        pltpu.make_async_copy(wgu_ref, wgu, weight_sems.at[0]),
        pltpu.make_async_copy(wd_ref, wd, weight_sems.at[1]),
    ]
    for load in loads:
        load.start()

    def load_dy(i):
        owner = xor(me, nth_block(i))
        return pltpu.make_async_copy(dy_ref.at[owner], dy.at[owner], dy_sems.at[i])

    for i in range(8):
        load_dy(i).start()
    greet([sib, xn, yn])
    begin()
    back_x, back_far = back["combine"](2), back["combine"](6)
    hooks = {
        (0, 6): [near0],
        (1, 0): [lambda: wait_from(1)],
        (1, 2): [near1],
        (1, 6): [near2],
        (2, 0): [near3],
        (2, 6): [far0],
        (3, 0): [lambda: wait_from(3)],
        (3, 4): [far1],
        (4, 3): [back_x],
        (5, 0): [lambda: wait_from(7)],
        (6, 3): [back_far],
        (7, 0): [lambda: wait_from(5)],
        (7, 4): [lambda: back["onward"](0)],
        (7, 6): [lambda: back["onward"](1)],
    }
    loads[0].wait()
    loads[1].wait()
    tile = fw // 4
    wide = width // 4

    def store(i):
        slot = rest(i, 2)
        return pltpu.make_async_copy(dgu.at[slot], dgu_out.at[xor(me, nth_block(i))], dgu_sems.at[slot])

    def keep(i):
        owner = xor(me, nth_block(i))
        return pltpu.make_async_copy(h.at[owner], h_out.at[owner], h_sems.at[i])

    def keep_inner(i):
        owner = xor(me, nth_block(i))
        return pltpu.make_async_copy(inner.at[owner], inner_out.at[owner], inner_sems.at[i])

    def body(i, _):
        slot = rest(i, 2)
        block = nth_block(i)
        owner = xor(me, block)

        def point(p):
            for (step, at), fns in hooks.items():
                if at == p:

                    @pl.when(i == step)
                    def _():
                        for fn in fns:
                            fn()

        @pl.when(i > 1)
        def _():
            store(i - 2).wait()

        for t in range(4):
            point(t)
            if t == 0:
                keep(i).start()
                load_dy(i).wait()
            left = h[owner]
            cols = slice(t * tile, (t + 1) * tile)
            gate = jnp.dot(left, wgu[:, cols], preferred_element_type=f32)
            up = jnp.dot(left, wgu[:, fw + t * tile : fw + (t + 1) * tile], preferred_element_type=f32)
            back_in = dots(dy[owner], wd[cols], 1, 1)
            sig = jax.nn.sigmoid(gate)
            act = gate * sig
            inner[owner, :, cols] = (act * up).astype(bf16)
            dgu[slot, :, cols] = (back_in * up * (sig * (1.0 + gate * (1.0 - sig)))).astype(bf16)
            dgu[slot, :, fw + t * tile : fw + (t + 1) * tile] = (back_in * act).astype(bf16)
        keep_inner(i).start()
        store(i).start()
        for t in range(4):
            point(4 + t)
            cols = slice(t * wide, (t + 1) * wide)
            mine[block, :, cols] = dots(dgu[slot], wgu[cols], 1, 1).astype(bf16)

        @pl.when(lax.rem(block, 2) == 1)
        def _():
            back["to_core"](block).start()

        return 0

    lax.fori_loop(0, 8, body, 0)
    back["combine"](4)()
    back["onward"](2)
    back["combine"](0)()
    store(6).wait()
    store(7).wait()

    def keep_down(t):
        return pltpu.make_async_copy(dgu.at[t % 2], down_out.at[pl.ds(t * tile, tile)], dgu_sems.at[t % 2])

    for t in range(4):
        if t > 1:
            keep_down(t - 2).wait()
        left = inner[:, :, t * tile : (t + 1) * tile].reshape(8 * tokens, tile)
        for at in range(0, width, wide):
            right = dy[:, :, at : at + wide].reshape(8 * tokens, wide)
            dgu[t % 2, :, at : at + wide] = dots(left, right, 0, 0).astype(bf16)
        keep_down(t).start()
    back["finish"]()
    keep_down(2).wait()
    keep_down(3).wait()
    for i in range(8):
        keep(i).wait()
        keep_inner(i).wait()
    gather_end()


def scatter_parts(mine, side, near, last, out_ref, sems):
    me = lax.axis_index("fsdp")
    sib, xn, yn = flip(me, 1), flip(me, 2), flip(me, 4)
    rows = out_ref.shape[0] // PIECES
    half = PIECES // 2
    core, sems = sems[:2], sems[2:]
    hop = {"xf": sems[0:2], "xo": sems[2:4], "yf": sems[4:6], "yo": sems[6:8], "last": sems[8:10]}

    def to_core(d):
        kind = quotient(d, 2)
        return send(mine.at[d], side.at[kind], core, kind, sib)

    def span(c):
        return pl.ds(c * rows, rows)

    def go(copy):
        copy.start()

    def travel(d, c):
        if d == 6:
            return send(mine.at[6, span(c)], near.at[0, span(c)], hop["xf" if c < half else "yf"], c, xn if c < half else yn)
        if d == 2:
            return send(mine.at[2, span(c)], near.at[1, span(c)], hop["xo"], c, xn)
        return send(mine.at[4, span(c)], near.at[1, span(c)], hop["yo"], c, yn)

    def leaves(d, c):
        return d == 6 or (d == 2 and c < half) or (d == 4 and c >= half)

    def step_on(c):
        return send(mine.at[4 if c < half else 2, span(c)], last.at[span(c)], hop["last"], c, yn if c < half else xn)

    def add(d, c, ref):
        total = mine.at[d]

        def body(i, _):
            here = pl.ds(pl.multiple_of(c * rows + i * 16, 16), 16)
            total[here] = (total[here].astype(f32) + ref[here].astype(f32)).astype(bf16)
            return 0

        lax.fori_loop(0, rows // 16, body, 0)

    def combine(d):
        def run():
            send(side.at[d // 2], side.at[d // 2], core, d // 2, sib).wait_recv()
            for c in range(PIECES):
                add(d, c, side.at[d // 2])
                if leaves(d, c):
                    go(travel(d, c))

        return run

    def onward(which):
        for c in range(half) if which == 2 else [half + which]:
            d = 4 if c < half else 2
            send(near.at[0, span(c)], near.at[0, span(c)], hop["xf" if c < half else "yf"], c, xn).wait_recv()
            add(d, c, near.at[0])
            go(step_on(c))

    def finish():
        total, came = mine.at[0], near.at[1]
        for j in range(half):
            for c in (j + half, j):
                send(near.at[1, span(c)], near.at[1, span(c)], hop["xo" if c < half else "yo"], c, xn).wait_recv()
                send(last.at[span(c)], last.at[span(c)], hop["last"], c, xn).wait_recv()

                def body(i, _):
                    here = pl.ds(pl.multiple_of(c * rows + i * 16, 16), 16)
                    out_ref[here] = total[here].astype(f32) + came[here].astype(f32) + last[here].astype(f32)
                    return 0

                lax.fori_loop(0, rows // 16, body, 0)
        for d in (1, 3, 5, 7):
            to_core(d).wait_send()
        for d in (2, 4, 6):
            for c in range(PIECES):
                if leaves(d, c):
                    travel(d, c).wait_send()
        for c in range(PIECES):
            step_on(c).wait_send()

    return {"to_core": to_core, "combine": combine, "onward": onward, "finish": finish}


SCATTER_SEMS = [pltpu.SemaphoreType.DMA((4,))] * 2 + [pltpu.SemaphoreType.DMA((PIECES,))] * 10


def scatter_boxes(rows, columns):
    return [pltpu.VMEM((k, rows, columns), bf16) for k in (8, 4, 2)] + [pltpu.VMEM((rows, columns), bf16)]


def mlp(h_own, wgu, w_down, dy, collective_id):
    n, rows, width = dy.shape
    fw = w_down.shape[0]
    if n != 8:
        h = lax.all_gather(h_own, "fsdp", axis=0)
        gate_up = mm(h.reshape(n * rows, width), wgu)
        gate, up = gate_up[:, :fw], gate_up[:, fw:]
        sig = jax.nn.sigmoid(gate)
        inner = (gate * sig * up).astype(bf16)
        back_in = mm_t(dy.reshape(n * rows, width), w_down)
        d_gate = (back_in * up * (sig * (1.0 + gate * (1.0 - sig)))).astype(bf16)
        d_gu = jnp.concatenate([d_gate, (back_in * (gate * sig)).astype(bf16)], axis=1)
        d_h = lax.psum_scatter(mm_t(d_gu, wgu).astype(bf16), "fsdp", scatter_dimension=0, tiled=True).astype(f32)
        down = t_mm(inner, dy.reshape(n * rows, width)).astype(bf16)
        return h, inner.reshape(n, rows, fw), d_gu.reshape(n, rows, 2 * fw), down, d_h
    sems = pltpu.SemaphoreType.DMA
    return pl.pallas_call(
        mlp_kernel,
        in_specs=[ANYWHERE] * 4,
        out_specs=[ANYWHERE] * 4 + [pl.BlockSpec(memory_space=pltpu.VMEM)],
        out_shape=[
            jax.ShapeDtypeStruct((n, rows, width), bf16),
            jax.ShapeDtypeStruct((n, rows, fw), bf16),
            jax.ShapeDtypeStruct((n, rows, 2 * fw), bf16),
            jax.ShapeDtypeStruct((fw, width), bf16),
            jax.ShapeDtypeStruct((rows, width), f32),
        ],
        scratch_shapes=[
            pltpu.VMEM(wgu.shape, bf16),
            pltpu.VMEM(w_down.shape, bf16),
            pltpu.VMEM((n, rows, width), bf16),
            pltpu.VMEM((n, rows, width), bf16),
            pltpu.VMEM((n, rows, fw), bf16),
            pltpu.VMEM((2, rows, 2 * fw), bf16),
            *scatter_boxes(rows, width),
            *[sems((k,)) for k in (2, 8, 8, 8, 2)],
            *GATHER_SEMS,
            *SCATTER_SEMS,
        ],
        compiler_params=params(collective_id, 60),
        cost_estimate=pl.CostEstimate(flops=10 * n * rows * width * fw, transcendentals=n * rows * fw, bytes_accessed=64 << 20),
        name="mlp",
    )(h_own, wgu, w_down, dy)


def product_tiles(lhs, rhs, box, out_ref, sems, over_rows, hooks):
    columns = rhs.shape[1]
    count = out_ref.shape[0] // 256

    def rows(i):
        return pl.ds(pl.multiple_of(i * 256, 256), 256)

    def store(i):
        return pltpu.make_async_copy(
            box.at[rest(i, 2), :, pl.ds(0, columns)], out_ref.at[rows(i)], sems.at[rest(i, 2)]
        )

    def body(i, _):
        for step, fns in hooks.items():

            @pl.when(i == step)
            def _():
                for fn in fns:
                    fn()

        @pl.when(i > 1)
        def _():
            store(i - 2).wait()

        left = lhs[:, rows(i)] if over_rows else lhs[rows(i)]
        for at in range(0, columns, 512):
            here = slice(at, min(at + 512, columns))
            box[rest(i, 2), :, here] = dots(left, rhs[:, here], 0 if over_rows else 1, 0).astype(bf16)
        store(i).start()
        return 0

    lax.fori_loop(0, count, body, 0)
    for i in range(max(0, count - 2), count):
        store(i).wait()


def gather_products_kernel(x_ref, h_ref, dgu_ref, inner_ref, wd_ref, out_ref, gu_ref, mlp_ref, h, dgu, inner, wd, box, load_sems, sems, *refs):
    loads = [
        pltpu.make_async_copy(src, dst, load_sems.at[i])
        for i, (src, dst) in enumerate(((h_ref, h), (dgu_ref, dgu), (inner_ref, inner), (wd_ref, wd)))
    ]
    me = lax.axis_index("fsdp")
    greet([other(me, d) for d in (1, 2, 4)])
    begin, near0, near1, near2, near3, far0, far1, wait_from, end = gather_parts(x_ref, out_ref, *refs)
    begin()
    for load in loads:
        load.start()
    loads[0].wait()
    loads[1].wait()
    product_tiles(h, dgu, box, gu_ref, sems, True, {1: [near0], 3: [near1], 5: [near2], 7: [near3]})
    loads[2].wait()
    loads[3].wait()
    product_tiles(inner, wd, box, mlp_ref, sems, False, {3: [far0], 7: [far1]})
    for d in (1, 3, 5, 7):
        wait_from(d)
    end()


def gather_products(x, h, dgu, inner, w_down, collective_id):
    n = lax.axis_size("fsdp")
    if n != 8:
        return lax.all_gather(x, "fsdp", axis=0), t_mm(h, dgu).astype(bf16), mm(inner, w_down).astype(bf16)
    total, width = h.shape
    sems = pltpu.SemaphoreType.DMA
    return pl.pallas_call(
        gather_products_kernel,
        in_specs=[ANYWHERE] * 5,
        out_specs=[ANYWHERE] * 3,
        out_shape=[
            jax.ShapeDtypeStruct((n, *x.shape), bf16),
            jax.ShapeDtypeStruct((width, dgu.shape[1]), bf16),
            jax.ShapeDtypeStruct((total, width), bf16),
        ],
        scratch_shapes=[pltpu.VMEM(a.shape, bf16) for a in (h, dgu, inner, w_down)]
        + [pltpu.VMEM((2, 256, max(width, dgu.shape[1])), bf16), sems((4,)), sems((2,)), *GATHER_SEMS],
        compiler_params=params(collective_id, 56),
        cost_estimate=pl.CostEstimate(
            flops=2 * total * width * (inner.shape[1] + dgu.shape[1]), transcendentals=0, bytes_accessed=48 << 20
        ),
        name="gather_products",
    )(x, h, dgu, inner, w_down)


def block_products(me, lhs, rhs, mine, turned, back, block):
    wide = mine.shape[2] // 4
    left = lhs[xor(me, block)]
    for t in range(4):
        cols = slice(t * wide, (t + 1) * wide)
        made = dots(left, rhs[cols], 1, 1) if turned else dots(left, rhs[:, cols], 1, 0)
        mine[block, :, cols] = made.astype(bf16)
    if block % 2 == 1:
        back["to_core"](block).start()


def product_scatter_kernel(lhs_ref, rhs_ref, out_ref, lhs, rhs, mine, side, near, last, load_sems, *sems):
    me = lax.axis_index("fsdp")
    loads = [pltpu.make_async_copy(lhs_ref, lhs, load_sems.at[0]), pltpu.make_async_copy(rhs_ref, rhs, load_sems.at[1])]
    for load in loads:
        load.start()
    greet([other(me, d) for d in (1, 2, 4)])
    back = scatter_parts(mine, side, near, last, out_ref, sems)
    for load in loads:
        load.wait()
    for block in (6, 7, 4, 5, 2, 3, 0, 1):
        block_products(me, lhs, rhs, mine, False, back, block)
        if block in (4, 2, 0):
            back["combine"](block + 2)()
    back["combine"](0)()
    for which in range(3):
        back["onward"](which)
    back["finish"]()


def product_scatter(lhs, rhs, collective_id):
    n, rows, depth = lhs.shape
    width = rhs.shape[1]
    if n != 8:
        made = mm(lhs.reshape(n * rows, depth), rhs).astype(bf16)
        return lax.psum_scatter(made, "fsdp", scatter_dimension=0, tiled=True).astype(f32)
    sems = pltpu.SemaphoreType.DMA
    return pl.pallas_call(
        product_scatter_kernel,
        in_specs=[ANYWHERE] * 2,
        out_specs=pl.BlockSpec(memory_space=pltpu.VMEM),
        out_shape=jax.ShapeDtypeStruct((rows, width), f32),
        scratch_shapes=[pltpu.VMEM(lhs.shape, bf16), pltpu.VMEM(rhs.shape, bf16), *scatter_boxes(rows, width), sems((2,)), *SCATTER_SEMS],
        compiler_params=params(collective_id, 40),
        cost_estimate=pl.CostEstimate(flops=2 * n * rows * depth * width, transcendentals=0, bytes_accessed=8 << 20),
        name="product_scatter",
    )(lhs, rhs)


SLOTS = 4


def chunks_of(gu_rows, out_rows, qkv_rows):
    out = [(0, d, r, 64) for d in ORDER for r in range(0, gu_rows, 64)]
    out += [(1, None, r, 64) for r in range(0, out_rows, 64)]
    return out + [(2, d, r, 128) for d in ORDER for r in range(0, qkv_rows, 128)]


def finish_kernel(*refs):
    small_ref, normed_ref, gu_ref, dqkv_ref, wqkv_ref, mixed_ref, dattn_ref, hin_ref, *refs = refs
    small_out, dhin_ref, part_out, part_qkv, *refs = refs
    ins = [gu_ref, part_out, part_qkv]
    kinds = 3
    outs, refs = refs[:kinds], refs[kinds:]
    first, refs = refs[:kinds], refs[kinds:]
    second, refs = refs[:kinds], refs[kinds:]
    come, refs = {0: refs[0], 2: refs[1]}, refs[2:]
    (dqkv, wqkv, mixed, dattn, hin, tiles), refs = refs[:6], refs[6:]
    (mine, side, near, last), refs = refs[:4], refs[4:]
    (task_loads, box_sems), refs = refs[:2], refs[2:]
    scatter_sems, refs = refs[: len(SCATTER_SEMS)], refs[len(SCATTER_SEMS) :]
    small_work, small_come, small_sum, small_in, small_back, *refs = refs
    small_move, small_line_sems, refs = refs[0:2], refs[2:4], refs[4:]
    g_buf, a_buf, t_buf, b_buf, u_buf, loads, stores, *sems = refs
    move = {0: sems[0:2], 2: sems[2:4]}
    sems = sems[4:]
    go_in, cross, back = sems[0:2], sems[2:4], sems[4:6]
    me, place = lax.axis_index("fsdp"), lax.axis_index("seq")
    is_end = (place == 0) | (place == 3)
    chunks = chunks_of(gu_ref.shape[1], part_out.shape[0], part_qkv.shape[1])
    inward = jnp.where(place < 2, 1, 2)
    outward = jnp.where(place < 2, 0, 3)
    opposite = 3 - inward
    barrier = pltpu.get_barrier_semaphore()
    for d in range(1, 8):
        pl.semaphore_signal(barrier, inc=1, device_id={"fsdp": other(me, d)}, device_id_type=pl.DeviceIdType.MESH)

    @pl.when(is_end)
    def _():
        pl.semaphore_signal(barrier, inc=1, device_id={"seq": inward}, device_id_type=pl.DeviceIdType.MESH)
        pl.semaphore_wait(barrier, 8)

    @pl.when(jnp.logical_not(is_end))
    def _():
        for peer in (outward, opposite):
            pl.semaphore_signal(barrier, inc=1, device_id={"seq": peer}, device_id_type=pl.DeviceIdType.MESH)
        pl.semaphore_wait(barrier, 9)

    def moving(t, d):
        return link(ins[t].at[other(me, d)], come[t].at[me], move[t], d, "fsdp", other(me, d))

    def arrival(t, d):
        owner = other(me, d)
        return link(come[t].at[owner], come[t].at[owner], move[t], d, "fsdp", owner)

    def small_moving(d):
        return link(small_work.at[other(me, d)], small_come.at[me], small_move, d, "fsdp", other(me, d))

    def small_arrival(d):
        there = small_come.at[other(me, d)]
        return link(there, there, small_move, d, "fsdp", other(me, d))

    def small_hop(src, dst, slot, peer):
        return link(src, dst, small_line_sems, slot, "seq", peer)

    plan = [(t, d) for t in (0, 2) for d in ORDER[1:]]
    begun = []

    def feed(count):
        while plan and count:
            t, d = plan.pop(0)
            moving(t, d).start()
            begun.append((t, d))
            count -= 1

    def view(refs, k):
        t, d, r, rows = chunks[k]
        if d is None:
            return refs[t].at[pl.ds(r, rows)]
        return refs[t].at[other(me, d), pl.ds(r, rows)]

    def windows(k):
        t, d, r, rows = chunks[k]
        buf = box(u_buf, k, SLOTS)
        if d is None:
            return [(buf, outs[t].at[pl.ds(r, rows)])]
        kinds = outs[t].shape[0]
        c = ins[t].shape[2] // kinds
        columns = pl.ds(pl.multiple_of(other(me, d) * c, 128), c)
        return [(buf.at[:, pl.ds(i * c, c)], outs[t].at[i, pl.ds(r, rows), columns]) for i in range(kinds)]

    def source(k):
        t, d, r, rows = chunks[k]
        if d is None:
            return ins[t].at[pl.ds(r, rows)]
        if d == 0:
            return ins[t].at[me, pl.ds(r, rows)]
        return come[t].at[other(me, d), pl.ds(r, rows)]

    def await_source(k):
        t, d, r, rows = chunks[k]
        if d and r == 0:
            arrival(t, d).wait_recv()

    def box(buf, k, depth):
        t, d, r, rows = chunks[k]
        return buf.at[k % depth, pl.ds(0, rows), pl.ds(0, ins[t].shape[-1])]

    def add(dst, left, right):
        rows = dst.shape[0]

        def body(i, _):
            here = pl.ds(pl.multiple_of(i * 16, 16), 16)
            dst[here] = (left[here].astype(f32) + right[here].astype(f32)).astype(bf16)
            return 0

        lax.fori_loop(0, rows // 16, body, 0)

    def end_send(k):
        return link(source(k), view(first, k), go_in, k, "seq", inward)

    def mid_cross(k):
        return link(box(t_buf, k, SLOTS), view(second, k), cross, k, "seq", opposite)

    def mid_back(k):
        return [link(src, dst, back, k, "seq", outward) for src, dst in windows(k)]

    def store(k):
        return [pltpu.make_async_copy(src, dst, stores.at[k % SLOTS]) for src, dst in windows(k)]

    def all_back(k):
        return link(box(u_buf, k, SLOTS), box(u_buf, k, SLOTS), back, k, "seq", outward)

    def all_stored(k):
        return pltpu.make_async_copy(box(u_buf, k, SLOTS), box(u_buf, k, SLOTS), stores.at[k % SLOTS])

    def finish(k):
        link(view(second, k), view(second, k), cross, k, "seq", opposite).wait_recv()
        load = pltpu.make_async_copy(view(second, k), box(b_buf, k, 2), loads.at[2])
        load.start()
        if k >= SLOTS:
            all_back(k - SLOTS).wait_send()
            all_stored(k - SLOTS).wait()
        load.wait()
        add(box(u_buf, k, SLOTS), box(t_buf, k, SLOTS), box(b_buf, k, 2))
        for copy in mid_back(k) + store(k):
            copy.start()

    count = len(chunks)
    way = scatter_parts(mine, side, near, last, dhin_ref, scatter_sems)
    pairs = ((dqkv_ref, dqkv), (wqkv_ref, wqkv), (mixed_ref, mixed), (dattn_ref, dattn), (hin_ref, hin))
    fetches = [pltpu.make_async_copy(src, dst, task_loads.at[i]) for i, (src, dst) in enumerate(pairs)]

    def products(block):
        return lambda: block_products(me, dqkv, wqkv, mine, True, way, block)

    def fetched(*which):
        def run():
            for i in which:
                fetches[i].wait()

        return run

    def put(j, columns):
        src = tiles.at[j % 2, :, pl.ds(0, columns)]
        return pltpu.make_async_copy(src, part_out if j == 0 else part_qkv.at[j - 1], box_sems.at[j % 2])

    def out_tile():
        for at in range(0, tiles.shape[2], 512):
            right = dattn[:, :, at : at + 512].reshape(-1, 512)
            tiles[0, :, at : at + 512] = dots(mixed[...].reshape(-1, mixed.shape[2]), right, 0, 0).astype(bf16)
        put(0, tiles.shape[2]).start()

    columns = dqkv.shape[2]

    def qkv_tile(j):
        def run():
            if j >= 2:
                put(j - 2, tiles.shape[2] if j == 2 else columns).wait()
            rows = part_qkv.shape[1]
            left = hin[:, :, (j - 1) * rows : j * rows].reshape(-1, rows)
            for at in range(0, columns, 256):
                right = dqkv[:, :, at : at + 256].reshape(-1, 256)
                tiles[j % 2, :, at : at + 256] = dots(left, right, 0, 0).astype(bf16)
            put(j, columns).start()

        return run

    def all_put():
        put(7, columns).wait()
        put(8, columns).wait()

    def small_start():
        small_work[...] = small_ref[...]
        c = small_work.shape[2]
        for j in range(8):
            here = slice(j * c, (j + 1) * c)
            small_work[j, 0:1] = jnp.sum(normed_ref[:, here] * dhin_ref[:, here], axis=0, keepdims=True)
        for d in range(1, 8):
            small_moving(d).start()
        small_come[me] = small_work[me]

    def small_first():
        for d in range(1, 8):
            small_arrival(d).wait_recv()
        small_sum[...] = jnp.sum(small_come[...], axis=0)

        @pl.when(is_end)
        def _():
            small_hop(small_sum, small_in, 0, inward).start()

        @pl.when(jnp.logical_not(is_end))
        def _():
            small_hop(small_in, small_in, 0, outward).wait_recv()
            small_sum[...] = small_sum[...] + small_in[...]
            small_hop(small_sum, small_back, 1, opposite).start()

    work = {
        0: [fetched(0, 1), products(6), products(7)],
        1: [products(4), way["combine"](6), products(5)],
        2: [products(2), way["combine"](4), products(3)],
        3: [products(0), way["combine"](2), products(1)],
        4: [way["combine"](0), fetched(2, 3), out_tile],
        5: [lambda: way["onward"](0), fetched(4), qkv_tile(1)],
        6: [lambda: way["onward"](1), qkv_tile(2)],
        7: [lambda: way["onward"](2), qkv_tile(3)],
        8: [qkv_tile(4), qkv_tile(5)],
        9: [qkv_tile(6), qkv_tile(7)],
        10: [qkv_tile(8), all_put],
        12: [way["finish"]],
        13: [small_start],
        18: [small_first],
    }
    for fetch in fetches:
        fetch.start()
    feed(3)
    for k in range(count):
        if k % 4 == 3 and k < 16:
            feed(1)
        if k >= 18 and k % 2 == 0:
            feed(1)
        await_source(k)

        @pl.when(is_end)
        def _():
            end_send(k).start()

        @pl.when(jnp.logical_not(is_end))
        def _():
            own = pltpu.make_async_copy(source(k), box(g_buf, k, 2), loads.at[0])
            own.start()
            link(view(first, k), view(first, k), go_in, k, "seq", outward).wait_recv()
            got = pltpu.make_async_copy(view(first, k), box(a_buf, k, 2), loads.at[1])
            got.start()
            if k >= SLOTS:
                mid_cross(k - SLOTS).wait_send()
            own.wait()
            got.wait()
            add(box(t_buf, k, SLOTS), box(g_buf, k, 2), box(a_buf, k, 2))
            mid_cross(k).start()
            if k >= 1:
                finish(k - 1)

        for fn in work.get(k, ()):
            fn()

    @pl.when(jnp.logical_not(is_end))
    def _():
        small_hop(small_back, small_back, 1, opposite).wait_recv()
        small_hop(small_sum, small_back, 1, opposite).wait_send()
        small_out[...] = small_sum[...] + small_back[...]
        small_hop(small_out, small_out, 2, outward).start()

    @pl.when(is_end)
    def _():
        small_hop(small_out, small_out, 2, inward).wait_recv()
        small_hop(small_sum, small_in, 0, inward).wait_send()
        for k in range(count):
            all_back(k).wait_recv()
            end_send(k).wait_send()

    @pl.when(jnp.logical_not(is_end))
    def _():
        finish(count - 1)
        small_hop(small_out, small_out, 2, outward).wait_send()
        for k in range(max(0, count - SLOTS), count):
            mid_cross(k).wait_send()
            all_back(k).wait_send()
            all_stored(k).wait()

    for t, d in begun:
        moving(t, d).wait_send()
    for d in range(1, 8):
        small_moving(d).wait_send()


def finish(small, normed, gu, dqkv, wqkv, mixed, dattn, hin, collective_id):
    n, per, _ = gu.shape
    rows, width = normed.shape
    cw = mixed.shape[2]
    if lax.axis_size("seq") != 4 or n != 8:
        total = n * rows
        dhin = mm_t(dqkv.reshape(total, 3 * cw), wqkv).astype(bf16)
        dhin = lax.psum_scatter(dhin, "fsdp", scatter_dimension=0, tiled=True).astype(f32)
        small = small.at[:, 0].set(jnp.sum(normed * dhin, axis=0).reshape(n, per))
        out = lax.psum(t_mm(mixed.reshape(total, cw), dattn.reshape(total, width)).astype(bf16), "seq")
        qkv = t_mm(hin.reshape(total, width), dqkv.reshape(total, 3 * cw)).astype(bf16).reshape(n, per, 3 * cw)
        moved = []
        for x, count in ((gu, 2), (qkv, 3)):
            c = x.shape[2] // count
            x = lax.psum(lax.all_to_all(x, "fsdp", split_axis=0, concat_axis=0, tiled=True), "seq")
            moved.append(x.reshape(n, per, count, c).transpose(2, 1, 0, 3).reshape(count, per, n * c))
        small = lax.psum(lax.psum_scatter(small, "fsdp", scatter_dimension=0), "seq")
        return small, dhin, out, *moved
    qkv = jax.ShapeDtypeStruct((n, per, 3 * cw), bf16)
    out = jax.ShapeDtypeStruct((cw, width), bf16)
    gu_shape = jax.ShapeDtypeStruct(gu.shape, bf16)
    count = len(chunks_of(per, cw, per))
    inside = pl.BlockSpec(memory_space=pltpu.VMEM)
    sems = pltpu.SemaphoreType.DMA
    small_sum, dhin, _, _, sum_gu, sum_out, sum_qkv, *_ = pl.pallas_call(
        finish_kernel,
        in_specs=[inside] * 2 + [ANYWHERE] * 6,
        out_specs=[inside] * 2 + [ANYWHERE] * 13,
        out_shape=[
            jax.ShapeDtypeStruct(small.shape[1:], f32),
            jax.ShapeDtypeStruct((rows, width), f32),
            out,
            qkv,
            jax.ShapeDtypeStruct((2, per, gu.shape[2] // 2 * n), bf16),
            out,
            jax.ShapeDtypeStruct((3, per, cw * n), bf16),
            *[gu_shape, out, qkv] * 2,
            gu_shape,
            qkv,
        ],
        scratch_shapes=[pltpu.VMEM(x.shape, bf16) for x in (dqkv, wqkv, mixed, dattn, hin)]
        + [pltpu.VMEM((2, per, width), bf16)]
        + scatter_boxes(rows, width)
        + [sems((5,)), sems((2,)), *SCATTER_SEMS]
        + [pltpu.VMEM(small.shape, f32)] * 2
        + [pltpu.VMEM(small.shape[1:], f32)] * 3
        + [sems((8,)), sems((8,)), sems((3,)), sems((3,))]
        + [pltpu.VMEM((depth, 128, gu.shape[2]), bf16) for depth in (2, 2, SLOTS, 2, SLOTS)]
        + [sems((3,)), sems((SLOTS,))]
        + [sems((8,))] * 4
        + [sems((count,))] * 6,
        compiler_params=params(collective_id, 60),
        name="finish",
    )(small, normed, gu, dqkv, wqkv, mixed, dattn, hin)
    return small_sum, dhin, sum_out, sum_gu, sum_qkv


def shards(
    tokens,
    doc_starts,
    norm_in,
    w_query,
    w_key,
    w_value,
    mix_bias,
    w_out,
    norm_mid,
    w_gate,
    w_up,
    w_down,
    cotangent,
):
    rows = tokens.shape[2]
    width = tokens.shape[3]
    n = lax.axis_size("fsdp")
    s = lax.axis_size("seq")
    own = NSEG * rows
    total = n * own
    seg_len = rows * n
    heads = HEADS // n
    cw = heads * HEAD_DIM
    fw = w_gate.shape[1] // n

    wgu = to_columns_in_turns([w_gate, w_up], 7)
    flat_in = tokens.reshape(own, width)
    all_in, gains, wqkv = front(flat_in, jnp.stack([norm_in, norm_mid]), [w_query, w_key, w_value], 0)
    gain_in, gain_mid = gains[0][None], gains[1][None]

    def normed(rows_in):
        rows_in = rows_in.astype(f32)
        inverse = lax.rsqrt(jnp.mean(rows_in * rows_in, axis=1, keepdims=True) + norm_eps)
        return rows_in * inverse, inverse

    flat_in = flat_in.astype(f32)
    normed_in, inv_in = normed(flat_in)
    start_row = doc_starts[0]
    docs = doc_number(start_row, jnp.arange(NSEG * seg_len, dtype=jnp.int32)).reshape(NSEG, seg_len)
    side = (docs == docs[1, 0]).astype(f32)[:, :, None]
    doc_col, doc_row = docs[:, :, None], docs[:, None, :]
    blend = jax.nn.sigmoid(mix_bias)
    blend_row = jnp.repeat(blend, HEAD_DIM)[None]
    h_in, qkv, dy, mixed, diff, lse, memory, norm_vec = attend(
        all_in, gain_in, wqkv, cotangent.reshape(own, width), doc_col, doc_row, side, blend_row, heads, 4
    )
    h_in, dy = h_in.reshape(total, width), dy.reshape(total, width)
    mixed = mixed.reshape(total, cw)

    attn_sum = product_scatter(mixed.reshape(n, own, cw), w_out, 3)
    residual = flat_in + attn_sum
    inv_mid = lax.rsqrt(jnp.mean(residual * residual, axis=1, keepdims=True) + norm_eps)
    normed_mid = residual * inv_mid
    h_mid = (normed_mid * gain_mid).astype(bf16)
    h_mid, inner, d_gu, part_down, d_hmid = mlp(h_mid, wgu, w_down, dy.reshape(n, own, width), 1)
    h_mid, inner, d_gu = (x.reshape(total, x.shape[2]) for x in (h_mid, inner, d_gu))

    gain_mid_term = jnp.sum(normed_mid * d_hmid, axis=0)
    d_resid = cotangent.reshape(own, width).astype(f32) + norm_back(d_hmid * gain_mid, normed_mid, inv_mid)
    d_attn, part_gu, part_mlp = gather_products(d_resid.astype(bf16), h_mid, d_gu, inner, w_down, 2)
    part_gu = part_gu.reshape(n, width // n, 2 * fw)
    grad_down = lax.psum(part_down, "seq").astype(f32)

    d_mixed = mm_t(d_attn.reshape(total, width), w_out).reshape(n, NSEG, rows, cw)
    d_qkv, bias_rows = attention_back(
        qkv, d_mixed, diff, lse, doc_col, doc_row, side, blend_row, memory, norm_vec, heads
    )
    bias_term = jnp.sum(bias_rows.reshape(heads, HEAD_DIM), axis=1) * blend * (1.0 - blend)

    mlp_sum = lax.psum_scatter(part_mlp, "fsdp", scatter_dimension=0, tiled=True)
    block_out = (residual + mlp_sum.astype(f32)).astype(bf16).reshape(tokens.shape)
    per = width // n
    mine = (jnp.arange(n) == lax.axis_index("fsdp"))[:, None, None]
    bias = jnp.where(mine, jnp.pad(bias_term, (0, per - heads))[None, None], 0.0)
    terms = jnp.concatenate(
        [jnp.zeros((n, 1, per), f32), gain_mid_term.reshape(n, 1, per), bias, jnp.zeros((n, 5, per), f32)], axis=1
    )
    small, d_hin, sum_out, sum_gu, sum_qkv = finish(
        terms,
        normed_in,
        part_gu,
        d_qkv.reshape(n, own, 3 * cw),
        wqkv,
        mixed.reshape(n, own, cw),
        d_attn,
        h_in.reshape(n, own, width),
        6,
    )
    grad_out = sum_out.astype(f32)
    grad_gate, grad_up = sum_gu[0].astype(f32), sum_gu[1].astype(f32)
    grad_q, grad_k, grad_v = (sum_qkv[i].astype(f32) for i in range(3))
    grad_tokens = (d_resid + norm_back(d_hin * gain_in, normed_in, inv_in)).reshape(tokens.shape)

    return (
        block_out,
        grad_tokens,
        small[0],
        grad_q,
        grad_k,
        grad_v,
        small[2, :heads],
        grad_out,
        small[1],
        grad_gate,
        grad_up,
        grad_down,
    )


def solution(mesh):
    whole = P("seq", None, "fsdp", None)
    matrix, vector = P("fsdp", None), P("fsdp")
    return jax.shard_map(
        shards,
        mesh=mesh,
        in_specs=(whole, P("seq", None), vector, matrix, matrix, matrix, vector, matrix, vector, matrix, matrix, matrix, whole),
        out_specs=(whole, whole, vector, matrix, matrix, matrix, vector, matrix, vector, matrix, matrix, matrix),
        check_vma=False,
    )
```

```python
import functools

import jax
import jax.numpy as jnp
from jax import lax
from jax.experimental import pallas as pl
from jax.experimental.pallas import tpu as pltpu
from jax.sharding import PartitionSpec as P

HEADS = 16
HEAD_DIM = 128
NSEG = 2

highest = lax.Precision.HIGHEST
norm_eps = 1e-05
f32 = jnp.float32
bf16 = jnp.bfloat16


def doc_number(start_row, places):
    return jnp.sum((start_row[None, :] <= places[:, None]).astype(jnp.int32), axis=1) - 1


def norm_back(grad_in, normed, inverse):
    return inverse * (grad_in - normed * jnp.mean(grad_in * normed, axis=-1, keepdims=True))


def mm(a, b):
    return lax.dot_general(a, b, (((1,), (0,)), ((), ())), preferred_element_type=f32)


def mm_t(a, b):
    return lax.dot_general(a, b, (((1,), (1,)), ((), ())), preferred_element_type=f32)


def t_mm(a, b):
    return lax.dot_general(a, b, (((0,), (0,)), ((), ())), preferred_element_type=f32)


def dots(a, b, ca, cb, precision=None):
    return lax.dot_general(a, b, (((ca,), (cb,)), ((), ())), preferred_element_type=f32, precision=precision)


def phi(u):
    return jnp.where(u > 0, u + 1.0, jnp.exp(jnp.minimum(u, 0.0)))


def phi_slope(u):
    return jnp.where(u > 0, 1.0, jnp.exp(jnp.minimum(u, 0.0)))


def when(condition):
    if isinstance(condition, bool):
        return (lambda run: run()) if condition else (lambda run: None)
    return pl.when(condition)


def docs_at(starts_ref, places):
    total = -1
    for k in range(starts_ref.shape[0]):
        total = total + (starts_ref[k] <= places).astype(jnp.int32)
    return total


def cross_doc(starts_ref, length):
    total = -1
    for k in range(starts_ref.shape[0]):
        total = total + jnp.where(starts_ref[k] <= length, 1, 0)
    return total


def in_cross(starts_ref, length, segment, first, count):
    places = lax.broadcasted_iota(jnp.int32, (count, 1), 0) + (segment * length + first)
    return (docs_at(starts_ref, places) == cross_doc(starts_ref, length)).astype(f32)


def may_see(starts_ref, length, segment, first, block, span):
    rows = lax.broadcasted_iota(jnp.int32, (block, 1), 0) + first
    cols = lax.broadcasted_iota(jnp.int32, (1, span), 1)
    own = docs_at(starts_ref, rows + segment * length)
    return (cols <= rows) & (docs_at(starts_ref, cols + segment * length) == own)


def head_columns(kind, h, heads):
    at = kind * heads * HEAD_DIM + h * HEAD_DIM
    return slice(at, at + HEAD_DIM) if isinstance(at, int) else pl.ds(pl.multiple_of(at, HEAD_DIM), HEAD_DIM)


def attention_head(h, heads, segment, starts_ref, blend_ref, qkv_ref, mixed_ref, diff_ref, lse_ref, mem_ref, nv_ref):
    n, _, rows, _ = qkv_ref.shape
    length = n * rows
    take = max(1, 256 // rows)
    block = take * rows
    scale = HEAD_DIM ** (-0.5)
    cols = head_columns(0, h, heads)

    def part(kind, lo, hi):
        return qkv_ref[lo:hi, 0, :, head_columns(kind, h, heads)].reshape((hi - lo) * rows, HEAD_DIM)

    @when(segment == 0)
    def _():
        fk = phi(part(1, 0, n).astype(f32)) * in_cross(starts_ref, length, 0, 0, length)
        mem_ref[h] = dots(fk, part(2, 0, n).astype(f32), 0, 0, highest)
        nv_ref[h] = jnp.sum(fk, axis=0, keepdims=True)

    blend = blend_ref[:, cols]
    for i in range(n // take):
        lo, hi = i * take, (i + 1) * take
        span = (i + 1) * block
        q = part(0, lo, hi)
        s = dots(q, part(1, 0, hi), 1, 1) * scale
        s = jnp.where(may_see(starts_ref, length, segment, i * block, block, span), s, -1000000000.0)
        top = jnp.max(s, axis=1, keepdims=True)
        p = jnp.exp(s - top)
        tot = jnp.sum(p, axis=1, keepdims=True)
        lse_ref[h, 0, i * block : (i + 1) * block] = top + jnp.log(tot)
        direct = dots((p / tot).astype(bf16), part(2, 0, hi), 1, 0)
        shape = (take, rows, HEAD_DIM)

        @when(segment == 0)
        def _():
            mixed_ref[lo:hi, 0, :, cols] = ((1.0 - blend) * direct).astype(bf16).reshape(shape)
            diff_ref[lo:hi, 0, :, cols] = (-direct).reshape(shape)

        @when(segment != 0)
        def _():
            fq = phi(q.astype(f32))
            numer = dots(fq, mem_ref[h], 1, 0, highest)
            den = jnp.sum(fq * nv_ref[h], axis=1, keepdims=True) + 1.0
            ret = in_cross(starts_ref, length, 1, i * block, block) * numer / den
            mixed_ref[lo:hi, 0, :, cols] = (blend * ret + (1.0 - blend) * direct).astype(bf16).reshape(shape)
            diff_ref[lo:hi, 0, :, cols] = (ret - direct).reshape(shape)


def attention_kernel(heads, starts_ref, blend_ref, *refs):
    for h in range(heads):
        attention_head(h, heads, pl.program_id(0), starts_ref, blend_ref, *refs)


def back_block(i, h, heads, segment, starts_ref, blend_ref, qkv_ref, dmix_ref, diff_ref, lse_ref, mem_ref, nv_ref, out_ref, bias_ref, dk_acc, dv_acc, dmem, dnv):
    n, _, rows, _ = qkv_ref.shape
    length = n * rows
    take = max(1, 256 // rows)
    block = take * rows
    scale = HEAD_DIM ** (-0.5)
    shape = (take, rows, HEAD_DIM)
    cols = head_columns(0, h, heads)
    blend = blend_ref[:, cols]
    lo, hi = i * take, (i + 1) * take
    span = (i + 1) * block
    here = slice(i * block, (i + 1) * block)

    def part(kind, lo, hi):
        return qkv_ref[lo:hi, 0, :, head_columns(kind, h, heads)].reshape((hi - lo) * rows, HEAD_DIM)

    if i == 0:
        dk_acc[h] = jnp.zeros(dk_acc.shape[1:], f32)
        dv_acc[h] = jnp.zeros(dv_acc.shape[1:], f32)
    q, k, v = part(0, lo, hi), part(1, 0, hi), part(2, 0, hi)
    dmix = dmix_ref[lo:hi, 0, :, cols].reshape(block, HEAD_DIM)
    bias_ref[:, cols] += jnp.sum(dmix * diff_ref[lo:hi, 0, :, cols].reshape(block, HEAD_DIM), axis=0, keepdims=True)
    ddir = ((1.0 - blend) * dmix).astype(bf16)
    s = dots(q, k, 1, 1) * scale
    allowed = may_see(starts_ref, length, segment, i * block, block, span)
    e = jnp.exp(jnp.where(allowed, s, -1000000000.0) - lse_ref[h, 0, here])
    dp = dots(ddir, v, 1, 1)
    bal = jnp.sum(e * dp, axis=1, keepdims=True)
    ds = (e * (dp - bal)).astype(bf16)
    dv_acc[h, :span] += dots(e.astype(bf16), ddir, 0, 0)
    dk_acc[h, :span] += dots(ds, q, 0, 0) * scale
    dq = dots(ds, k, 1, 0) * scale

    @when(segment == 0)
    def _():
        out_ref[lo:hi, 0, :, cols] = dq.astype(bf16).reshape(shape)

    @when(segment != 0)
    def _():
        q32 = q.astype(f32)
        fq = phi(q32)
        numer = dots(fq, mem_ref[h], 1, 0, highest)
        den = jnp.sum(fq * nv_ref[h], axis=1, keepdims=True) + 1.0
        dnum = in_cross(starts_ref, length, 1, i * block, block) * (blend * dmix) / den
        dden = -jnp.sum(dnum * numer, axis=1, keepdims=True) / den
        dmem[h] += dots(fq, dnum, 0, 0, highest)
        dnv[h] += jnp.sum(dden * fq, axis=0, keepdims=True)
        dfq = dots(dnum, mem_ref[h], 1, 1, highest) + dden * nv_ref[h]
        out_ref[lo:hi, 0, :, cols] = (dq + dfq * phi_slope(q32)).astype(bf16).reshape(shape)


def back_end(h, heads, segment, starts_ref, qkv_ref, out_ref, dk_acc, dv_acc, dmem, dnv):
    n, _, rows, _ = qkv_ref.shape
    length = n * rows
    whole = (n, rows, HEAD_DIM)
    kcols, vcols = head_columns(1, h, heads), head_columns(2, h, heads)

    @when(segment != 0)
    def _():
        out_ref[:, 0, :, kcols] = dk_acc[h].astype(bf16).reshape(whole)
        out_ref[:, 0, :, vcols] = dv_acc[h].astype(bf16).reshape(whole)

    @when(segment == 0)
    def _():
        k32 = qkv_ref[:, 0, :, kcols].reshape(length, HEAD_DIM).astype(f32)
        v32 = qkv_ref[:, 0, :, vcols].reshape(length, HEAD_DIM).astype(f32)
        key_set = in_cross(starts_ref, length, 0, 0, length)
        mem_v = key_set * dots(phi(k32), dmem[h], 1, 0, highest)
        mem_k = key_set * (dots(v32, dmem[h], 1, 1, highest) + dnv[h]) * phi_slope(k32)
        out_ref[:, 0, :, kcols] = (dk_acc[h] + mem_k).astype(bf16).reshape(whole)
        out_ref[:, 0, :, vcols] = (dv_acc[h] + mem_v).astype(bf16).reshape(whole)


def attention_back_kernel(heads, starts_ref, blend_ref, qkv_ref, dmix_ref, diff_ref, lse_ref, mem_ref, nv_ref, out_ref, bias_ref, dk_acc, dv_acc, dmem, dnv):
    n, _, rows, _ = qkv_ref.shape

    @pl.when(pl.program_id(0) == 0)
    def _():
        bias_ref[...] = jnp.zeros_like(bias_ref)
        dmem[...] = jnp.zeros_like(dmem)
        dnv[...] = jnp.zeros_like(dnv)

    segment = NSEG - 1 - pl.program_id(0)
    for h in range(heads):
        for i in range(n * rows // (max(1, 256 // rows) * rows)):
            back_block(
                i, h, heads, segment, starts_ref, blend_ref, qkv_ref, dmix_ref, diff_ref, lse_ref, mem_ref, nv_ref,
                out_ref, bias_ref, dk_acc, dv_acc, dmem, dnv,
            )
        back_end(h, heads, segment, starts_ref, qkv_ref, out_ref, dk_acc, dv_acc, dmem, dnv)


def attention_specs(n, rows, heads, pick):
    length = n * rows
    cw = heads * HEAD_DIM
    starts = pl.BlockSpec(memory_space=pltpu.SMEM)
    wide = pl.BlockSpec((n, 1, rows, 3 * cw), lambda g: (0, pick(g), 0, 0))
    narrow = pl.BlockSpec((n, 1, rows, cw), lambda g: (0, pick(g), 0, 0))
    lse = pl.BlockSpec((heads, 1, length, 1), lambda g: (0, pick(g), 0, 0))
    line = pl.BlockSpec((1, cw), lambda g: (0, 0))
    mem = pl.BlockSpec((heads, HEAD_DIM, HEAD_DIM), lambda g: (0, 0, 0))
    nv = pl.BlockSpec((heads, 1, HEAD_DIM), lambda g: (0, 0, 0))
    return starts, wide, narrow, lse, line, mem, nv


def attention(starts_row, blend_row, qkv, heads):
    n, _, rows, _ = qkv.shape
    length = n * rows
    cw = heads * HEAD_DIM
    starts, wide, narrow, lse, line, mem, nv = attention_specs(n, rows, heads, lambda g: g)
    pairs = heads * NSEG * length * length // 2
    return pl.pallas_call(
        functools.partial(attention_kernel, heads),
        grid=(NSEG,),
        in_specs=[starts, line, wide],
        out_specs=[narrow, narrow, lse, mem, nv],
        out_shape=attention_shapes(n, rows, heads),
        compiler_params=pltpu.CompilerParams(vmem_limit_bytes=48 << 20),
        cost_estimate=pl.CostEstimate(flops=pairs * 4 * HEAD_DIM, transcendentals=pairs, bytes_accessed=8 << 20),
        name="attention",
    )(starts_row, blend_row, qkv)


def attention_shapes(n, rows, heads):
    return [
        jax.ShapeDtypeStruct((n, NSEG, rows, heads * HEAD_DIM), bf16),
        jax.ShapeDtypeStruct((n, NSEG, rows, heads * HEAD_DIM), f32),
        jax.ShapeDtypeStruct((heads, NSEG, n * rows, 1), f32),
        jax.ShapeDtypeStruct((heads, HEAD_DIM, HEAD_DIM), f32),
        jax.ShapeDtypeStruct((heads, 1, HEAD_DIM), f32),
    ]


def back_boxes(n, rows, heads):
    return [
        pltpu.VMEM((heads, n * rows, HEAD_DIM), f32),
        pltpu.VMEM((heads, n * rows, HEAD_DIM), f32),
        pltpu.VMEM((heads, HEAD_DIM, HEAD_DIM), f32),
        pltpu.VMEM((heads, 1, HEAD_DIM), f32),
    ]


def attention_back(starts_row, blend_row, qkv, dmix, diff, lse_rows, mem_all, nv_all, heads):
    n, _, rows, _ = qkv.shape
    length = n * rows
    cw = heads * HEAD_DIM
    starts, wide, narrow, lse, line, mem, nv = attention_specs(n, rows, heads, lambda g: NSEG - 1 - g)
    pairs = heads * NSEG * length * length // 2
    return pl.pallas_call(
        functools.partial(attention_back_kernel, heads),
        grid=(NSEG,),
        in_specs=[starts, line, wide, narrow, narrow, lse, mem, nv],
        out_specs=[wide, line],
        out_shape=[
            jax.ShapeDtypeStruct((n, NSEG, rows, 3 * cw), bf16),
            jax.ShapeDtypeStruct((1, cw), f32),
        ],
        scratch_shapes=back_boxes(n, rows, heads),
        compiler_params=pltpu.CompilerParams(vmem_limit_bytes=56 << 20),
        cost_estimate=pl.CostEstimate(flops=pairs * 10 * HEAD_DIM, transcendentals=pairs, bytes_accessed=16 << 20),
        name="attention_back",
    )(starts_row, blend_row, qkv, dmix, diff, lse_rows, mem_all, nv_all)


def flip(index, bit):
    return index + bit - 2 * bit * lax.rem(lax.div(index, bit), 2)


def other(index, bits):
    for bit in (1, 2, 4):
        if bits & bit:
            index = flip(index, bit)
    return index


def link(src, dst, sems, slot, axis, peer):
    return pltpu.make_async_remote_copy(
        src_ref=src, dst_ref=dst, send_sem=sems[0].at[slot], recv_sem=sems[1].at[slot],
        device_id={axis: peer}, device_id_type=pl.DeviceIdType.MESH,
    )


def send(src, dst, sems, slot, peer):
    return link(src, dst, sems, slot, "fsdp", peer)


def greet(peers):
    barrier = pltpu.get_barrier_semaphore()
    for peer in peers:
        pl.semaphore_signal(barrier, inc=1, device_id={"fsdp": peer}, device_id_type=pl.DeviceIdType.MESH)
    pl.semaphore_wait(barrier, len(peers))


PIECES = 4
ORDER = (0, 1, 2, 4, 3, 5, 6, 7)
GATHER_SEMS = [pltpu.SemaphoreType.DMA] + [pltpu.SemaphoreType.DMA((PIECES,))] * 14


def gather_parts(x_ref, out_ref, local_sem, *sems, own_first=False):
    me = lax.axis_index("fsdp")
    sib, xn, yn, far_owner = flip(me, 1), flip(me, 2), flip(me, 4), other(me, 6)
    rows = x_ref.shape[0] // PIECES
    half = PIECES // 2
    own, over_x, over_y, far = sems[0:2], sems[2:4], sems[4:6], sems[6:8]
    side_x, side_y, side_far = sems[8:10], sems[10:12], sems[12:14]
    started = []

    def at(owner, c):
        return out_ref.at[owner, pl.ds(c * rows, rows)]

    def mine(c):
        return x_ref.at[pl.ds(c * rows, rows)]

    def go(make):
        make().start()
        started.append(make)

    def pass_on(owner, c, sems, peer):
        go(lambda: send(at(owner, c), at(owner, c), sems, c, peer))

    def arrived(owner, c, sems):
        send(at(owner, c), at(owner, c), sems, c, sib).wait_recv()

    local = pltpu.make_async_copy(x_ref, out_ref.at[me], local_sem)

    def begin_one(c, sems, peer):
        return send(mine(c), at(me, c), sems, c, peer)

    def begin():
        local.start()
        for j in range(PIECES):
            c, d = j, (j + half) % PIECES
            go(functools.partial(begin_one, c, over_x, xn))
            go(functools.partial(begin_one, d, over_y, yn))
        for c in range(PIECES):
            go(functools.partial(begin_one, c, own, sib))
        if own_first:
            local.wait()

    def near(j):
        c, d = j, (j + half) % PIECES
        arrived(xn, c, over_x)
        if c < half:
            pass_on(xn, c, far, yn)
        pass_on(xn, c, side_x, sib)
        arrived(yn, d, over_y)
        if d >= half:
            pass_on(yn, d, far, xn)
        pass_on(yn, d, side_y, sib)

    def beyond(j):
        for c in (j, j + half):
            arrived(far_owner, c, far)
            pass_on(far_owner, c, side_far, sib)

    def wait_from(d):
        for c in range(PIECES):
            arrived(other(me, d), c, {1: own, 3: side_x, 5: side_y, 7: side_far}[d])

    def end():
        for make in started:
            make().wait_send()
        if not own_first:
            local.wait()

    near_steps = [functools.partial(near, j) for j in range(PIECES)]
    far_steps = [functools.partial(beyond, j) for j in range(half)]
    return [begin, *near_steps, *far_steps, wait_from, end]


def gather_steps(x_ref, out_ref, *sems):
    *steps, wait_from, end = gather_parts(x_ref, out_ref, *sems)

    def finish():
        for d in (1, 3, 5, 7):
            wait_from(d)
        end()

    return [*steps, finish]


def params(collective_id, mib=32):
    return pltpu.CompilerParams(collective_id=collective_id, has_side_effects=True, vmem_limit_bytes=mib << 20)


ANYWHERE = pl.BlockSpec(memory_space=pltpu.HBM)


def move_steps(ins, out_ref, first, rows, sems, local_sem):
    me = lax.axis_index("fsdp")
    count = len(ins)
    c = out_ref.shape[1] // count

    def piece(kind, d):
        peer = other(me, d)
        src = ins[kind].at[pl.ds(first, rows), pl.ds(pl.multiple_of(peer * c, 128), c)]
        dst = out_ref.at[pl.ds(pl.multiple_of(me * rows, 16), rows), pl.ds(kind * c, c)]
        return src, dst, peer

    def moving(kind, d):
        src, dst, peer = piece(kind, d)
        return send(src, dst, sems, d * count + kind, peer)

    def local(kind):
        src, dst, _ = piece(kind, 0)
        return pltpu.make_async_copy(src, dst, local_sem.at[kind])

    def begin():
        for d in (6, 7, 2, 4, 3, 5, 1):
            for kind in range(count):
                moving(kind, d).start()
        for kind in range(count):
            local(kind).start()

    def end():
        for d in ORDER[1:]:
            for kind in range(count):
                there = out_ref.at[pl.ds(pl.multiple_of(other(me, d) * rows, 16), rows), pl.ds(kind * c, c)]
                send(there, there, sems, d * count + kind, other(me, d)).wait_recv()
                moving(kind, d).wait_send()
        for kind in range(count):
            local(kind).wait()

    return [begin, end]


def move_kernel(count, rows, *refs):
    ins, (out_ref, local_sem, *sems) = refs[:count], refs[count:]
    me = lax.axis_index("fsdp")
    greet([other(me, d) for d in range(1, 8)])
    for step in move_steps(ins, out_ref, lax.axis_index("seq") * rows, rows, sems, local_sem):
        step()


def to_columns(weights, first, rows):
    n = lax.axis_size("fsdp")
    cols = weights[0].shape[1]
    weights = [lax.dynamic_slice_in_dim(w, first, rows, 0) for w in weights]
    parts = jnp.stack([w.reshape(rows, n, cols // n) for w in weights], axis=2)
    parts = parts.reshape(rows, n, len(weights) * (cols // n))
    out = lax.all_to_all(parts, "fsdp", split_axis=1, concat_axis=0, tiled=True)
    return out.reshape(n * rows, len(weights) * (cols // n))


def to_columns_in_turns(weights, collective_id):
    n, s = lax.axis_size("fsdp"), lax.axis_size("seq")
    count = len(weights)
    share = weights[0].shape[0] // s
    width = count * (weights[0].shape[1] // n)
    if n != 8:
        part = to_columns(weights, lax.axis_index("seq") * share, share)
    else:
        part = pl.pallas_call(
            functools.partial(move_kernel, count, share),
            in_specs=[ANYWHERE] * count,
            out_specs=ANYWHERE,
            out_shape=jax.ShapeDtypeStruct((n * share, width), bf16),
            scratch_shapes=[pltpu.SemaphoreType.DMA((count,))] + [pltpu.SemaphoreType.DMA((n * count,))] * 2,
            compiler_params=params(collective_id),
            name="move",
        )(*weights)
    part = part.reshape(n, share, width)
    return lax.all_gather(part, "seq", axis=1, tiled=True).reshape(n * share * s, width)


def front_kernel(count, *refs):
    x_ref, gain_ref, *refs = refs
    ins, refs = refs[:count], refs[count:]
    out_ref, gains_ref, w_ref, *sems = refs
    gain_sems, sems = sems[:3], sems[3:]
    move_sems, sems = sems[:3], sems[3:]
    me = lax.axis_index("fsdp")
    greet([other(me, d) for d in range(1, 8)])

    def gain(d):
        return send(gain_ref, gains_ref.at[me], gain_sems[1:], d, other(me, d))

    own = pltpu.make_async_copy(gain_ref, gains_ref.at[me], gain_sems[0])
    own.start()
    for d in range(1, 8):
        gain(d).start()
    first, *steps = gather_steps(x_ref, out_ref, *sems)
    begin, end = move_steps(ins, w_ref, 0, ins[0].shape[0], move_sems[1:], move_sems[0])
    first()
    begin()
    for step in steps:
        step()
    end()
    own.wait()
    for d in range(1, 8):
        there = gains_ref.at[other(me, d)]
        send(there, there, gain_sems[1:], d, other(me, d)).wait_recv()
        gain(d).wait_send()


def front(x, gains, weights, collective_id):
    n = lax.axis_size("fsdp")
    if n != 8:
        return (
            lax.all_gather(x, "fsdp", axis=0),
            lax.all_gather(gains, "fsdp", axis=1, tiled=True),
            to_columns(weights, 0, weights[0].shape[0]),
        )
    count = len(weights)
    kinds, c = gains.shape
    gains = jnp.concatenate([gains, jnp.zeros((8 - kinds, c), f32)])
    rows, cols = weights[0].shape
    sems = pltpu.SemaphoreType.DMA
    x, gains, w = pl.pallas_call(
        functools.partial(front_kernel, count),
        in_specs=[ANYWHERE] * (2 + count),
        out_specs=[ANYWHERE] * 3,
        out_shape=[
            jax.ShapeDtypeStruct((n, *x.shape), x.dtype),
            jax.ShapeDtypeStruct((n, 8, c), f32),
            jax.ShapeDtypeStruct((n * rows, count * (cols // n)), bf16),
        ],
        scratch_shapes=[sems, sems((8,)), sems((8,)), sems((count,)), sems((8 * count,)), sems((8 * count,)), *GATHER_SEMS],
        compiler_params=params(collective_id),
        name="front",
    )(x, gains, *weights)
    return x, gains[:, :kinds].transpose(1, 0, 2).reshape(kinds, n * c), w


def attend_kernel(heads, all_ref, gain_ref, w_ref, dy_ref, starts_ref, blend_ref, *refs):
    h_out, qkv_out, dy_out, mixed_ref, diff_ref, lse_ref, mem_ref, nv_ref, x, w, hid, qkv, load_sems, x_sems, h_sems, q_sems, *sems = refs
    n, tokens, width = all_ref.shape
    rows = tokens // NSEG
    me = lax.axis_index("fsdp")
    weights = pltpu.make_async_copy(w_ref, w, load_sems.at[0])
    weights.start()

    def load(i):
        return pltpu.make_async_copy(all_ref.at[i], x.at[rest(i, 2)], x_sems.at[rest(i, 2)])

    def store(i):
        return pltpu.make_async_copy(hid.at[rest(i, 2)], h_out.at[i], h_sems.at[rest(i, 2)])

    load(0).start()
    greet([other(me, d) for d in (1, 2, 4)])
    begin, near0, near1, near2, near3, far0, far1, wait_from, end = gather_parts(dy_ref, dy_out, *sems)
    begin()
    weights.wait()

    def project(i, _):
        slot = rest(i, 2)
        for at, fn in ((3, near0), (6, near1)):

            @pl.when(i == at)
            def _():
                fn()

        @pl.when(i < n - 1)
        def _():
            load(i + 1).start()

        @pl.when(i > 1)
        def _():
            store(i - 2).wait()

        load(i).wait()
        for r in range(0, tokens, 64):
            here = x[slot, r : r + 64].astype(f32)
            inverse = lax.rsqrt(jnp.mean(here * here, axis=1, keepdims=True) + norm_eps)
            hid[slot, r : r + 64] = (here * inverse * gain_ref[...]).astype(bf16)
        store(i).start()
        made = jnp.dot(hid[slot], w[...], preferred_element_type=f32).astype(bf16)
        qkv[i] = made.reshape(NSEG, rows, made.shape[1])
        return 0

    lax.fori_loop(0, n, project, 0)
    store(n - 2).wait()
    store(n - 1).wait()
    keep = pltpu.make_async_copy(qkv, qkv_out, q_sems.at[0])
    keep.start()
    hooks = {0: near2, heads - 1: near3, heads: far0, 2 * heads - 1: far1}

    def turn(i, _):
        segment, h = lax.div(i, heads), lax.rem(i, heads)
        here = pl.ds(segment, 1)
        for at, fn in hooks.items():

            @pl.when(i == at)
            def _():
                fn()

        attention_head(
            h, heads, segment, starts_ref, blend_ref, qkv.at[:, here], mixed_ref.at[:, here], diff_ref.at[:, here],
            lse_ref.at[:, here], mem_ref, nv_ref,
        )
        return 0

    lax.fori_loop(0, NSEG * heads, turn, 0)
    for d in (1, 3, 5, 7):
        wait_from(d)
    end()
    keep.wait()


def attend(x_all, gain, wqkv, dy, starts, blend, heads, collective_id):
    n, tokens, width = x_all.shape
    rows = tokens // NSEG
    cw = heads * HEAD_DIM
    if n != 8 or heads == 1:
        here = x_all.reshape(n * tokens, width).astype(f32)
        inverse = lax.rsqrt(jnp.mean(here * here, axis=1, keepdims=True) + norm_eps)
        h_in = (here * inverse * gain).astype(bf16)
        qkv = mm(h_in, wqkv).astype(bf16).reshape(n, NSEG, rows, 3 * cw)
        dy = lax.all_gather(dy, "fsdp", axis=0)
        return h_in.reshape(x_all.shape), qkv, dy, *attention(starts, blend, qkv, heads)
    length = n * rows
    sems = pltpu.SemaphoreType.DMA
    inside = pl.BlockSpec(memory_space=pltpu.VMEM)
    pairs = heads * NSEG * length * length // 2
    return pl.pallas_call(
        functools.partial(attend_kernel, heads),
        in_specs=[ANYWHERE, inside, ANYWHERE, ANYWHERE, pl.BlockSpec(memory_space=pltpu.SMEM), inside],
        out_specs=[ANYWHERE] * 3 + [inside] * 5,
        out_shape=[
            jax.ShapeDtypeStruct(x_all.shape, bf16),
            jax.ShapeDtypeStruct((n, NSEG, rows, 3 * cw), bf16),
            jax.ShapeDtypeStruct((n, *dy.shape), bf16),
            *attention_shapes(n, rows, heads),
        ],
        scratch_shapes=[
            pltpu.VMEM((2, tokens, width), bf16),
            pltpu.VMEM(wqkv.shape, bf16),
            pltpu.VMEM((2, tokens, width), bf16),
            pltpu.VMEM((n, NSEG, rows, 3 * cw), bf16),
            *[sems((k,)) for k in (1, 2, 2, 1)],
            *GATHER_SEMS,
        ],
        compiler_params=params(collective_id, 48),
        cost_estimate=pl.CostEstimate(
            flops=pairs * 4 * HEAD_DIM + 6 * n * tokens * width * cw, transcendentals=pairs, bytes_accessed=32 << 20
        ),
        name="attend",
    )(x_all, gain, wqkv, dy, starts, blend)


def quotient(a, b):
    return a // b if isinstance(a, int) else lax.div(a, b)


def rest(a, b):
    return a % b if isinstance(a, int) else lax.rem(a, b)


def xor(index, bits):
    total = 0
    for bit in (1, 2, 4):
        a, b = rest(quotient(index, bit), 2), rest(quotient(bits, bit), 2)
        total = total + bit * (a + b - 2 * a * b)
    return total


def nth_block(i):
    return i + quotient(i, 4) * (2 - 4 * rest(quotient(i, 2), 2))


def mlp_kernel(own_ref, wgu_ref, wd_ref, dy_ref, h_out, inner_out, dgu_out, down_out, out_ref, *refs):
    wgu, wd, h, dy, inner, dgu, mine, side, near, last, weight_sems, dy_sems, h_sems, inner_sems, dgu_sems, *sems = refs
    gather_sems, sems = sems[:15], sems[15:]
    me = lax.axis_index("fsdp")
    sib, xn, yn = flip(me, 1), flip(me, 2), flip(me, 4)
    tokens, width = own_ref.shape
    fw = wd.shape[0]
    begin, near0, near1, near2, near3, far0, far1, wait_from, gather_end = gather_parts(own_ref, h, *gather_sems, own_first=True)
    back = scatter_parts(mine, side, near, last, out_ref, sems)
    loads = [
        pltpu.make_async_copy(wgu_ref, wgu, weight_sems.at[0]),
        pltpu.make_async_copy(wd_ref, wd, weight_sems.at[1]),
    ]
    for load in loads:
        load.start()

    def load_dy(i):
        owner = xor(me, nth_block(i))
        return pltpu.make_async_copy(dy_ref.at[owner], dy.at[owner], dy_sems.at[i])

    for i in range(8):
        load_dy(i).start()
    greet([sib, xn, yn])
    begin()
    back_x, back_far = back["combine"](2), back["combine"](6)
    hooks = {
        (0, 6): [near0],
        (1, 0): [lambda: wait_from(1)],
        (1, 2): [near1],
        (1, 6): [near2],
        (2, 0): [near3],
        (2, 6): [far0],
        (3, 0): [lambda: wait_from(3)],
        (3, 4): [far1],
        (4, 3): [back_x],
        (5, 0): [lambda: wait_from(7)],
        (6, 3): [back_far],
        (7, 0): [lambda: wait_from(5)],
        (7, 4): [lambda: back["onward"](0)],
        (7, 6): [lambda: back["onward"](1)],
    }
    loads[0].wait()
    loads[1].wait()
    tile = fw // 4
    wide = width // 4

    def store(i):
        slot = rest(i, 2)
        return pltpu.make_async_copy(dgu.at[slot], dgu_out.at[xor(me, nth_block(i))], dgu_sems.at[slot])

    def keep(i):
        owner = xor(me, nth_block(i))
        return pltpu.make_async_copy(h.at[owner], h_out.at[owner], h_sems.at[i])

    def keep_inner(i):
        owner = xor(me, nth_block(i))
        return pltpu.make_async_copy(inner.at[owner], inner_out.at[owner], inner_sems.at[i])

    def body(i, _):
        slot = rest(i, 2)
        block = nth_block(i)
        owner = xor(me, block)

        def point(p):
            for (step, at), fns in hooks.items():
                if at == p:

                    @pl.when(i == step)
                    def _():
                        for fn in fns:
                            fn()

        @pl.when(i > 1)
        def _():
            store(i - 2).wait()

        for t in range(4):
            point(t)
            if t == 0:
                keep(i).start()
                load_dy(i).wait()
            left = h[owner]
            cols = slice(t * tile, (t + 1) * tile)
            gate = jnp.dot(left, wgu[:, cols], preferred_element_type=f32)
            up = jnp.dot(left, wgu[:, fw + t * tile : fw + (t + 1) * tile], preferred_element_type=f32)
            back_in = dots(dy[owner], wd[cols], 1, 1)
            sig = jax.nn.sigmoid(gate)
            act = gate * sig
            inner[owner, :, cols] = (act * up).astype(bf16)
            dgu[slot, :, cols] = (back_in * up * (sig * (1.0 + gate * (1.0 - sig)))).astype(bf16)
            dgu[slot, :, fw + t * tile : fw + (t + 1) * tile] = (back_in * act).astype(bf16)
        keep_inner(i).start()
        store(i).start()
        for t in range(4):
            point(4 + t)
            cols = slice(t * wide, (t + 1) * wide)
            mine[block, :, cols] = dots(dgu[slot], wgu[cols], 1, 1).astype(bf16)

        @pl.when(lax.rem(block, 2) == 1)
        def _():
            back["to_core"](block).start()

        return 0

    lax.fori_loop(0, 8, body, 0)
    back["combine"](4)()
    back["onward"](2)
    back["combine"](0)()
    store(6).wait()
    store(7).wait()

    def keep_down(t):
        return pltpu.make_async_copy(dgu.at[t % 2], down_out.at[pl.ds(t * tile, tile)], dgu_sems.at[t % 2])

    for t in range(4):
        if t > 1:
            keep_down(t - 2).wait()
        left = inner[:, :, t * tile : (t + 1) * tile].reshape(8 * tokens, tile)
        for at in range(0, width, wide):
            right = dy[:, :, at : at + wide].reshape(8 * tokens, wide)
            dgu[t % 2, :, at : at + wide] = dots(left, right, 0, 0).astype(bf16)
        keep_down(t).start()
    back["finish"]()
    keep_down(2).wait()
    keep_down(3).wait()
    for i in range(8):
        keep(i).wait()
        keep_inner(i).wait()
    gather_end()


def scatter_parts(mine, side, near, last, out_ref, sems):
    me = lax.axis_index("fsdp")
    sib, xn, yn = flip(me, 1), flip(me, 2), flip(me, 4)
    rows = out_ref.shape[0] // PIECES
    half = PIECES // 2
    core, sems = sems[:2], sems[2:]
    hop = {"xf": sems[0:2], "xo": sems[2:4], "yf": sems[4:6], "yo": sems[6:8], "last": sems[8:10]}

    def to_core(d):
        kind = quotient(d, 2)
        return send(mine.at[d], side.at[kind], core, kind, sib)

    def span(c):
        return pl.ds(c * rows, rows)

    def go(copy):
        copy.start()

    def travel(d, c):
        if d == 6:
            return send(mine.at[6, span(c)], near.at[0, span(c)], hop["xf" if c < half else "yf"], c, xn if c < half else yn)
        if d == 2:
            return send(mine.at[2, span(c)], near.at[1, span(c)], hop["xo"], c, xn)
        return send(mine.at[4, span(c)], near.at[1, span(c)], hop["yo"], c, yn)

    def leaves(d, c):
        return d == 6 or (d == 2 and c < half) or (d == 4 and c >= half)

    def step_on(c):
        return send(mine.at[4 if c < half else 2, span(c)], last.at[span(c)], hop["last"], c, yn if c < half else xn)

    def add(d, c, ref):
        total = mine.at[d]

        def body(i, _):
            here = pl.ds(pl.multiple_of(c * rows + i * 16, 16), 16)
            total[here] = (total[here].astype(f32) + ref[here].astype(f32)).astype(bf16)
            return 0

        lax.fori_loop(0, rows // 16, body, 0)

    def combine(d):
        def run():
            send(side.at[d // 2], side.at[d // 2], core, d // 2, sib).wait_recv()
            for c in range(PIECES):
                add(d, c, side.at[d // 2])
                if leaves(d, c):
                    go(travel(d, c))

        return run

    def onward(which):
        for c in range(half) if which == 2 else [half + which]:
            d = 4 if c < half else 2
            send(near.at[0, span(c)], near.at[0, span(c)], hop["xf" if c < half else "yf"], c, xn).wait_recv()
            add(d, c, near.at[0])
            go(step_on(c))

    def finish():
        total, came = mine.at[0], near.at[1]
        for j in range(half):
            for c in (j + half, j):
                send(near.at[1, span(c)], near.at[1, span(c)], hop["xo" if c < half else "yo"], c, xn).wait_recv()
                send(last.at[span(c)], last.at[span(c)], hop["last"], c, xn).wait_recv()

                def body(i, _):
                    here = pl.ds(pl.multiple_of(c * rows + i * 16, 16), 16)
                    out_ref[here] = total[here].astype(f32) + came[here].astype(f32) + last[here].astype(f32)
                    return 0

                lax.fori_loop(0, rows // 16, body, 0)
        for d in (1, 3, 5, 7):
            to_core(d).wait_send()
        for d in (2, 4, 6):
            for c in range(PIECES):
                if leaves(d, c):
                    travel(d, c).wait_send()
        for c in range(PIECES):
            step_on(c).wait_send()

    return {"to_core": to_core, "combine": combine, "onward": onward, "finish": finish}


SCATTER_SEMS = [pltpu.SemaphoreType.DMA((4,))] * 2 + [pltpu.SemaphoreType.DMA((PIECES,))] * 10


def scatter_boxes(rows, columns):
    return [pltpu.VMEM((k, rows, columns), bf16) for k in (8, 4, 2)] + [pltpu.VMEM((rows, columns), bf16)]


def mlp(h_own, wgu, w_down, dy, collective_id):
    n, rows, width = dy.shape
    fw = w_down.shape[0]
    if n != 8:
        h = lax.all_gather(h_own, "fsdp", axis=0)
        gate_up = mm(h.reshape(n * rows, width), wgu)
        gate, up = gate_up[:, :fw], gate_up[:, fw:]
        sig = jax.nn.sigmoid(gate)
        inner = (gate * sig * up).astype(bf16)
        back_in = mm_t(dy.reshape(n * rows, width), w_down)
        d_gate = (back_in * up * (sig * (1.0 + gate * (1.0 - sig)))).astype(bf16)
        d_gu = jnp.concatenate([d_gate, (back_in * (gate * sig)).astype(bf16)], axis=1)
        d_h = lax.psum_scatter(mm_t(d_gu, wgu).astype(bf16), "fsdp", scatter_dimension=0, tiled=True).astype(f32)
        down = t_mm(inner, dy.reshape(n * rows, width)).astype(bf16)
        return h, inner.reshape(n, rows, fw), d_gu.reshape(n, rows, 2 * fw), down, d_h
    sems = pltpu.SemaphoreType.DMA
    return pl.pallas_call(
        mlp_kernel,
        in_specs=[ANYWHERE] * 4,
        out_specs=[ANYWHERE] * 4 + [pl.BlockSpec(memory_space=pltpu.VMEM)],
        out_shape=[
            jax.ShapeDtypeStruct((n, rows, width), bf16),
            jax.ShapeDtypeStruct((n, rows, fw), bf16),
            jax.ShapeDtypeStruct((n, rows, 2 * fw), bf16),
            jax.ShapeDtypeStruct((fw, width), bf16),
            jax.ShapeDtypeStruct((rows, width), f32),
        ],
        scratch_shapes=[
            pltpu.VMEM(wgu.shape, bf16),
            pltpu.VMEM(w_down.shape, bf16),
            pltpu.VMEM((n, rows, width), bf16),
            pltpu.VMEM((n, rows, width), bf16),
            pltpu.VMEM((n, rows, fw), bf16),
            pltpu.VMEM((2, rows, 2 * fw), bf16),
            *scatter_boxes(rows, width),
            *[sems((k,)) for k in (2, 8, 8, 8, 2)],
            *GATHER_SEMS,
            *SCATTER_SEMS,
        ],
        compiler_params=params(collective_id, 60),
        cost_estimate=pl.CostEstimate(flops=10 * n * rows * width * fw, transcendentals=n * rows * fw, bytes_accessed=64 << 20),
        name="mlp",
    )(h_own, wgu, w_down, dy)


def product_tiles(lhs, rhs, box, out_ref, sems, over_rows, hooks):
    columns = rhs.shape[1]
    count = out_ref.shape[0] // 256

    def rows(i):
        return pl.ds(pl.multiple_of(i * 256, 256), 256)

    def store(i):
        return pltpu.make_async_copy(
            box.at[rest(i, 2), :, pl.ds(0, columns)], out_ref.at[rows(i)], sems.at[rest(i, 2)]
        )

    def body(i, _):
        for step, fns in hooks.items():

            @pl.when(i == step)
            def _():
                for fn in fns:
                    fn()

        @pl.when(i > 1)
        def _():
            store(i - 2).wait()

        left = lhs[:, rows(i)] if over_rows else lhs[rows(i)]
        for at in range(0, columns, 512):
            here = slice(at, min(at + 512, columns))
            box[rest(i, 2), :, here] = dots(left, rhs[:, here], 0 if over_rows else 1, 0).astype(bf16)
        store(i).start()
        return 0

    lax.fori_loop(0, count, body, 0)
    for i in range(max(0, count - 2), count):
        store(i).wait()


def line_places():
    place = lax.axis_index("seq")
    inward = jnp.where(place < 2, 1, 2)
    return (place == 0) | (place == 3), inward, jnp.where(place < 2, 0, 3), 3 - inward


def greet_line(bits):
    me = lax.axis_index("fsdp")
    is_end, inward, outward, opposite = line_places()
    barrier = pltpu.get_barrier_semaphore()
    for d in bits:
        pl.semaphore_signal(barrier, inc=1, device_id={"fsdp": other(me, d)}, device_id_type=pl.DeviceIdType.MESH)

    @pl.when(is_end)
    def _():
        pl.semaphore_signal(barrier, inc=1, device_id={"seq": inward}, device_id_type=pl.DeviceIdType.MESH)
        pl.semaphore_wait(barrier, len(bits) + 1)

    @pl.when(jnp.logical_not(is_end))
    def _():
        for peer in (outward, opposite):
            pl.semaphore_signal(barrier, inc=1, device_id={"seq": peer}, device_id_type=pl.DeviceIdType.MESH)
        pl.semaphore_wait(barrier, len(bits) + 2)


HEAD_STEPS = 12


def head_rows(rows):
    return rows * 3 // 8


def head_line(own, came, half, crossed, total, sems):
    is_end, inward, outward, opposite = line_places()
    rows = own.shape[0] // HEAD_STEPS
    go_in, cross, back = sems[0:2], sems[2:4], sems[4:6]

    def at(ref, c):
        return ref.at[pl.ds(c * rows, rows)]

    def add(dst, left, right):
        def body(i, _):
            here = pl.ds(pl.multiple_of(i * 16, 16), 16)
            dst[here] = (left[here].astype(f32) + right[here].astype(f32)).astype(bf16)
            return 0

        lax.fori_loop(0, rows // 16, body, 0)

    def first(c):
        return link(at(own, c), at(came, c), go_in, c, "seq", inward)

    def second(c):
        return link(at(half, c), at(crossed, c), cross, c, "seq", opposite)

    def third(c):
        return link(at(total, c), at(total, c), back, c, "seq", outward)

    def begin():
        @pl.when(is_end)
        def _():
            for c in range(HEAD_STEPS):
                first(c).start()

    def step(j):
        def run():
            @pl.when(jnp.logical_not(is_end))
            def _():
                if j < HEAD_STEPS:
                    link(at(came, j), at(came, j), go_in, j, "seq", outward).wait_recv()
                    add(at(half, j), at(own, j), at(came, j))
                    second(j).start()
                if j >= 2:
                    c = j - 2
                    link(at(crossed, c), at(crossed, c), cross, c, "seq", opposite).wait_recv()
                    add(at(total, c), at(half, c), at(crossed, c))
                    third(c).start()

        return run

    def end():
        @pl.when(is_end)
        def _():
            for c in range(HEAD_STEPS):
                link(at(total, c), at(total, c), back, c, "seq", inward).wait_recv()
                first(c).wait_send()

        @pl.when(jnp.logical_not(is_end))
        def _():
            for c in range(HEAD_STEPS):
                second(c).wait_send()
                third(c).wait_send()

    return begin, [step(j) for j in range(HEAD_STEPS + 2)], end


def gather_products_kernel(x_ref, h_ref, dgu_ref, inner_ref, wd_ref, down_ref, out_ref, gu_ref, mlp_ref, head_ref, h, dgu, inner, wd, box, *refs):
    (own, came, half, crossed, total), refs = refs[:5], refs[5:]
    load_sems, sems, line_sems, refs = refs[0], refs[1], refs[2:8], refs[8:]
    line_begin, steps, line_end = head_line(own, came, half, crossed, total, line_sems)
    head = pltpu.make_async_copy(down_ref.at[pl.ds(0, own.shape[0])], own, load_sems.at[4])
    head.start()
    loads = [
        pltpu.make_async_copy(src, dst, load_sems.at[i])
        for i, (src, dst) in enumerate(((h_ref, h), (dgu_ref, dgu), (inner_ref, inner), (wd_ref, wd)))
    ]
    greet_line((1, 2, 4))
    begin, near0, near1, near2, near3, far0, far1, wait_from, end = gather_parts(x_ref, out_ref, *refs)
    begin()
    head.wait()
    line_begin()
    for load in loads:
        load.start()
    loads[0].wait()
    loads[1].wait()
    hooks = {i: [steps[i - 1]] for i in range(1, 8)}
    for i, fn in ((1, near0), (3, near1), (5, near2), (7, near3)):
        hooks[i].append(fn)
    product_tiles(h, dgu, box, gu_ref, sems, True, hooks)
    loads[2].wait()
    loads[3].wait()
    hooks = {0: [steps[7]], 2: [steps[8]], 3: [far0], 4: [steps[9]], 6: [steps[10]], 7: [far1]}
    product_tiles(inner, wd, box, mlp_ref, sems, False, hooks)
    for step in steps[11:]:
        step()
    for d in (1, 3, 5, 7):
        wait_from(d)
    line_end()
    out = pltpu.make_async_copy(total, head_ref, load_sems.at[4])
    out.start()
    end()
    out.wait()


def gather_products(x, h, dgu, inner, w_down, down, collective_id):
    n = lax.axis_size("fsdp")
    ahead = head_rows(down.shape[0])
    if n != 8 or lax.axis_size("seq") != 4:
        head = lax.psum(down[:ahead], "seq")
        return lax.all_gather(x, "fsdp", axis=0), t_mm(h, dgu).astype(bf16), mm(inner, w_down).astype(bf16), head
    total, width = h.shape
    sems = pltpu.SemaphoreType.DMA
    return pl.pallas_call(
        gather_products_kernel,
        in_specs=[ANYWHERE] * 6,
        out_specs=[ANYWHERE] * 4,
        out_shape=[
            jax.ShapeDtypeStruct((n, *x.shape), bf16),
            jax.ShapeDtypeStruct((width, dgu.shape[1]), bf16),
            jax.ShapeDtypeStruct((total, width), bf16),
            jax.ShapeDtypeStruct((ahead, width), bf16),
        ],
        scratch_shapes=[pltpu.VMEM(a.shape, bf16) for a in (h, dgu, inner, w_down)]
        + [pltpu.VMEM((2, 256, max(width, dgu.shape[1])), bf16), *[pltpu.VMEM((ahead, width), bf16)] * 5]
        + [sems((5,)), sems((2,)), *[sems((HEAD_STEPS,))] * 6, *GATHER_SEMS],
        compiler_params=params(collective_id, 56),
        cost_estimate=pl.CostEstimate(
            flops=2 * total * width * (inner.shape[1] + dgu.shape[1]), transcendentals=0, bytes_accessed=48 << 20
        ),
        name="gather_products",
    )(x, h, dgu, inner, w_down, down)


def block_products(me, lhs, rhs, mine, turned, back, block):
    wide = mine.shape[2] // 4
    left = lhs[xor(me, block)].reshape(-1, lhs.shape[-1])
    for t in range(4):
        cols = slice(t * wide, (t + 1) * wide)
        made = dots(left, rhs[cols], 1, 1) if turned else dots(left, rhs[:, cols], 1, 0)
        mine[block, :, cols] = made.astype(bf16)
    if block % 2 == 1:
        back["to_core"](block).start()


def product_scatter_kernel(lhs_ref, rhs_ref, out_ref, lhs, rhs, mine, side, near, last, load_sems, *sems):
    me = lax.axis_index("fsdp")
    loads = [pltpu.make_async_copy(lhs_ref, lhs, load_sems.at[0]), pltpu.make_async_copy(rhs_ref, rhs, load_sems.at[1])]
    for load in loads:
        load.start()
    greet([other(me, d) for d in (1, 2, 4)])
    back = scatter_parts(mine, side, near, last, out_ref, sems)
    for load in loads:
        load.wait()
    for block in (6, 7, 4, 5, 2, 3, 0, 1):
        block_products(me, lhs, rhs, mine, False, back, block)
        if block in (4, 2, 0):
            back["combine"](block + 2)()
    back["combine"](0)()
    for which in range(3):
        back["onward"](which)
    back["finish"]()


def product_scatter(lhs, rhs, collective_id):
    n, rows, depth = lhs.shape
    width = rhs.shape[1]
    if n != 8:
        made = mm(lhs.reshape(n * rows, depth), rhs).astype(bf16)
        return lax.psum_scatter(made, "fsdp", scatter_dimension=0, tiled=True).astype(f32)
    sems = pltpu.SemaphoreType.DMA
    return pl.pallas_call(
        product_scatter_kernel,
        in_specs=[ANYWHERE] * 2,
        out_specs=pl.BlockSpec(memory_space=pltpu.VMEM),
        out_shape=jax.ShapeDtypeStruct((rows, width), f32),
        scratch_shapes=[pltpu.VMEM(lhs.shape, bf16), pltpu.VMEM(rhs.shape, bf16), *scatter_boxes(rows, width), sems((2,)), *SCATTER_SEMS],
        compiler_params=params(collective_id, 40),
        cost_estimate=pl.CostEstimate(flops=2 * n * rows * depth * width, transcendentals=0, bytes_accessed=8 << 20),
        name="product_scatter",
    )(lhs, rhs)


SLOTS = 6
LAG = 3


def chunks_of(gu_rows, out_rows, qkv_rows, down_rows):
    out = [(3, None, r, 64) for r in range(head_rows(down_rows), down_rows, 64)]
    out += [(0, d, r, 64) for d in ORDER for r in range(0, gu_rows, 64)]
    out += [(1, None, r, 64) for r in range(0, out_rows, 64)]
    return out + [(2, d, r, 128) for d in ORDER for r in range(0, qkv_rows, 128)]


def finish_kernel(*refs):
    starts_ref, blend_ref, small_ref, x_ref, inv_ref, gain_ref, dres_ref, *refs = refs
    (gu_ref, wqkv_ref, mixed_ref, dattn_ref, hin_ref, wout_ref, qkv_ref, diff_ref, lse_ref, mem_ref, nv_ref, down_ref), refs = refs[:12], refs[12:]
    small_out, dx_ref, part_out, part_qkv, *refs = refs
    ins = [gu_ref, part_out, part_qkv, down_ref]
    kinds = 4
    outs, refs = refs[:kinds], refs[kinds:]
    first, refs = refs[:kinds], refs[kinds:]
    second, refs = refs[:kinds], refs[kinds:]
    come, refs = {0: refs[0], 2: refs[1]}, refs[2:]
    (wqkv, mixed, wout, qkv, diff, lse, mem, nv, dqkv, dmix, bias, tiles), refs = refs[:12], refs[12:]
    back_refs, refs = refs[:4], refs[4:]
    (big, side, near, last), refs = refs[:4], refs[4:]
    dattn = mine = hin = big
    (fetch_sems, box_sems), refs = refs[:2], refs[2:]
    scatter_sems, refs = refs[: len(SCATTER_SEMS)], refs[len(SCATTER_SEMS) :]
    small_work, small_come, small_sum, small_in, small_back, *refs = refs
    small_move, small_line_sems, refs = refs[0:2], refs[2:4], refs[4:]
    g_buf, a_buf, t_buf, b_buf, u_buf, loads, stores, *sems = refs
    move = {0: sems[0:2], 2: sems[2:4]}
    sems = sems[4:]
    go_in, cross, back = sems[0:2], sems[2:4], sems[4:6]
    heads = mem.shape[0]
    seg_rows = qkv.shape[2]
    me, place = lax.axis_index("fsdp"), lax.axis_index("seq")
    is_end = (place == 0) | (place == 3)
    chunks = chunks_of(gu_ref.shape[1], part_out.shape[0], part_qkv.shape[1], down_ref.shape[0])
    inward = jnp.where(place < 2, 1, 2)
    outward = jnp.where(place < 2, 0, 3)
    opposite = 3 - inward
    barrier = pltpu.get_barrier_semaphore()
    for d in range(1, 8):
        pl.semaphore_signal(barrier, inc=1, device_id={"fsdp": other(me, d)}, device_id_type=pl.DeviceIdType.MESH)

    @pl.when(is_end)
    def _():
        pl.semaphore_signal(barrier, inc=1, device_id={"seq": inward}, device_id_type=pl.DeviceIdType.MESH)
        pl.semaphore_wait(barrier, 8)

    @pl.when(jnp.logical_not(is_end))
    def _():
        for peer in (outward, opposite):
            pl.semaphore_signal(barrier, inc=1, device_id={"seq": peer}, device_id_type=pl.DeviceIdType.MESH)
        pl.semaphore_wait(barrier, 9)

    def moving(t, d):
        return link(ins[t].at[other(me, d)], come[t].at[me], move[t], d, "fsdp", other(me, d))

    def arrival(t, d):
        owner = other(me, d)
        return link(come[t].at[owner], come[t].at[owner], move[t], d, "fsdp", owner)

    def small_moving(d):
        return link(small_work.at[other(me, d)], small_come.at[me], small_move, d, "fsdp", other(me, d))

    def small_arrival(d):
        there = small_come.at[other(me, d)]
        return link(there, there, small_move, d, "fsdp", other(me, d))

    def small_hop(src, dst, slot, peer):
        return link(src, dst, small_line_sems, slot, "seq", peer)

    plan = [(t, d) for t in (0, 2) for d in ORDER[1:]]
    begun = []

    def feed(count):
        while plan and count:
            t, d = plan.pop(0)
            moving(t, d).start()
            begun.append((t, d))
            count -= 1

    def view(refs, k):
        t, d, r, rows = chunks[k]
        if d is None:
            return refs[t].at[pl.ds(r, rows)]
        return refs[t].at[other(me, d), pl.ds(r, rows)]

    def windows(k):
        t, d, r, rows = chunks[k]
        buf = box(u_buf, k, SLOTS)
        if d is None:
            return [(buf, outs[t].at[pl.ds(r, rows)])]
        kinds = outs[t].shape[0]
        c = ins[t].shape[2] // kinds
        columns = pl.ds(pl.multiple_of(other(me, d) * c, 128), c)
        return [(buf.at[:, pl.ds(i * c, c)], outs[t].at[i, pl.ds(r, rows), columns]) for i in range(kinds)]

    def source(k):
        t, d, r, rows = chunks[k]
        if d is None:
            return ins[t].at[pl.ds(r, rows)]
        if d == 0:
            return ins[t].at[me, pl.ds(r, rows)]
        return come[t].at[other(me, d), pl.ds(r, rows)]

    def await_source(k):
        t, d, r, rows = chunks[k]
        if d and r == 0:
            arrival(t, d).wait_recv()

    def box(buf, k, depth):
        t, d, r, rows = chunks[k]
        return buf.at[k % depth, pl.ds(0, rows), pl.ds(0, ins[t].shape[-1])]

    def add(dst, left, right):
        rows = dst.shape[0]

        def body(i, _):
            here = pl.ds(pl.multiple_of(i * 16, 16), 16)
            dst[here] = (left[here].astype(f32) + right[here].astype(f32)).astype(bf16)
            return 0

        lax.fori_loop(0, rows // 16, body, 0)

    def end_send(k):
        return link(source(k), view(first, k), go_in, k, "seq", inward)

    def mid_cross(k):
        return link(box(t_buf, k, SLOTS), view(second, k), cross, k, "seq", opposite)

    def mid_back(k):
        return [link(src, dst, back, k, "seq", outward) for src, dst in windows(k)]

    def store(k):
        return [pltpu.make_async_copy(src, dst, stores.at[k % SLOTS]) for src, dst in windows(k)]

    def all_back(k):
        return link(box(u_buf, k, SLOTS), box(u_buf, k, SLOTS), back, k, "seq", outward)

    def all_stored(k):
        return pltpu.make_async_copy(box(u_buf, k, SLOTS), box(u_buf, k, SLOTS), stores.at[k % SLOTS])

    def finish(k):
        link(view(second, k), view(second, k), cross, k, "seq", opposite).wait_recv()
        load = pltpu.make_async_copy(view(second, k), box(b_buf, k, 2), loads.at[2])
        load.start()
        if k >= SLOTS:
            all_back(k - SLOTS).wait_send()
            all_stored(k - SLOTS).wait()
        load.wait()
        add(box(u_buf, k, SLOTS), box(t_buf, k, SLOTS), box(b_buf, k, 2))
        for copy in mid_back(k) + store(k):
            copy.start()

    count = len(chunks)
    way = scatter_parts(mine, side, near, last, dx_ref, scatter_sems)
    pairs = (
        (dattn_ref, dattn), (wout_ref, wout), (mixed_ref, mixed), (qkv_ref, qkv), (diff_ref, diff), (lse_ref, lse),
        (mem_ref, mem), (nv_ref, nv), (wqkv_ref, wqkv), (hin_ref, hin),
    )
    fetches = [pltpu.make_async_copy(src, dst, fetch_sems.at[i]) for i, (src, dst) in enumerate(pairs)]

    def d_mixed():
        bias[...] = jnp.zeros_like(bias)
        for ref in back_refs[2:]:
            ref[...] = jnp.zeros_like(ref)

        def body(i, _):
            dmix[i] = dots(dattn[i], wout[...], 1, 1).reshape(dmix.shape[1:])
            return 0

        lax.fori_loop(0, 8, body, 0)

    def attention_part(segment, i):
        def run():
            here = slice(segment, segment + 1)

            def body(h, _):
                back_block(
                    i, h, heads, segment, starts_ref, blend_ref, qkv.at[:, here], dmix.at[:, here], diff.at[:, here],
                    lse.at[:, here], mem, nv, dqkv.at[:, here], bias, *back_refs,
                )
                return 0

            lax.fori_loop(0, heads, body, 0)

        return run

    def attention_end(segment):
        def run():
            here = slice(segment, segment + 1)

            def body(h, _):
                back_end(h, heads, segment, starts_ref, qkv.at[:, here], dqkv.at[:, here], *back_refs)
                return 0

            lax.fori_loop(0, heads, body, 0)

        return run

    def products(block):
        return lambda: block_products(me, dqkv, wqkv, mine, True, way, block)

    def fetched(*which):
        def run():
            for i in which:
                fetches[i].wait()

        return run

    def put(j, columns):
        src = tiles.at[j % 2, :, pl.ds(0, columns)]
        return pltpu.make_async_copy(src, part_out if j == 0 else part_qkv.at[j - 1], box_sems.at[j % 2])

    def out_tile():
        for at in range(0, tiles.shape[2], 512):
            right = dattn[:, :, at : at + 512].reshape(-1, 512)
            tiles[0, :, at : at + 512] = dots(mixed[...].reshape(-1, mixed.shape[2]), right, 0, 0).astype(bf16)
        put(0, tiles.shape[2]).start()

    columns = dqkv.shape[3]

    def qkv_tile(j):
        def run():
            if j >= 2:
                put(j - 2, tiles.shape[2] if j == 2 else columns).wait()
            rows = part_qkv.shape[1]
            left = hin[:, :, (j - 1) * rows : j * rows].reshape(-1, rows)
            for at in range(0, columns, 256):
                right = dqkv[:, :, :, at : at + 256].reshape(-1, 256)
                tiles[j % 2, :, at : at + 256] = dots(left, right, 0, 0).astype(bf16)
            put(j, columns).start()

        return run

    def all_put():
        put(7, columns).wait()
        put(8, columns).wait()

    def small_start():
        small_work[...] = small_ref[...]
        c = small_work.shape[2]
        inverse = inv_ref[...]
        for j in range(8):
            here = slice(j * c, (j + 1) * c)
            normed = x_ref[:, here].astype(f32) * inverse
            small_work[j, 0:1] = jnp.sum(normed * dx_ref[:, here], axis=0, keepdims=True)
        lanes = lax.broadcasted_iota(jnp.int32, (1, c), 1)
        row = jnp.zeros((1, c), f32)
        for h in range(heads):
            cols = slice(h * HEAD_DIM, (h + 1) * HEAD_DIM)
            gate = blend_ref[:, cols]
            row = row + jnp.where(lanes == h, jnp.sum(bias[:, cols] * gate * (1.0 - gate), axis=1, keepdims=True), 0.0)
        small_work[me, 2:3] = row
        for d in range(1, 8):
            small_moving(d).start()
        small_come[me] = small_work[me]
        for r in range(0, dx_ref.shape[0], 64):
            here = slice(r, r + 64)
            normed = x_ref[here].astype(f32) * inv_ref[here]
            t = dx_ref[here] * gain_ref[...]
            dx_ref[here] = dres_ref[here] + norm_back(t, normed, inv_ref[here])

    def small_first():
        for d in range(1, 8):
            small_arrival(d).wait_recv()
        small_sum[...] = jnp.sum(small_come[...], axis=0)

        @pl.when(is_end)
        def _():
            small_hop(small_sum, small_in, 0, inward).start()

        @pl.when(jnp.logical_not(is_end))
        def _():
            small_hop(small_in, small_in, 0, outward).wait_recv()
            small_sum[...] = small_sum[...] + small_in[...]
            small_hop(small_sum, small_back, 1, opposite).start()

    blocks = 8 * qkv.shape[2] // 256
    work = {
        0: [fetched(0, 1), d_mixed],
        1: [fetched(2, 3, 4, 5, 6, 7, 8)],
        10: [products(4), products(5)],
        11: [way["combine"](6), products(2), products(3)],
        12: [way["combine"](4), products(0), products(1)],
        13: [way["combine"](2)],
        14: [way["combine"](0)],
        19: [lambda: way["onward"](0)],
        20: [lambda: way["onward"](1)],
        21: [lambda: way["onward"](2)],
        26: [way["finish"], fetches[9].start],
        27: [small_start],
        28: [fetched(9), qkv_tile(1), qkv_tile(2)],
        29: [qkv_tile(3), qkv_tile(4)],
        30: [qkv_tile(5), qkv_tile(6)],
        31: [qkv_tile(7), qkv_tile(8)],
        32: [all_put],
        38: [small_first],
    }
    for i in range(4):
        work[1 + i] = work.get(1 + i, []) + [attention_part(1, i)]
        work[5 + i] = ([attention_end(1)] if i == 0 else []) + [attention_part(0, i)]
    work[9] = [attention_end(0), out_tile, products(6), products(7)]
    for fetch in fetches[:9]:
        fetch.start()
    feed(3)
    ahead = 4
    for k in range(count):
        if k % 4 == 3 and k < 16:
            feed(1)
        if k >= 33:
            feed(2)

        @pl.when(is_end)
        def _():
            for j in range(ahead + 1) if k == 0 else [k + ahead]:
                if j < count:
                    await_source(j)
                    end_send(j).start()

        @pl.when(jnp.logical_not(is_end))
        def _():
            await_source(k)
            own = pltpu.make_async_copy(source(k), box(g_buf, k, 2), loads.at[0])
            own.start()
            link(view(first, k), view(first, k), go_in, k, "seq", outward).wait_recv()
            got = pltpu.make_async_copy(view(first, k), box(a_buf, k, 2), loads.at[1])
            got.start()
            if k >= SLOTS:
                mid_cross(k - SLOTS).wait_send()
            own.wait()
            got.wait()
            add(box(t_buf, k, SLOTS), box(g_buf, k, 2), box(a_buf, k, 2))
            mid_cross(k).start()
            if k >= LAG:
                finish(k - LAG)

        for fn in work.get(k, ()):
            fn()

    @pl.when(jnp.logical_not(is_end))
    def _():
        small_hop(small_back, small_back, 1, opposite).wait_recv()
        small_hop(small_sum, small_back, 1, opposite).wait_send()
        small_out[...] = small_sum[...] + small_back[...]
        small_hop(small_out, small_out, 2, outward).start()

    @pl.when(is_end)
    def _():
        small_hop(small_out, small_out, 2, inward).wait_recv()
        small_hop(small_sum, small_in, 0, inward).wait_send()
        for k in range(count):
            all_back(k).wait_recv()
            end_send(k).wait_send()

    @pl.when(jnp.logical_not(is_end))
    def _():
        for k in range(count - LAG, count):
            finish(k)
        small_hop(small_out, small_out, 2, outward).wait_send()
        for k in range(max(0, count - SLOTS), count):
            mid_cross(k).wait_send()
            all_back(k).wait_send()
            all_stored(k).wait()

    for t, d in begun:
        moving(t, d).wait_send()
    for d in range(1, 8):
        small_moving(d).wait_send()


def finish(starts, blend, small, x, inv, gain, dres, gu, wqkv, mixed, dattn, hin, wout, qkv, diff, lse, mem, nv, down, collective_id):
    n, per, _ = gu.shape
    rows, width = x.shape
    heads = mem.shape[0]
    cw = heads * HEAD_DIM
    if lax.axis_size("seq") != 4 or n != 8 or heads == 1:
        total = n * rows
        dmix = mm_t(dattn.reshape(total, width), wout).reshape(diff.shape)
        dqkv, bias = attention_back(starts, blend, qkv, dmix, diff, lse, mem, nv, heads)
        dqkv = dqkv.reshape(total, 3 * cw)
        dhin = lax.psum_scatter(mm_t(dqkv, wqkv).astype(bf16), "fsdp", scatter_dimension=0, tiled=True).astype(f32)
        normed = x.astype(f32) * inv
        small = small.at[:, 0].set(jnp.sum(normed * dhin, axis=0).reshape(n, per))
        bias = jnp.sum((bias * blend * (1.0 - blend)).reshape(heads, HEAD_DIM), axis=1)
        own = (jnp.arange(n) == lax.axis_index("fsdp"))[:, None]
        small = small.at[:, 2].set(jnp.where(own, jnp.pad(bias, (0, per - heads))[None], 0.0))
        dx = dres + norm_back(dhin * gain, normed, inv)
        out = lax.psum(t_mm(mixed.reshape(total, cw), dattn.reshape(total, width)).astype(bf16), "seq")
        made = t_mm(hin.reshape(total, width), dqkv).astype(bf16).reshape(n, per, 3 * cw)
        moved = []
        for y, count in ((gu, 2), (made, 3)):
            c = y.shape[2] // count
            y = lax.psum(lax.all_to_all(y, "fsdp", split_axis=0, concat_axis=0, tiled=True), "seq")
            moved.append(y.reshape(n, per, count, c).transpose(2, 1, 0, 3).reshape(count, per, n * c))
        small = lax.psum(lax.psum_scatter(small, "fsdp", scatter_dimension=0), "seq")
        return small, dx, out, *moved, lax.psum(down, "seq")
    made = jax.ShapeDtypeStruct((n, per, 3 * cw), bf16)
    out = jax.ShapeDtypeStruct((cw, width), bf16)
    gu_shape = jax.ShapeDtypeStruct(gu.shape, bf16)
    count = len(chunks_of(per, cw, per, down.shape[0]))
    down_shape = jax.ShapeDtypeStruct(down.shape, bf16)
    inside = pl.BlockSpec(memory_space=pltpu.VMEM)
    sems = pltpu.SemaphoreType.DMA
    small_sum, dx, _, _, sum_gu, sum_out, sum_qkv, sum_down, *_ = pl.pallas_call(
        finish_kernel,
        in_specs=[pl.BlockSpec(memory_space=pltpu.SMEM)] + [inside] * 6 + [ANYWHERE] * 12,
        out_specs=[inside] * 2 + [ANYWHERE] * 16,
        out_shape=[
            jax.ShapeDtypeStruct(small.shape[1:], f32),
            jax.ShapeDtypeStruct((rows, width), f32),
            out,
            made,
            jax.ShapeDtypeStruct((2, per, gu.shape[2] // 2 * n), bf16),
            out,
            jax.ShapeDtypeStruct((3, per, cw * n), bf16),
            down_shape,
            *[gu_shape, out, made, down_shape] * 2,
            gu_shape,
            made,
        ],
        scratch_shapes=[pltpu.VMEM(y.shape, y.dtype) for y in (wqkv, mixed, wout, qkv, diff, lse, mem, nv)]
        + [pltpu.VMEM(qkv.shape, bf16), pltpu.VMEM(diff.shape, f32), pltpu.VMEM((1, cw), f32)]
        + [pltpu.VMEM((2, per, width), bf16)]
        + back_boxes(n, qkv.shape[2], heads)
        + scatter_boxes(rows, width)
        + [sems((10,)), sems((2,)), *SCATTER_SEMS]
        + [pltpu.VMEM(small.shape, f32)] * 2
        + [pltpu.VMEM(small.shape[1:], f32)] * 3
        + [sems((8,)), sems((8,)), sems((3,)), sems((3,))]
        + [pltpu.VMEM((depth, 128, gu.shape[2]), bf16) for depth in (2, 2, SLOTS, 2, SLOTS)]
        + [sems((3,)), sems((SLOTS,))]
        + [sems((8,))] * 4
        + [sems((count,))] * 6,
        compiler_params=params(collective_id, 62),
        name="finish",
    )(starts, blend, small, x, inv, gain, dres, gu, wqkv, mixed, dattn, hin, wout, qkv, diff, lse, mem, nv, down)
    return small_sum, dx, sum_out, sum_gu, sum_qkv, sum_down


def shards(
    tokens,
    doc_starts,
    norm_in,
    w_query,
    w_key,
    w_value,
    mix_bias,
    w_out,
    norm_mid,
    w_gate,
    w_up,
    w_down,
    cotangent,
):
    rows = tokens.shape[2]
    width = tokens.shape[3]
    n = lax.axis_size("fsdp")
    s = lax.axis_size("seq")
    own = NSEG * rows
    total = n * own
    seg_len = rows * n
    heads = HEADS // n
    cw = heads * HEAD_DIM
    fw = w_gate.shape[1] // n

    wgu = to_columns_in_turns([w_gate, w_up], 7)
    flat_in = tokens.reshape(own, width)
    all_in, gains, wqkv = front(flat_in, jnp.stack([norm_in, norm_mid]), [w_query, w_key, w_value], 0)
    gain_in, gain_mid = gains[0][None], gains[1][None]

    def normed(rows_in):
        rows_in = rows_in.astype(f32)
        inverse = lax.rsqrt(jnp.mean(rows_in * rows_in, axis=1, keepdims=True) + norm_eps)
        return rows_in * inverse, inverse

    flat_in = flat_in.astype(f32)
    normed_in, inv_in = normed(flat_in)
    blend = jax.nn.sigmoid(mix_bias)
    blend_row = jnp.repeat(blend, HEAD_DIM)[None]
    h_in, qkv, dy, mixed, diff, lse, memory, norm_vec = attend(
        all_in, gain_in, wqkv, cotangent.reshape(own, width), doc_starts[0], blend_row, heads, 4
    )
    h_in, dy = h_in.reshape(total, width), dy.reshape(total, width)
    mixed = mixed.reshape(total, cw)

    attn_sum = product_scatter(mixed.reshape(n, own, cw), w_out, 3)
    residual = flat_in + attn_sum
    inv_mid = lax.rsqrt(jnp.mean(residual * residual, axis=1, keepdims=True) + norm_eps)
    normed_mid = residual * inv_mid
    h_mid = (normed_mid * gain_mid).astype(bf16)
    h_mid, inner, d_gu, part_down, d_hmid = mlp(h_mid, wgu, w_down, dy.reshape(n, own, width), 1)
    h_mid, inner, d_gu = (x.reshape(total, x.shape[2]) for x in (h_mid, inner, d_gu))

    gain_mid_term = jnp.sum(normed_mid * d_hmid, axis=0)
    d_resid = cotangent.reshape(own, width).astype(f32) + norm_back(d_hmid * gain_mid, normed_mid, inv_mid)
    d_attn, part_gu, part_mlp, sum_head = gather_products(d_resid.astype(bf16), h_mid, d_gu, inner, w_down, part_down, 2)
    part_gu = part_gu.reshape(n, width // n, 2 * fw)

    mlp_sum = lax.psum_scatter(part_mlp, "fsdp", scatter_dimension=0, tiled=True)
    block_out = (residual + mlp_sum.astype(f32)).astype(bf16).reshape(tokens.shape)
    per = width // n
    terms = jnp.pad(gain_mid_term.reshape(n, 1, per), ((0, 0), (1, 6), (0, 0)))
    small, grad_tokens, sum_out, sum_gu, sum_qkv, sum_down = finish(
        doc_starts[0],
        blend_row,
        terms,
        tokens.reshape(own, width),
        inv_in,
        gain_in,
        d_resid,
        part_gu,
        wqkv,
        mixed.reshape(n, own, cw),
        d_attn,
        h_in.reshape(n, own, width),
        w_out,
        qkv,
        diff,
        lse,
        memory,
        norm_vec,
        part_down,
        6,
    )
    grad_down = jnp.concatenate([sum_head, sum_down[sum_head.shape[0] :]]).astype(f32)
    grad_tokens = grad_tokens.reshape(tokens.shape)
    grad_out = sum_out.astype(f32)
    grad_gate, grad_up = sum_gu[0].astype(f32), sum_gu[1].astype(f32)
    grad_q, grad_k, grad_v = (sum_qkv[i].astype(f32) for i in range(3))

    return (
        block_out,
        grad_tokens,
        small[0],
        grad_q,
        grad_k,
        grad_v,
        small[2, :heads],
        grad_out,
        small[1],
        grad_gate,
        grad_up,
        grad_down,
    )


def solution(mesh):
    whole = P("seq", None, "fsdp", None)
    matrix, vector = P("fsdp", None), P("fsdp")
    return jax.shard_map(
        shards,
        mesh=mesh,
        in_specs=(whole, P("seq", None), vector, matrix, matrix, matrix, vector, matrix, vector, matrix, matrix, matrix, whole),
        out_specs=(whole, whole, vector, matrix, matrix, matrix, vector, matrix, vector, matrix, matrix, matrix),
        check_vma=False,
    )
```

```python
import functools

import jax
import jax.numpy as jnp
from jax import lax
from jax.experimental import pallas as pl
from jax.experimental.pallas import tpu as pltpu
from jax.sharding import PartitionSpec as P

HEADS = 16
HEAD_DIM = 128
NSEG = 2

highest = lax.Precision.HIGHEST
norm_eps = 1e-05
f32 = jnp.float32
bf16 = jnp.bfloat16


def doc_number(start_row, places):
    return jnp.sum((start_row[None, :] <= places[:, None]).astype(jnp.int32), axis=1) - 1


def norm_back(grad_in, normed, inverse):
    return inverse * (grad_in - normed * jnp.mean(grad_in * normed, axis=-1, keepdims=True))


def mm(a, b):
    return lax.dot_general(a, b, (((1,), (0,)), ((), ())), preferred_element_type=f32)


def mm_t(a, b):
    return lax.dot_general(a, b, (((1,), (1,)), ((), ())), preferred_element_type=f32)


def t_mm(a, b):
    return lax.dot_general(a, b, (((0,), (0,)), ((), ())), preferred_element_type=f32)


def dots(a, b, ca, cb, precision=None):
    return lax.dot_general(a, b, (((ca,), (cb,)), ((), ())), preferred_element_type=f32, precision=precision)


def phi(u):
    return jnp.where(u > 0, u + 1.0, jnp.exp(jnp.minimum(u, 0.0)))


def phi_slope(u):
    return jnp.where(u > 0, 1.0, jnp.exp(jnp.minimum(u, 0.0)))


def when(condition):
    if isinstance(condition, bool):
        return (lambda run: run()) if condition else (lambda run: None)
    return pl.when(condition)


def docs_at(starts_ref, places):
    total = -1
    for k in range(starts_ref.shape[0]):
        total = total + (starts_ref[k] <= places).astype(jnp.int32)
    return total


def cross_doc(starts_ref, length):
    total = -1
    for k in range(starts_ref.shape[0]):
        total = total + jnp.where(starts_ref[k] <= length, 1, 0)
    return total


def in_cross(starts_ref, length, segment, first, count):
    places = lax.broadcasted_iota(jnp.int32, (count, 1), 0) + (segment * length + first)
    return (docs_at(starts_ref, places) == cross_doc(starts_ref, length)).astype(f32)


def may_see(starts_ref, length, segment, first, block, span):
    rows = lax.broadcasted_iota(jnp.int32, (block, 1), 0) + first
    cols = lax.broadcasted_iota(jnp.int32, (1, span), 1)
    own = docs_at(starts_ref, rows + segment * length)
    return (cols <= rows) & (docs_at(starts_ref, cols + segment * length) == own)


def head_columns(kind, h, heads):
    at = kind * heads * HEAD_DIM + h * HEAD_DIM
    return slice(at, at + HEAD_DIM) if isinstance(at, int) else pl.ds(pl.multiple_of(at, HEAD_DIM), HEAD_DIM)


def attention_head(h, heads, segment, starts_ref, blend_ref, qkv_ref, mixed_ref, diff_ref, lse_ref, mem_ref, nv_ref):
    n, _, rows, _ = qkv_ref.shape
    length = n * rows
    take = max(1, 256 // rows)
    block = take * rows
    scale = HEAD_DIM ** (-0.5)
    cols = head_columns(0, h, heads)

    def part(kind, lo, hi):
        return qkv_ref[lo:hi, 0, :, head_columns(kind, h, heads)].reshape((hi - lo) * rows, HEAD_DIM)

    @when(segment == 0)
    def _():
        fk = phi(part(1, 0, n).astype(f32)) * in_cross(starts_ref, length, 0, 0, length)
        mem_ref[h] = dots(fk, part(2, 0, n).astype(f32), 0, 0, highest)
        nv_ref[h] = jnp.sum(fk, axis=0, keepdims=True)

    blend = blend_ref[:, cols]
    for i in range(n // take):
        lo, hi = i * take, (i + 1) * take
        span = (i + 1) * block
        q = part(0, lo, hi)
        s = dots(q, part(1, 0, hi), 1, 1) * scale
        s = jnp.where(may_see(starts_ref, length, segment, i * block, block, span), s, -1000000000.0)
        top = jnp.max(s, axis=1, keepdims=True)
        p = jnp.exp(s - top)
        tot = jnp.sum(p, axis=1, keepdims=True)
        lse_ref[h, 0, i * block : (i + 1) * block] = top + jnp.log(tot)
        direct = dots((p / tot).astype(bf16), part(2, 0, hi), 1, 0)
        shape = (take, rows, HEAD_DIM)

        @when(segment == 0)
        def _():
            mixed_ref[lo:hi, 0, :, cols] = ((1.0 - blend) * direct).astype(bf16).reshape(shape)
            diff_ref[lo:hi, 0, :, cols] = (-direct).reshape(shape)

        @when(segment != 0)
        def _():
            fq = phi(q.astype(f32))
            numer = dots(fq, mem_ref[h], 1, 0, highest)
            den = jnp.sum(fq * nv_ref[h], axis=1, keepdims=True) + 1.0
            ret = in_cross(starts_ref, length, 1, i * block, block) * numer / den
            mixed_ref[lo:hi, 0, :, cols] = (blend * ret + (1.0 - blend) * direct).astype(bf16).reshape(shape)
            diff_ref[lo:hi, 0, :, cols] = (ret - direct).reshape(shape)


def attention_kernel(heads, starts_ref, blend_ref, *refs):
    for h in range(heads):
        attention_head(h, heads, pl.program_id(0), starts_ref, blend_ref, *refs)


def back_block(i, h, heads, segment, starts_ref, blend_ref, qkv_ref, dmix_ref, diff_ref, lse_ref, mem_ref, nv_ref, out_ref, bias_ref, dk_acc, dv_acc, dmem, dnv):
    n, _, rows, _ = qkv_ref.shape
    length = n * rows
    take = max(1, 256 // rows)
    block = take * rows
    scale = HEAD_DIM ** (-0.5)
    shape = (take, rows, HEAD_DIM)
    cols = head_columns(0, h, heads)
    blend = blend_ref[:, cols]
    lo, hi = i * take, (i + 1) * take
    span = (i + 1) * block
    here = slice(i * block, (i + 1) * block)

    def part(kind, lo, hi):
        return qkv_ref[lo:hi, 0, :, head_columns(kind, h, heads)].reshape((hi - lo) * rows, HEAD_DIM)

    if i == 0:
        dk_acc[h] = jnp.zeros(dk_acc.shape[1:], f32)
        dv_acc[h] = jnp.zeros(dv_acc.shape[1:], f32)
    q, k, v = part(0, lo, hi), part(1, 0, hi), part(2, 0, hi)
    dmix = dmix_ref[lo:hi, 0, :, cols].reshape(block, HEAD_DIM)
    bias_ref[:, cols] += jnp.sum(dmix * diff_ref[lo:hi, 0, :, cols].reshape(block, HEAD_DIM), axis=0, keepdims=True)
    ddir = ((1.0 - blend) * dmix).astype(bf16)
    s = dots(q, k, 1, 1) * scale
    allowed = may_see(starts_ref, length, segment, i * block, block, span)
    e = jnp.exp(jnp.where(allowed, s, -1000000000.0) - lse_ref[h, 0, here])
    dp = dots(ddir, v, 1, 1)
    bal = jnp.sum(e * dp, axis=1, keepdims=True)
    ds = (e * (dp - bal)).astype(bf16)
    dv_acc[h, :span] += dots(e.astype(bf16), ddir, 0, 0)
    dk_acc[h, :span] += dots(ds, q, 0, 0) * scale
    dq = dots(ds, k, 1, 0) * scale

    @when(segment == 0)
    def _():
        out_ref[lo:hi, 0, :, cols] = dq.astype(bf16).reshape(shape)

    @when(segment != 0)
    def _():
        q32 = q.astype(f32)
        fq = phi(q32)
        numer = dots(fq, mem_ref[h], 1, 0, highest)
        den = jnp.sum(fq * nv_ref[h], axis=1, keepdims=True) + 1.0
        dnum = in_cross(starts_ref, length, 1, i * block, block) * (blend * dmix) / den
        dden = -jnp.sum(dnum * numer, axis=1, keepdims=True) / den
        dmem[h] += dots(fq, dnum, 0, 0, highest)
        dnv[h] += jnp.sum(dden * fq, axis=0, keepdims=True)
        dfq = dots(dnum, mem_ref[h], 1, 1, highest) + dden * nv_ref[h]
        out_ref[lo:hi, 0, :, cols] = (dq + dfq * phi_slope(q32)).astype(bf16).reshape(shape)


def back_end(h, heads, segment, starts_ref, qkv_ref, out_ref, dk_acc, dv_acc, dmem, dnv):
    n, _, rows, _ = qkv_ref.shape
    length = n * rows
    whole = (n, rows, HEAD_DIM)
    kcols, vcols = head_columns(1, h, heads), head_columns(2, h, heads)

    @when(segment != 0)
    def _():
        out_ref[:, 0, :, kcols] = dk_acc[h].astype(bf16).reshape(whole)
        out_ref[:, 0, :, vcols] = dv_acc[h].astype(bf16).reshape(whole)

    @when(segment == 0)
    def _():
        k32 = qkv_ref[:, 0, :, kcols].reshape(length, HEAD_DIM).astype(f32)
        v32 = qkv_ref[:, 0, :, vcols].reshape(length, HEAD_DIM).astype(f32)
        key_set = in_cross(starts_ref, length, 0, 0, length)
        mem_v = key_set * dots(phi(k32), dmem[h], 1, 0, highest)
        mem_k = key_set * (dots(v32, dmem[h], 1, 1, highest) + dnv[h]) * phi_slope(k32)
        out_ref[:, 0, :, kcols] = (dk_acc[h] + mem_k).astype(bf16).reshape(whole)
        out_ref[:, 0, :, vcols] = (dv_acc[h] + mem_v).astype(bf16).reshape(whole)


def attention_back_kernel(heads, starts_ref, blend_ref, qkv_ref, dmix_ref, diff_ref, lse_ref, mem_ref, nv_ref, out_ref, bias_ref, dk_acc, dv_acc, dmem, dnv):
    n, _, rows, _ = qkv_ref.shape

    @pl.when(pl.program_id(0) == 0)
    def _():
        bias_ref[...] = jnp.zeros_like(bias_ref)
        dmem[...] = jnp.zeros_like(dmem)
        dnv[...] = jnp.zeros_like(dnv)

    segment = NSEG - 1 - pl.program_id(0)
    for h in range(heads):
        for i in range(n * rows // (max(1, 256 // rows) * rows)):
            back_block(
                i, h, heads, segment, starts_ref, blend_ref, qkv_ref, dmix_ref, diff_ref, lse_ref, mem_ref, nv_ref,
                out_ref, bias_ref, dk_acc, dv_acc, dmem, dnv,
            )
        back_end(h, heads, segment, starts_ref, qkv_ref, out_ref, dk_acc, dv_acc, dmem, dnv)


def attention_specs(n, rows, heads, pick):
    length = n * rows
    cw = heads * HEAD_DIM
    starts = pl.BlockSpec(memory_space=pltpu.SMEM)
    wide = pl.BlockSpec((n, 1, rows, 3 * cw), lambda g: (0, pick(g), 0, 0))
    narrow = pl.BlockSpec((n, 1, rows, cw), lambda g: (0, pick(g), 0, 0))
    lse = pl.BlockSpec((heads, 1, length, 1), lambda g: (0, pick(g), 0, 0))
    line = pl.BlockSpec((1, cw), lambda g: (0, 0))
    mem = pl.BlockSpec((heads, HEAD_DIM, HEAD_DIM), lambda g: (0, 0, 0))
    nv = pl.BlockSpec((heads, 1, HEAD_DIM), lambda g: (0, 0, 0))
    return starts, wide, narrow, lse, line, mem, nv


def attention(starts_row, blend_row, qkv, heads):
    n, _, rows, _ = qkv.shape
    length = n * rows
    cw = heads * HEAD_DIM
    starts, wide, narrow, lse, line, mem, nv = attention_specs(n, rows, heads, lambda g: g)
    pairs = heads * NSEG * length * length // 2
    return pl.pallas_call(
        functools.partial(attention_kernel, heads),
        grid=(NSEG,),
        in_specs=[starts, line, wide],
        out_specs=[narrow, narrow, lse, mem, nv],
        out_shape=attention_shapes(n, rows, heads),
        compiler_params=pltpu.CompilerParams(vmem_limit_bytes=48 << 20),
        cost_estimate=pl.CostEstimate(flops=pairs * 4 * HEAD_DIM, transcendentals=pairs, bytes_accessed=8 << 20),
        name="attention",
    )(starts_row, blend_row, qkv)


def attention_shapes(n, rows, heads):
    return [
        jax.ShapeDtypeStruct((n, NSEG, rows, heads * HEAD_DIM), bf16),
        jax.ShapeDtypeStruct((n, NSEG, rows, heads * HEAD_DIM), f32),
        jax.ShapeDtypeStruct((heads, NSEG, n * rows, 1), f32),
        jax.ShapeDtypeStruct((heads, HEAD_DIM, HEAD_DIM), f32),
        jax.ShapeDtypeStruct((heads, 1, HEAD_DIM), f32),
    ]


def back_boxes(n, rows, heads):
    return [
        pltpu.VMEM((heads, n * rows, HEAD_DIM), f32),
        pltpu.VMEM((heads, n * rows, HEAD_DIM), f32),
        pltpu.VMEM((heads, HEAD_DIM, HEAD_DIM), f32),
        pltpu.VMEM((heads, 1, HEAD_DIM), f32),
    ]


def attention_back(starts_row, blend_row, qkv, dmix, diff, lse_rows, mem_all, nv_all, heads):
    n, _, rows, _ = qkv.shape
    length = n * rows
    cw = heads * HEAD_DIM
    starts, wide, narrow, lse, line, mem, nv = attention_specs(n, rows, heads, lambda g: NSEG - 1 - g)
    pairs = heads * NSEG * length * length // 2
    return pl.pallas_call(
        functools.partial(attention_back_kernel, heads),
        grid=(NSEG,),
        in_specs=[starts, line, wide, narrow, narrow, lse, mem, nv],
        out_specs=[wide, line],
        out_shape=[
            jax.ShapeDtypeStruct((n, NSEG, rows, 3 * cw), bf16),
            jax.ShapeDtypeStruct((1, cw), f32),
        ],
        scratch_shapes=back_boxes(n, rows, heads),
        compiler_params=pltpu.CompilerParams(vmem_limit_bytes=56 << 20),
        cost_estimate=pl.CostEstimate(flops=pairs * 10 * HEAD_DIM, transcendentals=pairs, bytes_accessed=16 << 20),
        name="attention_back",
    )(starts_row, blend_row, qkv, dmix, diff, lse_rows, mem_all, nv_all)


def flip(index, bit):
    return index + bit - 2 * bit * lax.rem(lax.div(index, bit), 2)


def other(index, bits):
    for bit in (1, 2, 4):
        if bits & bit:
            index = flip(index, bit)
    return index


def link(src, dst, sems, slot, axis, peer):
    return pltpu.make_async_remote_copy(
        src_ref=src, dst_ref=dst, send_sem=sems[0].at[slot], recv_sem=sems[1].at[slot],
        device_id={axis: peer}, device_id_type=pl.DeviceIdType.MESH,
    )


def send(src, dst, sems, slot, peer):
    return link(src, dst, sems, slot, "fsdp", peer)


def greet(peers):
    barrier = pltpu.get_barrier_semaphore()
    for peer in peers:
        pl.semaphore_signal(barrier, inc=1, device_id={"fsdp": peer}, device_id_type=pl.DeviceIdType.MESH)
    pl.semaphore_wait(barrier, len(peers))


PIECES = 4
ORDER = (0, 1, 2, 4, 3, 5, 6, 7)
GATHER_SEMS = [pltpu.SemaphoreType.DMA] + [pltpu.SemaphoreType.DMA((PIECES,))] * 14


def gather_parts(x_ref, out_ref, local_sem, *sems, own_first=False):
    me = lax.axis_index("fsdp")
    sib, xn, yn, far_owner = flip(me, 1), flip(me, 2), flip(me, 4), other(me, 6)
    rows = x_ref.shape[0] // PIECES
    half = PIECES // 2
    own, over_x, over_y, far = sems[0:2], sems[2:4], sems[4:6], sems[6:8]
    side_x, side_y, side_far = sems[8:10], sems[10:12], sems[12:14]
    started = []

    def at(owner, c):
        return out_ref.at[owner, pl.ds(c * rows, rows)]

    def mine(c):
        return x_ref.at[pl.ds(c * rows, rows)]

    def go(make):
        make().start()
        started.append(make)

    def pass_on(owner, c, sems, peer):
        go(lambda: send(at(owner, c), at(owner, c), sems, c, peer))

    def arrived(owner, c, sems):
        send(at(owner, c), at(owner, c), sems, c, sib).wait_recv()

    local = pltpu.make_async_copy(x_ref, out_ref.at[me], local_sem)

    def begin_one(c, sems, peer):
        return send(mine(c), at(me, c), sems, c, peer)

    def begin():
        local.start()
        for j in range(PIECES):
            c, d = j, (j + half) % PIECES
            go(functools.partial(begin_one, c, over_x, xn))
            go(functools.partial(begin_one, d, over_y, yn))
        for c in range(PIECES):
            go(functools.partial(begin_one, c, own, sib))
        if own_first:
            local.wait()

    def near(j):
        c, d = j, (j + half) % PIECES
        arrived(xn, c, over_x)
        if c < half:
            pass_on(xn, c, far, yn)
        pass_on(xn, c, side_x, sib)
        arrived(yn, d, over_y)
        if d >= half:
            pass_on(yn, d, far, xn)
        pass_on(yn, d, side_y, sib)

    def beyond(j):
        for c in (j, j + half):
            arrived(far_owner, c, far)
            pass_on(far_owner, c, side_far, sib)

    def wait_from(d):
        for c in range(PIECES):
            arrived(other(me, d), c, {1: own, 3: side_x, 5: side_y, 7: side_far}[d])

    def end():
        for make in started:
            make().wait_send()
        if not own_first:
            local.wait()

    near_steps = [functools.partial(near, j) for j in range(PIECES)]
    far_steps = [functools.partial(beyond, j) for j in range(half)]
    return [begin, *near_steps, *far_steps, wait_from, end]


def gather_steps(x_ref, out_ref, *sems):
    *steps, wait_from, end = gather_parts(x_ref, out_ref, *sems)

    def finish():
        for d in (1, 3, 5, 7):
            wait_from(d)
        end()

    return [*steps, finish]


def params(collective_id, mib=62):
    return pltpu.CompilerParams(collective_id=collective_id, has_side_effects=True, vmem_limit_bytes=mib << 20)


ANYWHERE = pl.BlockSpec(memory_space=pltpu.HBM)


def move_steps(ins, out_ref, first, rows, sems, local_sem):
    me = lax.axis_index("fsdp")
    count = len(ins)
    c = out_ref.shape[1] // count

    def piece(kind, d):
        peer = other(me, d)
        src = ins[kind].at[pl.ds(first, rows), pl.ds(pl.multiple_of(peer * c, 128), c)]
        dst = out_ref.at[pl.ds(pl.multiple_of(me * rows, 16), rows), pl.ds(kind * c, c)]
        return src, dst, peer

    def moving(kind, d):
        src, dst, peer = piece(kind, d)
        return send(src, dst, sems, d * count + kind, peer)

    def local(kind):
        src, dst, _ = piece(kind, 0)
        return pltpu.make_async_copy(src, dst, local_sem.at[kind])

    def begin():
        for d in (6, 7, 2, 4, 3, 5, 1):
            for kind in range(count):
                moving(kind, d).start()
        for kind in range(count):
            local(kind).start()

    def end():
        for d in ORDER[1:]:
            for kind in range(count):
                there = out_ref.at[pl.ds(pl.multiple_of(other(me, d) * rows, 16), rows), pl.ds(kind * c, c)]
                send(there, there, sems, d * count + kind, other(me, d)).wait_recv()
                moving(kind, d).wait_send()
        for kind in range(count):
            local(kind).wait()

    return [begin, end]


def move_kernel(count, rows, *refs):
    ins, (out_ref, local_sem, *sems) = refs[:count], refs[count:]
    me = lax.axis_index("fsdp")
    greet([other(me, d) for d in range(1, 8)])
    for step in move_steps(ins, out_ref, lax.axis_index("seq") * rows, rows, sems, local_sem):
        step()


def to_columns(weights, first, rows):
    n = lax.axis_size("fsdp")
    cols = weights[0].shape[1]
    weights = [lax.dynamic_slice_in_dim(w, first, rows, 0) for w in weights]
    parts = jnp.stack([w.reshape(rows, n, cols // n) for w in weights], axis=2)
    parts = parts.reshape(rows, n, len(weights) * (cols // n))
    out = lax.all_to_all(parts, "fsdp", split_axis=1, concat_axis=0, tiled=True)
    return out.reshape(n * rows, len(weights) * (cols // n))


def to_columns_in_turns(weights, collective_id):
    n, s = lax.axis_size("fsdp"), lax.axis_size("seq")
    count = len(weights)
    share = weights[0].shape[0] // s
    width = count * (weights[0].shape[1] // n)
    if n != 8:
        part = to_columns(weights, lax.axis_index("seq") * share, share)
    else:
        part = pl.pallas_call(
            functools.partial(move_kernel, count, share),
            in_specs=[ANYWHERE] * count,
            out_specs=ANYWHERE,
            out_shape=jax.ShapeDtypeStruct((n * share, width), bf16),
            scratch_shapes=[pltpu.SemaphoreType.DMA((count,))] + [pltpu.SemaphoreType.DMA((n * count,))] * 2,
            compiler_params=params(collective_id),
            name="move",
        )(*weights)
    part = part.reshape(n, share, width)
    return lax.all_gather(part, "seq", axis=1, tiled=True).reshape(n * share * s, width)


def front_kernel(count, *refs):
    x_ref, gain_ref, *refs = refs
    ins, refs = refs[:count], refs[count:]
    out_ref, gains_ref, w_ref, *sems = refs
    gain_sems, sems = sems[:3], sems[3:]
    move_sems, sems = sems[:3], sems[3:]
    me = lax.axis_index("fsdp")
    greet([other(me, d) for d in range(1, 8)])

    def gain(d):
        return send(gain_ref, gains_ref.at[me], gain_sems[1:], d, other(me, d))

    own = pltpu.make_async_copy(gain_ref, gains_ref.at[me], gain_sems[0])
    own.start()
    for d in range(1, 8):
        gain(d).start()
    first, *steps = gather_steps(x_ref, out_ref, *sems)
    begin, end = move_steps(ins, w_ref, 0, ins[0].shape[0], move_sems[1:], move_sems[0])
    first()
    begin()
    for step in steps:
        step()
    end()
    own.wait()
    for d in range(1, 8):
        there = gains_ref.at[other(me, d)]
        send(there, there, gain_sems[1:], d, other(me, d)).wait_recv()
        gain(d).wait_send()


def front(x, gains, weights, collective_id):
    n = lax.axis_size("fsdp")
    if n != 8:
        return (
            lax.all_gather(x, "fsdp", axis=0),
            lax.all_gather(gains, "fsdp", axis=1, tiled=True),
            to_columns(weights, 0, weights[0].shape[0]),
        )
    count = len(weights)
    kinds, c = gains.shape
    gains = jnp.concatenate([gains, jnp.zeros((8 - kinds, c), f32)])
    rows, cols = weights[0].shape
    sems = pltpu.SemaphoreType.DMA
    x, gains, w = pl.pallas_call(
        functools.partial(front_kernel, count),
        in_specs=[ANYWHERE] * (2 + count),
        out_specs=[ANYWHERE] * 3,
        out_shape=[
            jax.ShapeDtypeStruct((n, *x.shape), x.dtype),
            jax.ShapeDtypeStruct((n, 8, c), f32),
            jax.ShapeDtypeStruct((n * rows, count * (cols // n)), bf16),
        ],
        scratch_shapes=[sems, sems((8,)), sems((8,)), sems((count,)), sems((8 * count,)), sems((8 * count,)), *GATHER_SEMS],
        compiler_params=params(collective_id),
        name="front",
    )(x, gains, *weights)
    return x, gains[:, :kinds].transpose(1, 0, 2).reshape(kinds, n * c), w


def attend_kernel(heads, all_ref, gain_ref, w_ref, dy_ref, starts_ref, blend_ref, *refs):
    h_out, qkv_out, dy_out, mixed_ref, diff_ref, lse_ref, mem_ref, nv_ref, x, w, hid, qkv, load_sems, x_sems, h_sems, q_sems, *sems = refs
    n, tokens, width = all_ref.shape
    rows = tokens // NSEG
    me = lax.axis_index("fsdp")
    weights = pltpu.make_async_copy(w_ref, w, load_sems.at[0])
    weights.start()

    def load(i):
        return pltpu.make_async_copy(all_ref.at[i], x.at[rest(i, 2)], x_sems.at[rest(i, 2)])

    def store(i):
        return pltpu.make_async_copy(hid.at[rest(i, 2)], h_out.at[i], h_sems.at[rest(i, 2)])

    load(0).start()
    greet([other(me, d) for d in (1, 2, 4)])
    begin, near0, near1, near2, near3, far0, far1, wait_from, end = gather_parts(dy_ref, dy_out, *sems)
    begin()
    weights.wait()

    def project(i, _):
        slot = rest(i, 2)
        for at, fn in ((3, near0), (6, near1)):

            @pl.when(i == at)
            def _():
                fn()

        @pl.when(i < n - 1)
        def _():
            load(i + 1).start()

        @pl.when(i > 1)
        def _():
            store(i - 2).wait()

        load(i).wait()
        for r in range(0, tokens, 64):
            here = x[slot, r : r + 64].astype(f32)
            inverse = lax.rsqrt(jnp.mean(here * here, axis=1, keepdims=True) + norm_eps)
            hid[slot, r : r + 64] = (here * inverse * gain_ref[...]).astype(bf16)
        store(i).start()
        made = jnp.dot(hid[slot], w[...], preferred_element_type=f32).astype(bf16)
        qkv[i] = made.reshape(NSEG, rows, made.shape[1])
        return 0

    lax.fori_loop(0, n, project, 0)
    store(n - 2).wait()
    store(n - 1).wait()
    keep = pltpu.make_async_copy(qkv, qkv_out, q_sems.at[0])
    keep.start()
    hooks = {0: near2, heads - 1: near3, heads: far0, 2 * heads - 1: far1}

    def turn(i, _):
        segment, h = lax.div(i, heads), lax.rem(i, heads)
        here = pl.ds(segment, 1)
        for at, fn in hooks.items():

            @pl.when(i == at)
            def _():
                fn()

        attention_head(
            h, heads, segment, starts_ref, blend_ref, qkv.at[:, here], mixed_ref.at[:, here], diff_ref.at[:, here],
            lse_ref.at[:, here], mem_ref, nv_ref,
        )
        return 0

    lax.fori_loop(0, NSEG * heads, turn, 0)
    for d in (1, 3, 5, 7):
        wait_from(d)
    end()
    keep.wait()


def attend(x_all, gain, wqkv, dy, starts, blend, heads, collective_id):
    n, tokens, width = x_all.shape
    rows = tokens // NSEG
    cw = heads * HEAD_DIM
    if n != 8 or heads == 1:
        here = x_all.reshape(n * tokens, width).astype(f32)
        inverse = lax.rsqrt(jnp.mean(here * here, axis=1, keepdims=True) + norm_eps)
        h_in = (here * inverse * gain).astype(bf16)
        qkv = mm(h_in, wqkv).astype(bf16).reshape(n, NSEG, rows, 3 * cw)
        dy = lax.all_gather(dy, "fsdp", axis=0)
        return h_in.reshape(x_all.shape), qkv, dy, *attention(starts, blend, qkv, heads)
    length = n * rows
    sems = pltpu.SemaphoreType.DMA
    inside = pl.BlockSpec(memory_space=pltpu.VMEM)
    pairs = heads * NSEG * length * length // 2
    return pl.pallas_call(
        functools.partial(attend_kernel, heads),
        in_specs=[ANYWHERE, inside, ANYWHERE, ANYWHERE, pl.BlockSpec(memory_space=pltpu.SMEM), inside],
        out_specs=[ANYWHERE] * 3 + [inside] * 5,
        out_shape=[
            jax.ShapeDtypeStruct(x_all.shape, bf16),
            jax.ShapeDtypeStruct((n, NSEG, rows, 3 * cw), bf16),
            jax.ShapeDtypeStruct((n, *dy.shape), bf16),
            *attention_shapes(n, rows, heads),
        ],
        scratch_shapes=[
            pltpu.VMEM((2, tokens, width), bf16),
            pltpu.VMEM(wqkv.shape, bf16),
            pltpu.VMEM((2, tokens, width), bf16),
            pltpu.VMEM((n, NSEG, rows, 3 * cw), bf16),
            *[sems((k,)) for k in (1, 2, 2, 1)],
            *GATHER_SEMS,
        ],
        compiler_params=params(collective_id),
        cost_estimate=pl.CostEstimate(
            flops=pairs * 4 * HEAD_DIM + 6 * n * tokens * width * cw, transcendentals=pairs, bytes_accessed=32 << 20
        ),
        name="attend",
    )(x_all, gain, wqkv, dy, starts, blend)


def quotient(a, b):
    return a // b if isinstance(a, int) else lax.div(a, b)


def rest(a, b):
    return a % b if isinstance(a, int) else lax.rem(a, b)


def xor(index, bits):
    total = 0
    for bit in (1, 2, 4):
        a, b = rest(quotient(index, bit), 2), rest(quotient(bits, bit), 2)
        total = total + bit * (a + b - 2 * a * b)
    return total


def nth_block(i):
    return i + quotient(i, 4) * (2 - 4 * rest(quotient(i, 2), 2))


def mlp_kernel(own_ref, wgu_ref, wd_ref, dy_ref, h_out, inner_out, dgu_out, down_out, out_ref, *refs):
    wgu, wd, h, dy, inner, dgu, mine, side, near, last, weight_sems, dy_sems, h_sems, inner_sems, dgu_sems, *sems = refs
    gather_sems, sems = sems[:15], sems[15:]
    me = lax.axis_index("fsdp")
    sib, xn, yn = flip(me, 1), flip(me, 2), flip(me, 4)
    tokens, width = own_ref.shape
    fw = wd.shape[0]
    begin, near0, near1, near2, near3, far0, far1, wait_from, gather_end = gather_parts(own_ref, h, *gather_sems, own_first=True)
    back = scatter_parts(mine, side, near, last, out_ref, sems)
    loads = [
        pltpu.make_async_copy(wgu_ref, wgu, weight_sems.at[0]),
        pltpu.make_async_copy(wd_ref, wd, weight_sems.at[1]),
    ]
    for load in loads:
        load.start()

    def load_dy(i):
        owner = xor(me, nth_block(i))
        return pltpu.make_async_copy(dy_ref.at[owner], dy.at[owner], dy_sems.at[i])

    for i in range(8):
        load_dy(i).start()
    greet([sib, xn, yn])
    begin()
    back_x, back_far = back["combine"](2), back["combine"](6)
    hooks = {
        (0, 6): [near0],
        (1, 0): [lambda: wait_from(1)],
        (1, 2): [near1],
        (1, 6): [near2],
        (2, 0): [near3],
        (2, 6): [far0],
        (3, 0): [lambda: wait_from(3)],
        (3, 4): [far1],
        (4, 3): [back_x],
        (5, 0): [lambda: wait_from(7)],
        (6, 3): [back_far],
        (7, 0): [lambda: wait_from(5)],
        (7, 4): [lambda: back["onward"](0)],
        (7, 6): [lambda: back["onward"](1)],
    }
    loads[0].wait()
    loads[1].wait()
    tile = fw // 4
    wide = width // 4

    def store(i):
        slot = rest(i, 2)
        return pltpu.make_async_copy(dgu.at[slot], dgu_out.at[xor(me, nth_block(i))], dgu_sems.at[slot])

    def keep(i):
        owner = xor(me, nth_block(i))
        return pltpu.make_async_copy(h.at[owner], h_out.at[owner], h_sems.at[i])

    def keep_inner(i):
        owner = xor(me, nth_block(i))
        return pltpu.make_async_copy(inner.at[owner], inner_out.at[owner], inner_sems.at[i])

    def body(i, _):
        slot = rest(i, 2)
        block = nth_block(i)
        owner = xor(me, block)

        def point(p):
            for (step, at), fns in hooks.items():
                if at == p:

                    @pl.when(i == step)
                    def _():
                        for fn in fns:
                            fn()

        @pl.when(i > 1)
        def _():
            store(i - 2).wait()

        for t in range(4):
            point(t)
            if t == 0:
                keep(i).start()
                load_dy(i).wait()
            left = h[owner]
            cols = slice(t * tile, (t + 1) * tile)
            gate = jnp.dot(left, wgu[:, cols], preferred_element_type=f32)
            up = jnp.dot(left, wgu[:, fw + t * tile : fw + (t + 1) * tile], preferred_element_type=f32)
            back_in = dots(dy[owner], wd[cols], 1, 1)
            sig = jax.nn.sigmoid(gate)
            act = gate * sig
            inner[owner, :, cols] = (act * up).astype(bf16)
            dgu[slot, :, cols] = (back_in * up * (sig * (1.0 + gate * (1.0 - sig)))).astype(bf16)
            dgu[slot, :, fw + t * tile : fw + (t + 1) * tile] = (back_in * act).astype(bf16)
        keep_inner(i).start()
        store(i).start()
        for t in range(4):
            point(4 + t)
            cols = slice(t * wide, (t + 1) * wide)
            mine[block, :, cols] = dots(dgu[slot], wgu[cols], 1, 1).astype(bf16)

        @pl.when(lax.rem(block, 2) == 1)
        def _():
            back["to_core"](block).start()

        return 0

    lax.fori_loop(0, 8, body, 0)
    back["combine"](4)()
    back["onward"](2)
    back["combine"](0)()
    store(6).wait()
    store(7).wait()

    def keep_down(t):
        return pltpu.make_async_copy(dgu.at[t % 2], down_out.at[pl.ds(t * tile, tile)], dgu_sems.at[t % 2])

    for t in range(4):
        if t > 1:
            keep_down(t - 2).wait()
        left = inner[:, :, t * tile : (t + 1) * tile].reshape(8 * tokens, tile)
        for at in range(0, width, wide):
            right = dy[:, :, at : at + wide].reshape(8 * tokens, wide)
            dgu[t % 2, :, at : at + wide] = dots(left, right, 0, 0).astype(bf16)
        keep_down(t).start()
    back["finish"]()
    keep_down(2).wait()
    keep_down(3).wait()
    for i in range(8):
        keep(i).wait()
        keep_inner(i).wait()
    gather_end()


def scatter_parts(mine, side, near, last, out_ref, sems):
    me = lax.axis_index("fsdp")
    sib, xn, yn = flip(me, 1), flip(me, 2), flip(me, 4)
    rows = out_ref.shape[0] // PIECES
    half = PIECES // 2
    core, sems = sems[:2], sems[2:]
    hop = {"xf": sems[0:2], "xo": sems[2:4], "yf": sems[4:6], "yo": sems[6:8], "last": sems[8:10]}

    def to_core(d):
        kind = quotient(d, 2)
        return send(mine.at[d], side.at[kind], core, kind, sib)

    def span(c):
        return pl.ds(c * rows, rows)

    def go(copy):
        copy.start()

    def travel(d, c):
        if d == 6:
            return send(mine.at[6, span(c)], near.at[0, span(c)], hop["xf" if c < half else "yf"], c, xn if c < half else yn)
        if d == 2:
            return send(mine.at[2, span(c)], near.at[1, span(c)], hop["xo"], c, xn)
        return send(mine.at[4, span(c)], near.at[1, span(c)], hop["yo"], c, yn)

    def leaves(d, c):
        return d == 6 or (d == 2 and c < half) or (d == 4 and c >= half)

    def step_on(c):
        return send(mine.at[4 if c < half else 2, span(c)], last.at[span(c)], hop["last"], c, yn if c < half else xn)

    def add(d, c, ref):
        total = mine.at[d]

        def body(i, _):
            here = pl.ds(pl.multiple_of(c * rows + i * 16, 16), 16)
            total[here] = (total[here].astype(f32) + ref[here].astype(f32)).astype(bf16)
            return 0

        lax.fori_loop(0, rows // 16, body, 0)

    def combine(d):
        def run():
            send(side.at[d // 2], side.at[d // 2], core, d // 2, sib).wait_recv()
            for c in range(PIECES):
                add(d, c, side.at[d // 2])
                if leaves(d, c):
                    go(travel(d, c))

        return run

    def onward(which):
        for c in range(half) if which == 2 else [half + which]:
            d = 4 if c < half else 2
            send(near.at[0, span(c)], near.at[0, span(c)], hop["xf" if c < half else "yf"], c, xn).wait_recv()
            add(d, c, near.at[0])
            go(step_on(c))

    def finish():
        total, came = mine.at[0], near.at[1]
        for j in range(half):
            for c in (j + half, j):
                send(near.at[1, span(c)], near.at[1, span(c)], hop["xo" if c < half else "yo"], c, xn).wait_recv()
                send(last.at[span(c)], last.at[span(c)], hop["last"], c, xn).wait_recv()

                def body(i, _):
                    here = pl.ds(pl.multiple_of(c * rows + i * 16, 16), 16)
                    out_ref[here] = total[here].astype(f32) + came[here].astype(f32) + last[here].astype(f32)
                    return 0

                lax.fori_loop(0, rows // 16, body, 0)
        for d in (1, 3, 5, 7):
            to_core(d).wait_send()
        for d in (2, 4, 6):
            for c in range(PIECES):
                if leaves(d, c):
                    travel(d, c).wait_send()
        for c in range(PIECES):
            step_on(c).wait_send()

    return {"to_core": to_core, "combine": combine, "onward": onward, "finish": finish}


SCATTER_SEMS = [pltpu.SemaphoreType.DMA((4,))] * 2 + [pltpu.SemaphoreType.DMA((PIECES,))] * 10


def scatter_boxes(rows, columns):
    return [pltpu.VMEM((k, rows, columns), bf16) for k in (8, 4, 2)] + [pltpu.VMEM((rows, columns), bf16)]


def mlp(h_own, wgu, w_down, dy, collective_id):
    n, rows, width = dy.shape
    fw = w_down.shape[0]
    if n != 8:
        h = lax.all_gather(h_own, "fsdp", axis=0)
        gate_up = mm(h.reshape(n * rows, width), wgu)
        gate, up = gate_up[:, :fw], gate_up[:, fw:]
        sig = jax.nn.sigmoid(gate)
        inner = (gate * sig * up).astype(bf16)
        back_in = mm_t(dy.reshape(n * rows, width), w_down)
        d_gate = (back_in * up * (sig * (1.0 + gate * (1.0 - sig)))).astype(bf16)
        d_gu = jnp.concatenate([d_gate, (back_in * (gate * sig)).astype(bf16)], axis=1)
        d_h = lax.psum_scatter(mm_t(d_gu, wgu).astype(bf16), "fsdp", scatter_dimension=0, tiled=True).astype(f32)
        down = t_mm(inner, dy.reshape(n * rows, width)).astype(bf16)
        return h, inner.reshape(n, rows, fw), d_gu.reshape(n, rows, 2 * fw), down, d_h
    sems = pltpu.SemaphoreType.DMA
    return pl.pallas_call(
        mlp_kernel,
        in_specs=[ANYWHERE] * 4,
        out_specs=[ANYWHERE] * 4 + [pl.BlockSpec(memory_space=pltpu.VMEM)],
        out_shape=[
            jax.ShapeDtypeStruct((n, rows, width), bf16),
            jax.ShapeDtypeStruct((n, rows, fw), bf16),
            jax.ShapeDtypeStruct((n, rows, 2 * fw), bf16),
            jax.ShapeDtypeStruct((fw, width), bf16),
            jax.ShapeDtypeStruct((rows, width), f32),
        ],
        scratch_shapes=[
            pltpu.VMEM(wgu.shape, bf16),
            pltpu.VMEM(w_down.shape, bf16),
            pltpu.VMEM((n, rows, width), bf16),
            pltpu.VMEM((n, rows, width), bf16),
            pltpu.VMEM((n, rows, fw), bf16),
            pltpu.VMEM((2, rows, 2 * fw), bf16),
            *scatter_boxes(rows, width),
            *[sems((k,)) for k in (2, 8, 8, 8, 2)],
            *GATHER_SEMS,
            *SCATTER_SEMS,
        ],
        compiler_params=params(collective_id, 60),
        cost_estimate=pl.CostEstimate(flops=10 * n * rows * width * fw, transcendentals=n * rows * fw, bytes_accessed=64 << 20),
        name="mlp",
    )(h_own, wgu, w_down, dy)


def product_tiles(lhs, rhs, box, out_ref, sems, over_rows, hooks):
    columns = rhs.shape[1]
    count = out_ref.shape[0] // 256

    def rows(i):
        return pl.ds(pl.multiple_of(i * 256, 256), 256)

    def store(i):
        return pltpu.make_async_copy(
            box.at[rest(i, 2), :, pl.ds(0, columns)], out_ref.at[rows(i)], sems.at[rest(i, 2)]
        )

    def body(i, _):
        for step, fns in hooks.items():

            @pl.when(i == step)
            def _():
                for fn in fns:
                    fn()

        @pl.when(i > 1)
        def _():
            store(i - 2).wait()

        left = lhs[:, rows(i)] if over_rows else lhs[rows(i)]
        for at in range(0, columns, 512):
            here = slice(at, min(at + 512, columns))
            box[rest(i, 2), :, here] = dots(left, rhs[:, here], 0 if over_rows else 1, 0).astype(bf16)
        store(i).start()
        return 0

    lax.fori_loop(0, count, body, 0)
    for i in range(max(0, count - 2), count):
        store(i).wait()


def line_places():
    place = lax.axis_index("seq")
    inward = jnp.where(place < 2, 1, 2)
    return (place == 0) | (place == 3), inward, jnp.where(place < 2, 0, 3), 3 - inward


def greet_line(bits):
    me = lax.axis_index("fsdp")
    is_end, inward, outward, opposite = line_places()
    barrier = pltpu.get_barrier_semaphore()
    for d in bits:
        pl.semaphore_signal(barrier, inc=1, device_id={"fsdp": other(me, d)}, device_id_type=pl.DeviceIdType.MESH)

    @pl.when(is_end)
    def _():
        pl.semaphore_signal(barrier, inc=1, device_id={"seq": inward}, device_id_type=pl.DeviceIdType.MESH)
        pl.semaphore_wait(barrier, len(bits) + 1)

    @pl.when(jnp.logical_not(is_end))
    def _():
        for peer in (outward, opposite):
            pl.semaphore_signal(barrier, inc=1, device_id={"seq": peer}, device_id_type=pl.DeviceIdType.MESH)
        pl.semaphore_wait(barrier, len(bits) + 2)


HEAD_STEPS = 12


def head_rows(rows):
    return rows * 3 // 8


def head_line(own, came, half, crossed, total, sems):
    is_end, inward, outward, opposite = line_places()
    rows = own.shape[0] // HEAD_STEPS
    go_in, cross, back = sems[0:2], sems[2:4], sems[4:6]

    def at(ref, c):
        return ref.at[pl.ds(c * rows, rows)]

    def add(dst, left, right):
        def body(i, _):
            here = pl.ds(pl.multiple_of(i * 16, 16), 16)
            dst[here] = (left[here].astype(f32) + right[here].astype(f32)).astype(bf16)
            return 0

        lax.fori_loop(0, rows // 16, body, 0)

    def first(c):
        return link(at(own, c), at(came, c), go_in, c, "seq", inward)

    def second(c):
        return link(at(half, c), at(crossed, c), cross, c, "seq", opposite)

    def third(c):
        return link(at(total, c), at(total, c), back, c, "seq", outward)

    def begin():
        @pl.when(is_end)
        def _():
            for c in range(HEAD_STEPS):
                first(c).start()

    def step(j):
        def run():
            @pl.when(jnp.logical_not(is_end))
            def _():
                if j < HEAD_STEPS:
                    link(at(came, j), at(came, j), go_in, j, "seq", outward).wait_recv()
                    add(at(half, j), at(own, j), at(came, j))
                    second(j).start()
                if j >= 2:
                    c = j - 2
                    link(at(crossed, c), at(crossed, c), cross, c, "seq", opposite).wait_recv()
                    add(at(total, c), at(half, c), at(crossed, c))
                    third(c).start()

        return run

    def end():
        @pl.when(is_end)
        def _():
            for c in range(HEAD_STEPS):
                link(at(total, c), at(total, c), back, c, "seq", inward).wait_recv()
                first(c).wait_send()

        @pl.when(jnp.logical_not(is_end))
        def _():
            for c in range(HEAD_STEPS):
                second(c).wait_send()
                third(c).wait_send()

    return begin, [step(j) for j in range(HEAD_STEPS + 2)], end


def gather_products_kernel(x_ref, h_ref, dgu_ref, inner_ref, wd_ref, down_ref, out_ref, gu_ref, mlp_ref, head_ref, h, dgu, inner, wd, box, *refs):
    (own, came, half, crossed, total), refs = refs[:5], refs[5:]
    load_sems, sems, line_sems, refs = refs[0], refs[1], refs[2:8], refs[8:]
    line_begin, steps, line_end = head_line(own, came, half, crossed, total, line_sems)
    head = pltpu.make_async_copy(down_ref.at[pl.ds(0, own.shape[0])], own, load_sems.at[4])
    head.start()
    loads = [
        pltpu.make_async_copy(src, dst, load_sems.at[i])
        for i, (src, dst) in enumerate(((h_ref, h), (dgu_ref, dgu), (inner_ref, inner), (wd_ref, wd)))
    ]
    greet_line((1, 2, 4))
    begin, near0, near1, near2, near3, far0, far1, wait_from, end = gather_parts(x_ref, out_ref, *refs)
    begin()
    head.wait()
    line_begin()
    for load in loads:
        load.start()
    loads[0].wait()
    loads[1].wait()
    hooks = {i: [steps[i - 1]] for i in range(1, 8)}
    for i, fn in ((1, near0), (3, near1), (5, near2), (7, near3)):
        hooks[i].append(fn)
    product_tiles(h, dgu, box, gu_ref, sems, True, hooks)
    loads[2].wait()
    loads[3].wait()
    hooks = {0: [steps[7]], 2: [steps[8]], 3: [far0], 4: [steps[9]], 6: [steps[10]], 7: [far1]}
    product_tiles(inner, wd, box, mlp_ref, sems, False, hooks)
    for step in steps[11:]:
        step()
    for d in (1, 3, 5, 7):
        wait_from(d)
    line_end()
    out = pltpu.make_async_copy(total, head_ref, load_sems.at[4])
    out.start()
    end()
    out.wait()


def gather_products(x, h, dgu, inner, w_down, down, collective_id):
    n = lax.axis_size("fsdp")
    ahead = head_rows(down.shape[0])
    if n != 8 or lax.axis_size("seq") != 4:
        head = lax.psum(down[:ahead], "seq")
        return lax.all_gather(x, "fsdp", axis=0), t_mm(h, dgu).astype(bf16), mm(inner, w_down).astype(bf16), head
    total, width = h.shape
    sems = pltpu.SemaphoreType.DMA
    return pl.pallas_call(
        gather_products_kernel,
        in_specs=[ANYWHERE] * 6,
        out_specs=[ANYWHERE] * 4,
        out_shape=[
            jax.ShapeDtypeStruct((n, *x.shape), bf16),
            jax.ShapeDtypeStruct((width, dgu.shape[1]), bf16),
            jax.ShapeDtypeStruct((total, width), bf16),
            jax.ShapeDtypeStruct((ahead, width), bf16),
        ],
        scratch_shapes=[pltpu.VMEM(a.shape, bf16) for a in (h, dgu, inner, w_down)]
        + [pltpu.VMEM((2, 256, max(width, dgu.shape[1])), bf16), *[pltpu.VMEM((ahead, width), bf16)] * 5]
        + [sems((5,)), sems((2,)), *[sems((HEAD_STEPS,))] * 6, *GATHER_SEMS],
        compiler_params=params(collective_id, 56),
        cost_estimate=pl.CostEstimate(
            flops=2 * total * width * (inner.shape[1] + dgu.shape[1]), transcendentals=0, bytes_accessed=48 << 20
        ),
        name="gather_products",
    )(x, h, dgu, inner, w_down, down)


def block_products(me, lhs, rhs, mine, turned, back, block):
    wide = mine.shape[2] // 4
    left = lhs[xor(me, block)].reshape(-1, lhs.shape[-1])
    for t in range(4):
        cols = slice(t * wide, (t + 1) * wide)
        made = dots(left, rhs[cols], 1, 1) if turned else dots(left, rhs[:, cols], 1, 0)
        mine[block, :, cols] = made.astype(bf16)
    if block % 2 == 1:
        back["to_core"](block).start()


def product_scatter_kernel(lhs_ref, rhs_ref, out_ref, lhs, rhs, mine, side, near, last, load_sems, *sems):
    me = lax.axis_index("fsdp")
    loads = [pltpu.make_async_copy(lhs_ref, lhs, load_sems.at[0]), pltpu.make_async_copy(rhs_ref, rhs, load_sems.at[1])]
    for load in loads:
        load.start()
    greet([other(me, d) for d in (1, 2, 4)])
    back = scatter_parts(mine, side, near, last, out_ref, sems)
    for load in loads:
        load.wait()
    for block in (6, 7, 4, 5, 2, 3, 0, 1):
        block_products(me, lhs, rhs, mine, False, back, block)
        if block in (4, 2, 0):
            back["combine"](block + 2)()
    back["combine"](0)()
    for which in range(3):
        back["onward"](which)
    back["finish"]()


def product_scatter(lhs, rhs, collective_id):
    n, rows, depth = lhs.shape
    width = rhs.shape[1]
    if n != 8:
        made = mm(lhs.reshape(n * rows, depth), rhs).astype(bf16)
        return lax.psum_scatter(made, "fsdp", scatter_dimension=0, tiled=True).astype(f32)
    sems = pltpu.SemaphoreType.DMA
    return pl.pallas_call(
        product_scatter_kernel,
        in_specs=[ANYWHERE] * 2,
        out_specs=pl.BlockSpec(memory_space=pltpu.VMEM),
        out_shape=jax.ShapeDtypeStruct((rows, width), f32),
        scratch_shapes=[pltpu.VMEM(lhs.shape, bf16), pltpu.VMEM(rhs.shape, bf16), *scatter_boxes(rows, width), sems((2,)), *SCATTER_SEMS],
        compiler_params=params(collective_id),
        cost_estimate=pl.CostEstimate(flops=2 * n * rows * depth * width, transcendentals=0, bytes_accessed=8 << 20),
        name="product_scatter",
    )(lhs, rhs)


SLOTS = 6
LAG = 3


def chunks_of(gu_rows, out_rows, qkv_rows, down_rows):
    out = [(3, None, r, 64) for r in range(head_rows(down_rows), down_rows, 64)]
    out += [(0, d, r, 64) for d in ORDER for r in range(0, gu_rows, 64)]
    out += [(1, None, r, 64) for r in range(0, out_rows, 64)]
    return out + [(2, d, r, 128) for d in ORDER for r in range(0, qkv_rows, 128)]


def finish_kernel(*refs):
    starts_ref, blend_ref, small_ref, x_ref, inv_ref, gain_ref, dres_ref, *refs = refs
    (gu_ref, wqkv_ref, mixed_ref, dattn_ref, hin_ref, wout_ref, qkv_ref, diff_ref, lse_ref, mem_ref, nv_ref, down_ref), refs = refs[:12], refs[12:]
    small_out, dx_ref, part_out, part_qkv, *refs = refs
    ins = [gu_ref, part_out, part_qkv, down_ref]
    kinds = 4
    outs, refs = refs[:kinds], refs[kinds:]
    first, refs = refs[:kinds], refs[kinds:]
    second, refs = refs[:kinds], refs[kinds:]
    come, refs = {0: refs[0], 2: refs[1]}, refs[2:]
    (wqkv, mixed, wout, qkv, diff, lse, mem, nv, dqkv, dmix, bias, tiles), refs = refs[:12], refs[12:]
    back_refs, refs = refs[:4], refs[4:]
    (big, side, near, last), refs = refs[:4], refs[4:]
    dattn = mine = hin = big
    (fetch_sems, box_sems), refs = refs[:2], refs[2:]
    scatter_sems, refs = refs[: len(SCATTER_SEMS)], refs[len(SCATTER_SEMS) :]
    small_work, small_come, small_sum, small_in, small_back, *refs = refs
    small_move, small_line_sems, refs = refs[0:2], refs[2:4], refs[4:]
    g_buf, a_buf, t_buf, b_buf, u_buf, loads, stores, *sems = refs
    move = {0: sems[0:2], 2: sems[2:4]}
    sems = sems[4:]
    go_in, cross, back = sems[0:2], sems[2:4], sems[4:6]
    heads = mem.shape[0]
    seg_rows = qkv.shape[2]
    me, place = lax.axis_index("fsdp"), lax.axis_index("seq")
    is_end = (place == 0) | (place == 3)
    chunks = chunks_of(gu_ref.shape[1], part_out.shape[0], part_qkv.shape[1], down_ref.shape[0])
    inward = jnp.where(place < 2, 1, 2)
    outward = jnp.where(place < 2, 0, 3)
    opposite = 3 - inward
    barrier = pltpu.get_barrier_semaphore()
    for d in range(1, 8):
        pl.semaphore_signal(barrier, inc=1, device_id={"fsdp": other(me, d)}, device_id_type=pl.DeviceIdType.MESH)

    @pl.when(is_end)
    def _():
        pl.semaphore_signal(barrier, inc=1, device_id={"seq": inward}, device_id_type=pl.DeviceIdType.MESH)
        pl.semaphore_wait(barrier, 8)

    @pl.when(jnp.logical_not(is_end))
    def _():
        for peer in (outward, opposite):
            pl.semaphore_signal(barrier, inc=1, device_id={"seq": peer}, device_id_type=pl.DeviceIdType.MESH)
        pl.semaphore_wait(barrier, 9)

    def moving(t, d):
        return link(ins[t].at[other(me, d)], come[t].at[me], move[t], d, "fsdp", other(me, d))

    def arrival(t, d):
        owner = other(me, d)
        return link(come[t].at[owner], come[t].at[owner], move[t], d, "fsdp", owner)

    def small_moving(d):
        return link(small_work.at[other(me, d)], small_come.at[me], small_move, d, "fsdp", other(me, d))

    def small_arrival(d):
        there = small_come.at[other(me, d)]
        return link(there, there, small_move, d, "fsdp", other(me, d))

    def small_hop(src, dst, slot, peer):
        return link(src, dst, small_line_sems, slot, "seq", peer)

    plan = [(t, d) for t in (0, 2) for d in ORDER[1:]]
    begun = []

    def feed(count):
        while plan and count:
            t, d = plan.pop(0)
            moving(t, d).start()
            begun.append((t, d))
            count -= 1

    def view(refs, k):
        t, d, r, rows = chunks[k]
        if d is None:
            return refs[t].at[pl.ds(r, rows)]
        return refs[t].at[other(me, d), pl.ds(r, rows)]

    def windows(k):
        t, d, r, rows = chunks[k]
        buf = box(u_buf, k, SLOTS)
        if d is None:
            return [(buf, outs[t].at[pl.ds(r, rows)])]
        kinds = outs[t].shape[0]
        c = ins[t].shape[2] // kinds
        columns = pl.ds(pl.multiple_of(other(me, d) * c, 128), c)
        return [(buf.at[:, pl.ds(i * c, c)], outs[t].at[i, pl.ds(r, rows), columns]) for i in range(kinds)]

    def source(k):
        t, d, r, rows = chunks[k]
        if d is None:
            return ins[t].at[pl.ds(r, rows)]
        if d == 0:
            return ins[t].at[me, pl.ds(r, rows)]
        return come[t].at[other(me, d), pl.ds(r, rows)]

    def await_source(k):
        t, d, r, rows = chunks[k]
        if d and r == 0:
            arrival(t, d).wait_recv()

    def box(buf, k, depth):
        t, d, r, rows = chunks[k]
        return buf.at[k % depth, pl.ds(0, rows), pl.ds(0, ins[t].shape[-1])]

    def add(dst, left, right):
        rows = dst.shape[0]

        def body(i, _):
            here = pl.ds(pl.multiple_of(i * 16, 16), 16)
            dst[here] = (left[here].astype(f32) + right[here].astype(f32)).astype(bf16)
            return 0

        lax.fori_loop(0, rows // 16, body, 0)

    def end_send(k):
        return link(source(k), view(first, k), go_in, k, "seq", inward)

    def mid_cross(k):
        return link(box(t_buf, k, SLOTS), view(second, k), cross, k, "seq", opposite)

    def mid_back(k):
        return [link(src, dst, back, k, "seq", outward) for src, dst in windows(k)]

    def store(k):
        return [pltpu.make_async_copy(src, dst, stores.at[k % SLOTS]) for src, dst in windows(k)]

    def all_back(k):
        return link(box(u_buf, k, SLOTS), box(u_buf, k, SLOTS), back, k, "seq", outward)

    def all_stored(k):
        return pltpu.make_async_copy(box(u_buf, k, SLOTS), box(u_buf, k, SLOTS), stores.at[k % SLOTS])

    def finish(k):
        link(view(second, k), view(second, k), cross, k, "seq", opposite).wait_recv()
        load = pltpu.make_async_copy(view(second, k), box(b_buf, k, 2), loads.at[2])
        load.start()
        if k >= SLOTS:
            all_back(k - SLOTS).wait_send()
            all_stored(k - SLOTS).wait()
        load.wait()
        add(box(u_buf, k, SLOTS), box(t_buf, k, SLOTS), box(b_buf, k, 2))
        for copy in mid_back(k) + store(k):
            copy.start()

    count = len(chunks)
    way = scatter_parts(mine, side, near, last, dx_ref, scatter_sems)
    pairs = (
        (dattn_ref, dattn), (wout_ref, wout), (mixed_ref, mixed), (qkv_ref, qkv), (diff_ref, diff), (lse_ref, lse),
        (mem_ref, mem), (nv_ref, nv), (wqkv_ref, wqkv), (hin_ref, hin),
    )
    fetches = [pltpu.make_async_copy(src, dst, fetch_sems.at[i]) for i, (src, dst) in enumerate(pairs)]

    def d_mixed():
        bias[...] = jnp.zeros_like(bias)
        for ref in back_refs[2:]:
            ref[...] = jnp.zeros_like(ref)

        def body(i, _):
            dmix[i] = dots(dattn[i], wout[...], 1, 1).reshape(dmix.shape[1:])
            return 0

        lax.fori_loop(0, 8, body, 0)

    def attention_part(segment, i):
        def run():
            here = slice(segment, segment + 1)

            def body(h, _):
                back_block(
                    i, h, heads, segment, starts_ref, blend_ref, qkv.at[:, here], dmix.at[:, here], diff.at[:, here],
                    lse.at[:, here], mem, nv, dqkv.at[:, here], bias, *back_refs,
                )
                return 0

            lax.fori_loop(0, heads, body, 0)

        return run

    def attention_end(segment):
        def run():
            here = slice(segment, segment + 1)

            def body(h, _):
                back_end(h, heads, segment, starts_ref, qkv.at[:, here], dqkv.at[:, here], *back_refs)
                return 0

            lax.fori_loop(0, heads, body, 0)

        return run

    def products(block):
        return lambda: block_products(me, dqkv, wqkv, mine, True, way, block)

    def fetched(*which):
        def run():
            for i in which:
                fetches[i].wait()

        return run

    def put(j, columns):
        src = tiles.at[j % 2, :, pl.ds(0, columns)]
        return pltpu.make_async_copy(src, part_out if j == 0 else part_qkv.at[j - 1], box_sems.at[j % 2])

    def out_tile():
        for at in range(0, tiles.shape[2], 512):
            right = dattn[:, :, at : at + 512].reshape(-1, 512)
            tiles[0, :, at : at + 512] = dots(mixed[...].reshape(-1, mixed.shape[2]), right, 0, 0).astype(bf16)
        put(0, tiles.shape[2]).start()

    columns = dqkv.shape[3]

    def qkv_tile(j):
        def run():
            if j >= 2:
                put(j - 2, tiles.shape[2] if j == 2 else columns).wait()
            rows = part_qkv.shape[1]
            left = hin[:, :, (j - 1) * rows : j * rows].reshape(-1, rows)
            for at in range(0, columns, 256):
                right = dqkv[:, :, :, at : at + 256].reshape(-1, 256)
                tiles[j % 2, :, at : at + 256] = dots(left, right, 0, 0).astype(bf16)
            put(j, columns).start()

        return run

    def all_put():
        put(7, columns).wait()
        put(8, columns).wait()

    def small_start():
        small_work[...] = small_ref[...]
        c = small_work.shape[2]
        inverse = inv_ref[...]
        for j in range(8):
            here = slice(j * c, (j + 1) * c)
            normed = x_ref[:, here].astype(f32) * inverse
            small_work[j, 0:1] = jnp.sum(normed * dx_ref[:, here], axis=0, keepdims=True)
        lanes = lax.broadcasted_iota(jnp.int32, (1, c), 1)
        row = jnp.zeros((1, c), f32)
        for h in range(heads):
            cols = slice(h * HEAD_DIM, (h + 1) * HEAD_DIM)
            gate = blend_ref[:, cols]
            row = row + jnp.where(lanes == h, jnp.sum(bias[:, cols] * gate * (1.0 - gate), axis=1, keepdims=True), 0.0)
        small_work[me, 2:3] = row
        for d in range(1, 8):
            small_moving(d).start()
        small_come[me] = small_work[me]
        for r in range(0, dx_ref.shape[0], 64):
            here = slice(r, r + 64)
            normed = x_ref[here].astype(f32) * inv_ref[here]
            t = dx_ref[here] * gain_ref[...]
            dx_ref[here] = dres_ref[here] + norm_back(t, normed, inv_ref[here])

    def small_first():
        for d in range(1, 8):
            small_arrival(d).wait_recv()
        small_sum[...] = jnp.sum(small_come[...], axis=0)

        @pl.when(is_end)
        def _():
            small_hop(small_sum, small_in, 0, inward).start()

        @pl.when(jnp.logical_not(is_end))
        def _():
            small_hop(small_in, small_in, 0, outward).wait_recv()
            small_sum[...] = small_sum[...] + small_in[...]
            small_hop(small_sum, small_back, 1, opposite).start()

    blocks = 8 * qkv.shape[2] // 256
    work = {
        0: [fetched(0, 1), d_mixed],
        1: [fetched(2, 3, 4, 5, 6, 7, 8)],
        10: [products(4), products(5)],
        11: [way["combine"](6), products(2), products(3)],
        12: [way["combine"](4), products(0), products(1)],
        13: [way["combine"](2)],
        14: [way["combine"](0)],
        19: [lambda: way["onward"](0)],
        20: [lambda: way["onward"](1)],
        21: [lambda: way["onward"](2)],
        26: [way["finish"], fetches[9].start],
        27: [small_start],
        28: [fetched(9), qkv_tile(1), qkv_tile(2)],
        29: [qkv_tile(3), qkv_tile(4)],
        30: [qkv_tile(5), qkv_tile(6)],
        31: [qkv_tile(7), qkv_tile(8)],
        32: [all_put],
        38: [small_first],
    }
    for i in range(4):
        work[1 + i] = work.get(1 + i, []) + [attention_part(1, i)]
        work[5 + i] = ([attention_end(1)] if i == 0 else []) + [attention_part(0, i)]
    work[9] = [attention_end(0), out_tile, products(6), products(7)]
    for fetch in fetches[:9]:
        fetch.start()
    feed(3)
    ahead = 4
    for k in range(count):
        if k % 4 == 3 and k < 16:
            feed(1)
        if k >= 33:
            feed(2)

        @pl.when(is_end)
        def _():
            for j in range(ahead + 1) if k == 0 else [k + ahead]:
                if j < count:
                    await_source(j)
                    end_send(j).start()

        @pl.when(jnp.logical_not(is_end))
        def _():
            await_source(k)
            own = pltpu.make_async_copy(source(k), box(g_buf, k, 2), loads.at[0])
            own.start()
            link(view(first, k), view(first, k), go_in, k, "seq", outward).wait_recv()
            got = pltpu.make_async_copy(view(first, k), box(a_buf, k, 2), loads.at[1])
            got.start()
            if k >= SLOTS:
                mid_cross(k - SLOTS).wait_send()
            own.wait()
            got.wait()
            add(box(t_buf, k, SLOTS), box(g_buf, k, 2), box(a_buf, k, 2))
            mid_cross(k).start()
            if k >= LAG:
                finish(k - LAG)

        for fn in work.get(k, ()):
            fn()

    @pl.when(jnp.logical_not(is_end))
    def _():
        small_hop(small_back, small_back, 1, opposite).wait_recv()
        small_hop(small_sum, small_back, 1, opposite).wait_send()
        small_out[...] = small_sum[...] + small_back[...]
        small_hop(small_out, small_out, 2, outward).start()

    @pl.when(is_end)
    def _():
        small_hop(small_out, small_out, 2, inward).wait_recv()
        small_hop(small_sum, small_in, 0, inward).wait_send()
        for k in range(count):
            all_back(k).wait_recv()
            end_send(k).wait_send()

    @pl.when(jnp.logical_not(is_end))
    def _():
        for k in range(count - LAG, count):
            finish(k)
        small_hop(small_out, small_out, 2, outward).wait_send()
        for k in range(max(0, count - SLOTS), count):
            mid_cross(k).wait_send()
            all_back(k).wait_send()
            all_stored(k).wait()

    for t, d in begun:
        moving(t, d).wait_send()
    for d in range(1, 8):
        small_moving(d).wait_send()


def finish(starts, blend, small, x, inv, gain, dres, gu, wqkv, mixed, dattn, hin, wout, qkv, diff, lse, mem, nv, down, collective_id):
    n, per, _ = gu.shape
    rows, width = x.shape
    heads = mem.shape[0]
    cw = heads * HEAD_DIM
    if lax.axis_size("seq") != 4 or n != 8 or heads == 1:
        total = n * rows
        dmix = mm_t(dattn.reshape(total, width), wout).reshape(diff.shape)
        dqkv, bias = attention_back(starts, blend, qkv, dmix, diff, lse, mem, nv, heads)
        dqkv = dqkv.reshape(total, 3 * cw)
        dhin = lax.psum_scatter(mm_t(dqkv, wqkv).astype(bf16), "fsdp", scatter_dimension=0, tiled=True).astype(f32)
        normed = x.astype(f32) * inv
        small = small.at[:, 0].set(jnp.sum(normed * dhin, axis=0).reshape(n, per))
        bias = jnp.sum((bias * blend * (1.0 - blend)).reshape(heads, HEAD_DIM), axis=1)
        own = (jnp.arange(n) == lax.axis_index("fsdp"))[:, None]
        small = small.at[:, 2].set(jnp.where(own, jnp.pad(bias, (0, per - heads))[None], 0.0))
        dx = dres + norm_back(dhin * gain, normed, inv)
        out = lax.psum(t_mm(mixed.reshape(total, cw), dattn.reshape(total, width)).astype(bf16), "seq")
        made = t_mm(hin.reshape(total, width), dqkv).astype(bf16).reshape(n, per, 3 * cw)
        moved = []
        for y, count in ((gu, 2), (made, 3)):
            c = y.shape[2] // count
            y = lax.psum(lax.all_to_all(y, "fsdp", split_axis=0, concat_axis=0, tiled=True), "seq")
            moved.append(y.reshape(n, per, count, c).transpose(2, 1, 0, 3).reshape(count, per, n * c))
        small = lax.psum(lax.psum_scatter(small, "fsdp", scatter_dimension=0), "seq")
        return small, dx, out, *moved, lax.psum(down, "seq")
    made = jax.ShapeDtypeStruct((n, per, 3 * cw), bf16)
    out = jax.ShapeDtypeStruct((cw, width), bf16)
    gu_shape = jax.ShapeDtypeStruct(gu.shape, bf16)
    count = len(chunks_of(per, cw, per, down.shape[0]))
    down_shape = jax.ShapeDtypeStruct(down.shape, bf16)
    inside = pl.BlockSpec(memory_space=pltpu.VMEM)
    sems = pltpu.SemaphoreType.DMA
    small_sum, dx, _, _, sum_gu, sum_out, sum_qkv, sum_down, *_ = pl.pallas_call(
        finish_kernel,
        in_specs=[pl.BlockSpec(memory_space=pltpu.SMEM)] + [inside] * 6 + [ANYWHERE] * 12,
        out_specs=[inside] * 2 + [ANYWHERE] * 16,
        out_shape=[
            jax.ShapeDtypeStruct(small.shape[1:], f32),
            jax.ShapeDtypeStruct((rows, width), f32),
            out,
            made,
            jax.ShapeDtypeStruct((2, per, gu.shape[2] // 2 * n), bf16),
            out,
            jax.ShapeDtypeStruct((3, per, cw * n), bf16),
            down_shape,
            *[gu_shape, out, made, down_shape] * 2,
            gu_shape,
            made,
        ],
        scratch_shapes=[pltpu.VMEM(y.shape, y.dtype) for y in (wqkv, mixed, wout, qkv, diff, lse, mem, nv)]
        + [pltpu.VMEM(qkv.shape, bf16), pltpu.VMEM(diff.shape, f32), pltpu.VMEM((1, cw), f32)]
        + [pltpu.VMEM((2, per, width), bf16)]
        + back_boxes(n, qkv.shape[2], heads)
        + scatter_boxes(rows, width)
        + [sems((10,)), sems((2,)), *SCATTER_SEMS]
        + [pltpu.VMEM(small.shape, f32)] * 2
        + [pltpu.VMEM(small.shape[1:], f32)] * 3
        + [sems((8,)), sems((8,)), sems((3,)), sems((3,))]
        + [pltpu.VMEM((depth, 128, gu.shape[2]), bf16) for depth in (2, 2, SLOTS, 2, SLOTS)]
        + [sems((3,)), sems((SLOTS,))]
        + [sems((8,))] * 4
        + [sems((count,))] * 6,
        compiler_params=params(collective_id, 62),
        name="finish",
    )(starts, blend, small, x, inv, gain, dres, gu, wqkv, mixed, dattn, hin, wout, qkv, diff, lse, mem, nv, down)
    return small_sum, dx, sum_out, sum_gu, sum_qkv, sum_down


def shards(
    tokens,
    doc_starts,
    norm_in,
    w_query,
    w_key,
    w_value,
    mix_bias,
    w_out,
    norm_mid,
    w_gate,
    w_up,
    w_down,
    cotangent,
):
    rows = tokens.shape[2]
    width = tokens.shape[3]
    n = lax.axis_size("fsdp")
    s = lax.axis_size("seq")
    own = NSEG * rows
    total = n * own
    seg_len = rows * n
    heads = HEADS // n
    cw = heads * HEAD_DIM
    fw = w_gate.shape[1] // n

    wgu = to_columns_in_turns([w_gate, w_up], 7)
    flat_in = tokens.reshape(own, width)
    all_in, gains, wqkv = front(flat_in, jnp.stack([norm_in, norm_mid]), [w_query, w_key, w_value], 0)
    gain_in, gain_mid = gains[0][None], gains[1][None]

    def normed(rows_in):
        rows_in = rows_in.astype(f32)
        inverse = lax.rsqrt(jnp.mean(rows_in * rows_in, axis=1, keepdims=True) + norm_eps)
        return rows_in * inverse, inverse

    flat_in = flat_in.astype(f32)
    normed_in, inv_in = normed(flat_in)
    blend = jax.nn.sigmoid(mix_bias)
    blend_row = jnp.repeat(blend, HEAD_DIM)[None]
    h_in, qkv, dy, mixed, diff, lse, memory, norm_vec = attend(
        all_in, gain_in, wqkv, cotangent.reshape(own, width), doc_starts[0], blend_row, heads, 4
    )
    h_in, dy = h_in.reshape(total, width), dy.reshape(total, width)
    mixed = mixed.reshape(total, cw)

    attn_sum = product_scatter(mixed.reshape(n, own, cw), w_out, 3)
    residual = flat_in + attn_sum
    inv_mid = lax.rsqrt(jnp.mean(residual * residual, axis=1, keepdims=True) + norm_eps)
    normed_mid = residual * inv_mid
    h_mid = (normed_mid * gain_mid).astype(bf16)
    h_mid, inner, d_gu, part_down, d_hmid = mlp(h_mid, wgu, w_down, dy.reshape(n, own, width), 1)
    h_mid, inner, d_gu = (x.reshape(total, x.shape[2]) for x in (h_mid, inner, d_gu))

    gain_mid_term = jnp.sum(normed_mid * d_hmid, axis=0)
    d_resid = cotangent.reshape(own, width).astype(f32) + norm_back(d_hmid * gain_mid, normed_mid, inv_mid)
    d_attn, part_gu, part_mlp, sum_head = gather_products(d_resid.astype(bf16), h_mid, d_gu, inner, w_down, part_down, 2)
    part_gu = part_gu.reshape(n, width // n, 2 * fw)

    mlp_sum = lax.psum_scatter(part_mlp, "fsdp", scatter_dimension=0, tiled=True)
    block_out = (residual + mlp_sum.astype(f32)).astype(bf16).reshape(tokens.shape)
    per = width // n
    terms = jnp.pad(gain_mid_term.reshape(n, 1, per), ((0, 0), (1, 6), (0, 0)))
    small, grad_tokens, sum_out, sum_gu, sum_qkv, sum_down = finish(
        doc_starts[0],
        blend_row,
        terms,
        tokens.reshape(own, width),
        inv_in,
        gain_in,
        d_resid,
        part_gu,
        wqkv,
        mixed.reshape(n, own, cw),
        d_attn,
        h_in.reshape(n, own, width),
        w_out,
        qkv,
        diff,
        lse,
        memory,
        norm_vec,
        part_down,
        6,
    )
    grad_down = jnp.concatenate([sum_head, sum_down[sum_head.shape[0] :]]).astype(f32)
    grad_tokens = grad_tokens.reshape(tokens.shape)
    grad_out = sum_out.astype(f32)
    grad_gate, grad_up = sum_gu[0].astype(f32), sum_gu[1].astype(f32)
    grad_q, grad_k, grad_v = (sum_qkv[i].astype(f32) for i in range(3))

    return (
        block_out,
        grad_tokens,
        small[0],
        grad_q,
        grad_k,
        grad_v,
        small[2, :heads],
        grad_out,
        small[1],
        grad_gate,
        grad_up,
        grad_down,
    )


def solution(mesh):
    whole = P("seq", None, "fsdp", None)
    matrix, vector = P("fsdp", None), P("fsdp")
    return jax.shard_map(
        shards,
        mesh=mesh,
        in_specs=(whole, P("seq", None), vector, matrix, matrix, matrix, vector, matrix, vector, matrix, matrix, matrix, whole),
        out_specs=(whole, whole, vector, matrix, matrix, matrix, vector, matrix, vector, matrix, matrix, matrix),
        check_vma=False,
    )
```
